32 devices in a mesh: gx: 8 (over y, x, core), gy: 4 (over z).
Axes of the slice: x: 2, y: 2, z: 4, core: 2. Of those that a mesh axis runs over, the one named last changes fastest.
Arguments:
- flow_state: float32 [5, 64, 4096], P(None, 'gx', 'gy'), as said below
- x_codes: int32 [2, 128], P(None, 'gy'), may hold values from 0 to 1
- y_codes: int32 [2, 64], P(None, 'gx'), may hold values from 0 to 1
Outputs:
- increment: float32 [5, 64, 4096], P(None, 'gx', 'gy')
The draws below stay inside these ranges and needn't reach their ends.
Inputs may be any that keep to these rules, and one draw needn't show every extreme that they name: `flow_state`: density lies in [0.75, 1.33], each velocity in [-0.5, 0.5], pressure in [0.6, 1.4]. `x_codes`: 0: the increment beyond the face is zero; 1: it equals that of the boundary cell. `y_codes`: 0: the increment beyond the face is zero; 1: it equals that of the boundary cell.
All inputs are finite; a program needn't handle non-finite values.
Results may differ from the reference program's by a relative error of at most 0.0003.
Values sent between devices are 32-bit elements; how exact they have to be, the bound alone decides.
No kernel may reach another device: no remote copies, remote signals or barrier semaphores. Data moves between devices by JAX's collectives and lax.ppermute only.
A program may use at most 64 MiB of HBM per device.

```python
import math
import jax
import jax.numpy as jnp
from jax import lax

NZ = 32
NX = 64
NY = 128


def draw_flow_state(key, part):
    subkeys = jax.random.split(jax.random.fold_in(key, 17), 6)
    grid_shape = (NX, NY * NZ)
    phases = jax.random.uniform(subkeys[5], (4,), jnp.float32, 0.0, 2.0 * math.pi)
    rows_at = jnp.arange(NX, dtype=jnp.float32)[:, None] / NX
    columns_at = (jnp.arange(NY * NZ, dtype=jnp.int32) // NZ).astype(jnp.float32)[None, :] / NY
    wave_x = jnp.sin(2.0 * math.pi * rows_at + phases[0])
    wave_y = jnp.sin(2.0 * math.pi * columns_at + phases[1])
    wave_sum = jnp.sin(2.0 * math.pi * (rows_at + columns_at) + phases[2])
    wave_diff = jnp.sin(2.0 * math.pi * (rows_at - columns_at) + phases[3])
    density = jnp.clip(jnp.exp(0.08 * wave_sum + 0.08 * jax.random.normal(subkeys[0], grid_shape, jnp.float32)), 0.75, 1.33)
    vel_u = jnp.clip(0.15 * wave_x + 0.15 * jax.random.normal(subkeys[1], grid_shape, jnp.float32), -0.5, 0.5)
    vel_v = jnp.clip(0.15 * wave_y + 0.15 * jax.random.normal(subkeys[2], grid_shape, jnp.float32), -0.5, 0.5)
    vel_w = jnp.clip(0.2 * jax.random.normal(subkeys[3], grid_shape, jnp.float32), -0.5, 0.5)
    pressure = jnp.clip(jnp.exp(0.12 * wave_diff + 0.15 * jax.random.normal(subkeys[4], grid_shape, jnp.float32)), 0.6, 1.4)
    energy = pressure / 0.4 + 0.5 * density * (vel_u * vel_u + vel_v * vel_v + vel_w * vel_w)
    return jnp.stack([density, density * vel_u, density * vel_v, density * vel_w, energy])


def place_ends(drawn, key, least, largest):
    shape = drawn.shape
    place = [jax.random.randint(jax.random.fold_in(key, axis), (), 0, shape[axis]) for axis in range(len(shape))]
    drawn = drawn.at[tuple(place)].set(least)
    longest = shape.index(max(shape))
    place[longest] = (place[longest] + 1) % shape[longest]
    return drawn.at[tuple(place)].set(largest)


def setup_inputs(seed: int = 0) -> dict:
    arg_keys = jax.random.split(jax.random.key(seed), 4)
    return {
        "flow_state": draw_flow_state(jax.random.fold_in(arg_keys[3], 71), 0),
        "x_codes": place_ends(jax.random.randint(arg_keys[1], (2, NY), 0, 2), jax.random.fold_in(arg_keys[1], 1), 0, 1).astype(jnp.int32),
        "y_codes": place_ends(jax.random.randint(arg_keys[2], (2, NX), 0, 2), jax.random.fold_in(arg_keys[2], 1), 0, 1).astype(jnp.int32),
    }


GAMMA = 1.4
SIGMA = 0.5
DIFFUSE = 400.0

def primitives(conserved):
    density = conserved[0]
    vel_u = conserved[1] / density
    vel_v = conserved[2] / density
    vel_w = conserved[3] / density
    kinetic = 0.5 * (vel_u * vel_u + vel_v * vel_v + vel_w * vel_w)
    pressure = (GAMMA - 1.0) * (conserved[4] - density * kinetic)
    sound_speed = jnp.sqrt(GAMMA * pressure / density)
    return (density, vel_u, vel_v, vel_w, pressure, sound_speed)

def explicit_terms(padded):
    primitive = primitives(padded)
    density, vel_u, vel_v, vel_w, pressure, sound_speed = primitive
    enthalpy = padded[4] + pressure
    flux_x = jnp.stack([padded[1], padded[1] * vel_u + pressure, padded[2] * vel_u, padded[3] * vel_u, vel_u * enthalpy])
    flux_y = jnp.stack([padded[2], padded[1] * vel_v, padded[2] * vel_v + pressure, padded[3] * vel_v, vel_v * enthalpy])
    interior = padded[:, 1:-1, 1:-1]
    inner_speed = vel_w[1:-1, 1:-1]
    inner_pressure = pressure[1:-1, 1:-1]
    flux_z = jnp.stack([interior[3], interior[1] * inner_speed, interior[2] * inner_speed, interior[3] * inner_speed + inner_pressure, inner_speed * (interior[4] + inner_pressure)])
    change = flux_x[:, 2:, 1:-1] - flux_x[:, :-2, 1:-1] + (flux_y[:, 1:-1, 2:] - flux_y[:, 1:-1, :-2]) + (jnp.roll(flux_z, -1, axis=3) - jnp.roll(flux_z, 1, axis=3))
    smooth = padded[:, 2:, 1:-1] + padded[:, :-2, 1:-1] + padded[:, 1:-1, 2:] + padded[:, 1:-1, :-2] - 4.0 * interior
    residual = -0.5 * SIGMA * change + DIFFUSE * smooth
    return (residual, primitive)

def primitive_change(residual, primitive):
    density, vel_u, vel_v, vel_w, pressure, sound_speed = primitive
    change_u = (residual[1] - vel_u * residual[0]) / density
    change_v = (residual[2] - vel_v * residual[0]) / density
    change_w = (residual[3] - vel_w * residual[0]) / density
    kinetic = 0.5 * (vel_u * vel_u + vel_v * vel_v + vel_w * vel_w)
    change_pressure = (GAMMA - 1.0) * (residual[4] - vel_u * residual[1] - vel_v * residual[2] - vel_w * residual[3] + kinetic * residual[0])
    return (residual[0], change_u, change_v, change_w, change_pressure)

def to_characteristic(changes, primitive, normal_index):
    impedance = primitive[0] * primitive[5]
    normal_change = changes[normal_index]
    if normal_index == 1:
        tangent_one, tangent_two = (changes[2], changes[3])
    else:
        tangent_one, tangent_two = (changes[1], changes[3])
    pressure_change = changes[4]
    squared = primitive[5] * primitive[5]
    return jnp.stack([pressure_change - impedance * normal_change, squared * changes[0] - pressure_change, tangent_one, tangent_two, pressure_change + impedance * normal_change])

def from_characteristic(waves, primitive, normal_index):
    impedance = primitive[0] * primitive[5]
    squared = primitive[5] * primitive[5]
    pressure_change = 0.5 * (waves[0] + waves[4])
    normal_change = (waves[4] - waves[0]) / (2.0 * impedance)
    density_change = (waves[1] + pressure_change) / squared
    if normal_index == 1:
        return (density_change, normal_change, waves[2], waves[3], pressure_change)
    return (density_change, waves[2], normal_change, waves[3], pressure_change)

def to_conserved(changes, primitive):
    density, vel_u, vel_v, vel_w, pressure, sound_speed = primitive
    kinetic = 0.5 * (vel_u * vel_u + vel_v * vel_v + vel_w * vel_w)
    energy_change = kinetic * changes[0] + density * (vel_u * changes[1] + vel_v * changes[2] + vel_w * changes[3]) + changes[4] / (GAMMA - 1.0)
    return jnp.stack([changes[0], vel_u * changes[0] + density * changes[1], vel_v * changes[0] + density * changes[2], vel_w * changes[0] + density * changes[3], energy_change])

def eigenvalues(primitive, normal_index):
    normal_speed = primitive[normal_index]
    sound_speed = primitive[5]
    return jnp.stack([normal_speed - sound_speed, normal_speed, normal_speed, normal_speed, normal_speed + sound_speed])

def coefficients(speeds, face_codes, at_start, at_end):
    lower_band = -0.5 * SIGMA * speeds[:, :-2] - DIFFUSE
    upper_band = 0.5 * SIGMA * speeds[:, 2:] - DIFFUSE
    main_band = jnp.full(lower_band.shape, 1.0 + 2.0 * DIFFUSE, jnp.float32)
    first_neumann = jnp.logical_and(at_start, face_codes[0] == 1)
    last_neumann = jnp.logical_and(at_end, face_codes[1] == 1)
    main_band = main_band.at[:, 0].add(jnp.where(first_neumann, lower_band[:, 0], 0.0))
    main_band = main_band.at[:, -1].add(jnp.where(last_neumann, upper_band[:, -1], 0.0))
    lower_band = lower_band.at[:, 0].set(jnp.where(at_start, 0.0, lower_band[:, 0]))
    upper_band = upper_band.at[:, -1].set(jnp.where(at_end, 0.0, upper_band[:, -1]))
    return (lower_band, main_band, upper_band)

def thomas_rows(lower_band, main_band, upper_band, right_side):
    nothing = jnp.zeros_like(right_side[0])

    def forward_step(carry, row_set):
        prev_upper, prev_value = carry
        lower_row, main_row, upper_row, right_row = row_set
        pivot_value = main_row - lower_row * prev_upper
        next_upper = upper_row / pivot_value
        next_value = (right_row - lower_row * prev_value) / pivot_value
        return ((next_upper, next_value), (next_upper, next_value))
    final_carry, (uppers, values) = lax.scan(forward_step, (nothing, nothing), (lower_band, main_band, upper_band, right_side))

    def backward_step(later_value, row_set):
        upper_row, value_row = row_set
        current = value_row - upper_row * later_value
        return (current, current)
    last_carry, result = lax.scan(backward_step, nothing, (uppers, values), reverse=True)
    return result

def whole_lines(band_set, right_side):
    moved_items = [jnp.moveaxis(member, 1, 0) for member in (band_set[0], band_set[1], band_set[2], right_side)]
    solved = thomas_rows(moved_items[0], moved_items[1], moved_items[2], moved_items[3])
    return jnp.moveaxis(solved, 0, 1)

def reference(flow_state, x_codes, y_codes):
    conserved = flow_state.reshape(5, NX, NY, NZ)
    padded = jnp.pad(conserved, ((0, 0), (1, 1), (1, 1), (0, 0)), mode='edge')
    residual, primitive = explicit_terms(padded)
    interior = tuple((member[1:-1, 1:-1] for member in primitive))
    changes = primitive_change(residual, interior)
    speeds_x = eigenvalues(tuple((member[:, 1:-1] for member in primitive)), 1).reshape(5, NX + 2, NY * NZ)
    codes_x = jnp.broadcast_to(x_codes[:, :, None], (2, NY, NZ)).reshape(2, NY * NZ)
    band_set = coefficients(speeds_x, codes_x, True, True)
    right_x = to_characteristic(changes, interior, 1).reshape(5, NX, NY * NZ)
    solved_x = whole_lines(band_set, right_x).reshape(5, NX, NY, NZ)
    changes = from_characteristic(solved_x, interior, 1)
    right_y = jnp.transpose(to_characteristic(changes, interior, 2), (0, 2, 1, 3)).reshape(5, NY, NX * NZ)
    speeds_y = jnp.transpose(eigenvalues(tuple((member[1:-1] for member in primitive)), 2), (0, 2, 1, 3)).reshape(5, NY + 2, NX * NZ)
    codes_y = jnp.broadcast_to(y_codes[:, :, None], (2, NX, NZ)).reshape(2, NX * NZ)
    band_set = coefficients(speeds_y, codes_y, True, True)
    solved_y = jnp.transpose(whole_lines(band_set, right_y).reshape(5, NY, NX, NZ), (0, 2, 1, 3))
    changes = from_characteristic(solved_y, interior, 2)
    return to_conserved(changes, interior).reshape(5, NX, NY * NZ)
```

```python
import functools

import jax
import jax.numpy as jnp
from jax import lax
from jax.experimental import pallas as pl
from jax.experimental.pallas import tpu as pltpu
from jax.sharding import PartitionSpec as P

NZ = 32
GAMMA = 1.4
SIGMA = 0.5
DIFFUSE = 400.0
LANES = 128
GROUPS = LANES // NZ
SPEED_OF = (0, 1, 1, 1, 2)
ROWS = 22


def primitives(q):
    inverse = 1.0 / q[0]
    vel_u, vel_v, vel_w = q[1] * inverse, q[2] * inverse, q[3] * inverse
    kinetic = 0.5 * (vel_u * vel_u + vel_v * vel_v + vel_w * vel_w)
    pressure = (GAMMA - 1.0) * (q[4] - q[0] * kinetic)
    sound = jnp.sqrt(GAMMA * pressure * inverse)
    return inverse, vel_u, vel_v, vel_w, kinetic, pressure, sound


def flux(q, normal, speed, pressure):
    parts = [q[normal], q[1] * speed, q[2] * speed, q[3] * speed, speed * (q[4] + pressure)]
    parts[normal] = parts[normal] + pressure
    return parts


def flux_of(q, normal, speed, pressure):
    return [q[normal]] + [
        q[f] * speed + pressure if f == normal else q[f] * speed for f in (1, 2, 3)
    ] + [speed * (q[4] + pressure)]


def three_speeds(velocity, sound):
    return (velocity - sound, velocity, velocity + sound)


def sweep(speeds, rights, first, last):
    cells = len(rights)
    ups, owns, lefts = [], [], []
    for i in range(cells):
        up_i, own_i, left_i = [], [None] * 5, []
        for k in range(3):
            lower = -0.5 * SIGMA * speeds[i][k] - DIFFUSE
            upper = 0.5 * SIGMA * speeds[i + 2][k] - DIFFUSE
            main = 1.0 + 2.0 * DIFFUSE
            if i == 0:
                main = main + lower * first[1]
                lower = lower * first[0]
            if i == cells - 1:
                main = main + upper * last[1]
                upper = upper * last[0]
            pivot = main if i == 0 else main - lower * ups[-1][k]
            inverse = 1.0 / pivot
            up_i.append(upper * inverse)
            scaled = lower * inverse
            left_i.append(-scaled if i == 0 else -scaled * lefts[-1][k])
            for f in range(5):
                if SPEED_OF[f] == k:
                    own = rights[i][f] * inverse
                    own_i[f] = own if i == 0 else own - scaled * owns[-1][f]
        ups.append(up_i)
        owns.append(own_i)
        lefts.append(left_i)
    right_terms = [None] * cells
    right_terms[-1] = [-u for u in ups[-1]]
    for i in range(cells - 2, -1, -1):
        owns[i] = [owns[i][f] - ups[i][SPEED_OF[f]] * owns[i + 1][f] for f in range(5)]
        lefts[i] = [lefts[i][k] - ups[i][k] * lefts[i + 1][k] for k in range(3)]
        right_terms[i] = [-ups[i][k] * right_terms[i + 1][k] for k in range(3)]
    return owns, lefts, right_terms


def ends_of(owns, lefts, rights):
    return owns[0] + owns[-1] + lefts[0] + rights[0] + lefts[-1] + rights[-1]


def unpack(rows, fields=5, speeds=3):
    out, at = [], 0
    for n in (fields, fields, speeds, speeds, speeds, speeds):
        out.append(rows[at : at + n])
        at += n
    return out


def merge(low, own, other, speed_of):
    fields = len(speed_of)
    speeds = max(speed_of) + 1
    before = [jnp.where(low, a, b) for a, b in zip(own, other)]
    after = [jnp.where(low, b, a) for a, b in zip(own, other)]
    a_f, a_e, b_f, c_f, b_e, c_e = unpack(before, fields, speeds)
    a_g, a_h, b_g, c_g, b_h, c_h = unpack(after, fields, speeds)
    inv = [1.0 / (1.0 - c_e[k] * b_g[k]) for k in range(speeds)]
    e_1 = [b_e[k] * inv[k] for k in range(speeds)]
    f_2 = [c_g[k] * inv[k] for k in range(speeds)]
    e_2 = [c_e[k] * f_2[k] for k in range(speeds)]
    f_1 = [b_g[k] * e_1[k] for k in range(speeds)]
    e_0 = [(a_e[f] + c_e[speed_of[f]] * a_g[f]) * inv[speed_of[f]] for f in range(fields)]
    f_0 = [(a_g[f] + b_g[speed_of[f]] * a_e[f]) * inv[speed_of[f]] for f in range(fields)]
    joined = (
        [a_f[f] + c_f[speed_of[f]] * f_0[f] for f in range(fields)]
        + [a_h[f] + b_h[speed_of[f]] * e_0[f] for f in range(fields)]
        + [b_f[k] + c_f[k] * f_1[k] for k in range(speeds)]
        + [c_f[k] * f_2[k] for k in range(speeds)]
        + [b_h[k] * e_1[k] for k in range(speeds)]
        + [c_h[k] + b_h[k] * e_2[k] for k in range(speeds)]
    )
    side = [jnp.where(low, f, e) for f, e in zip(f_0 + f_1 + f_2, e_0 + e_1 + e_2)]
    return joined, side


def facing(low, rows, fields=5, speeds=3):
    a_f, a_e, b_f, c_f, b_e, c_e = unpack(rows, fields, speeds)
    return [jnp.where(low, e, f) for e, f in zip(a_e + c_e, a_f + b_f)]


def last_join(low, own, other, speed_of):
    fields = len(speed_of)
    result = []
    for f in range(fields):
        k = fields + speed_of[f]
        result.append((other[f] + other[k] * own[f]) / (1.0 - own[k] * other[k]))
    return result


def step_down(low, side, outer, speed_of):
    fields = len(speed_of)
    speeds = max(speed_of) + 1
    left, right = outer
    new = [
        side[f] + side[fields + speed_of[f]] * left[f] + side[fields + speeds + speed_of[f]] * right[f]
        for f in range(fields)
    ]
    return (
        [jnp.where(low, a, b) for a, b in zip(left, new)],
        [jnp.where(low, b, a) for a, b in zip(right, new)],
    )


def from_last(low, new):
    zero = jnp.zeros_like(new[0])
    return [jnp.where(low, zero, x) for x in new], [jnp.where(low, x, zero) for x in new]


def bit_low(axis, level):
    return (lax.axis_index(axis) >> level) % 2 == 0


def pack_kernel(flow_ref, qx_ref, near_ref, far_ref, one_ref, two_ref):
    cells = flow_ref.shape[1]
    chunks = flow_ref.shape[2] // LANES
    even_x = bit_low("gx", 0)
    even_y = bit_low("gy", 0)
    for f in range(5):
        for c in range(chunks):
            qx_ref[f, pl.ds(c, cells, stride=chunks), :] = flow_ref[f, :, c * LANES : (c + 1) * LANES]
        low = flow_ref[f, :, 0:LANES]
        high = flow_ref[f, :, (chunks - 1) * LANES : chunks * LANES]
        one_ref[f] = jnp.where(even_y, high, low)
        two_ref[f] = jnp.where(even_y, low, high)
    for f in range(5):
        low = qx_ref[f, 0:chunks, :]
        high = qx_ref[f, (cells - 1) * chunks : cells * chunks, :]
        near_ref[f] = jnp.where(even_x, high, low)
        far_ref[f] = jnp.where(even_x, low, high)


def y_halos(flow_ref, one_ref, two_ref, f):
    chunks = flow_ref.shape[2] // LANES
    at, count = lax.axis_index("gy"), lax.axis_size("gy")
    even = bit_low("gy", 0)
    one, two = one_ref[f], two_ref[f]
    low = jnp.where(even, two, one)
    high = jnp.where(even, one, two)
    own_low = pltpu.roll(flow_ref[f, :, 0:LANES], LANES - NZ, 1)
    own_high = pltpu.roll(flow_ref[f, :, (chunks - 1) * LANES : chunks * LANES], NZ, 1)
    return jnp.where(at == 0, own_low, low), jnp.where(at == count - 1, own_high, high)


def x_kernel(
    flow_ref, qx_ref, near_ref, far_ref, one_ref, two_ref, edge_ref,
    rows_ref, own_ref, left_ref, right_ref, halo_low, halo_high,
):
    cells = flow_ref.shape[1]
    chunks = flow_ref.shape[2] // LANES
    at, count = lax.axis_index("gx"), lax.axis_size("gx")
    even = bit_low("gx", 0)
    lane = lax.broadcasted_iota(jnp.int32, (chunks, LANES), 1)
    sub = lax.broadcasted_iota(jnp.int32, (chunks, LANES), 0)
    lows, highs = zip(*[y_halos(flow_ref, one_ref, two_ref, f) for f in range(5)])
    for ghosts, ref, turn in ((lows, halo_low, NZ), (highs, halo_high, LANES - NZ)):
        prim = primitives(ghosts)
        for n, value in enumerate(list(ghosts) + [prim[2], prim[5]]):
            ref[n] = pltpu.roll(value, turn, 1)
    rows = [[qx_ref[f, i * chunks : (i + 1) * chunks, :] for f in range(5)] for i in range(cells)]
    near, far = [near_ref[f] for f in range(5)], [far_ref[f] for f in range(5)]
    ghost_low = [
        jnp.where(at == 0, rows[0][f], jnp.where(even, far[f], near[f])) for f in range(5)
    ]
    ghost_high = [
        jnp.where(at == count - 1, rows[-1][f], jnp.where(even, near[f], far[f])) for f in range(5)
    ]
    padded = [ghost_low] + rows + [ghost_high]
    prims = [primitives(q) for q in padded]
    speeds = [three_speeds(p[1], p[6]) for p in prims]
    fluxes = [flux_of(q, 1, p[1], p[5]) for q, p in zip(padded, prims)]

    up_edge = jnp.logical_and(sub == chunks - 1, lane >= LANES - NZ)
    down_edge = jnp.logical_and(sub == 0, lane < NZ)
    z_of = lane % NZ

    def y_next(value, n, i):
        turned = pltpu.roll(value, LANES - NZ, 1)
        turned = jnp.where(lane >= LANES - NZ, pltpu.roll(turned, chunks - 1, 0), turned)
        ghost = jnp.broadcast_to(halo_high[n, i : i + 1, :], turned.shape)
        return jnp.where(up_edge, ghost, turned)

    def y_before(value, n, i):
        turned = pltpu.roll(value, NZ, 1)
        turned = jnp.where(lane < NZ, pltpu.roll(turned, 1, 0), turned)
        ghost = jnp.broadcast_to(halo_low[n, i : i + 1, :], turned.shape)
        return jnp.where(down_edge, ghost, turned)

    def z_change(value):
        after = jnp.where(z_of == NZ - 1, pltpu.roll(value, NZ - 1, 1), pltpu.roll(value, LANES - 1, 1))
        before = jnp.where(z_of == 0, pltpu.roll(value, LANES - NZ + 1, 1), pltpu.roll(value, 1, 1))
        return after - before

    rights = []
    for i in range(cells):
        q = padded[i + 1]
        inverse, vel_u, vel_v, vel_w, kinetic, pressure, sound = prims[i + 1]
        after = [y_next(v, n, i) for n, v in enumerate(list(q) + [vel_v, pressure])]
        before = [y_before(v, n, i) for n, v in enumerate(list(q) + [vel_v, pressure])]
        flux_after = flux_of(after, 2, after[5], after[6])
        flux_before = flux_of(before, 2, before[5], before[6])
        flux_z = flux_of(q, 3, vel_w, pressure)
        res = []
        for f in range(5):
            change = (
                (fluxes[i + 2][f] - fluxes[i][f])
                + (flux_after[f] - flux_before[f])
                + z_change(flux_z[f])
            )
            smooth = padded[i + 2][f] + padded[i][f] + after[f] + before[f] - 4.0 * q[f]
            res.append(-0.5 * SIGMA * change + DIFFUSE * smooth)
        du = (res[1] - vel_u * res[0]) * inverse
        dv = (res[2] - vel_v * res[0]) * inverse
        dw = (res[3] - vel_w * res[0]) * inverse
        dp = (GAMMA - 1.0) * (
            res[4] - vel_u * res[1] - vel_v * res[2] - vel_w * res[3] + kinetic * res[0]
        )
        normal = q[0] * sound * du
        rights.append([dp - normal, sound * sound * res[0] - dp, dv, dw, dp + normal])
    owns, lefts, right_terms = sweep(
        speeds, rights, (edge_ref[0], edge_ref[1]), (edge_ref[2], edge_ref[3])
    )
    for n, value in enumerate(ends_of(owns, lefts, right_terms)):
        rows_ref[n] = value
    for i in range(cells):
        for f in range(5):
            own_ref[f, i] = owns[i][f]
        for k in range(3):
            left_ref[k, i] = lefts[i][k]
            right_ref[k, i] = right_terms[i][k]


def merge_kernel(axis, level, final, speed_of, own_ref, other_ref, out_ref, side_ref):
    own = [own_ref[n] for n in range(own_ref.shape[0])]
    other = [other_ref[n] for n in range(other_ref.shape[0])]
    joined, side = merge(bit_low(axis, level), own, other, speed_of)
    if final:
        joined = facing(bit_low(axis, level + 1), joined, len(speed_of), max(speed_of) + 1)
    for n, value in enumerate(joined):
        out_ref[n] = value
    for n, value in enumerate(side):
        side_ref[n] = value


def outer_values(axis, levels, speed_of, own_ref, other_ref, side_refs):
    own = [own_ref[n] for n in range(own_ref.shape[0])]
    other = [other_ref[n] for n in range(other_ref.shape[0])]
    low = bit_low(axis, levels - 1)
    outer = from_last(low, last_join(low, own, other, speed_of))
    for level in range(levels - 2, -1, -1):
        ref = side_refs[level]
        side = [ref[n] for n in range(ref.shape[0])]
        outer = step_down(bit_low(axis, level), side, outer, speed_of)
    return outer


PACKED_SPEED = (0, 0)


def y_kernel(levels, *refs):
    (flow_ref, qx_ref, one_ref, two_ref, edge_ref, own_ref, left_ref, right_ref,
     mine_ref, other_ref) = refs[:10]
    sides = refs[10 : 10 + levels - 1]
    (out_ref, yown_ref, yleft_ref, yright_ref, s0_ref, s1_ref, turn_ref) = refs[10 + levels - 1 :]
    cells = flow_ref.shape[1]
    chunks = flow_ref.shape[2] // LANES
    steps = chunks
    outer_l, outer_r = outer_values("gx", levels, SPEED_OF, mine_ref, other_ref, sides)
    for i in range(cells):
        q = [qx_ref[f, i * chunks : (i + 1) * chunks, :] for f in range(5)]
        inverse, vel_u, vel_v, vel_w, kinetic, pressure, sound = primitives(q)
        wave = [
            own_ref[f, i] + left_ref[SPEED_OF[f], i] * outer_l[f] + right_ref[SPEED_OF[f], i] * outer_r[f]
            for f in range(5)
        ]
        impedance = q[0] * sound
        squared = sound * sound
        dp = 0.5 * (wave[0] + wave[4])
        du = (wave[4] - wave[0]) / (2.0 * impedance)
        dr = (wave[1] + dp) / squared
        normal = impedance * wave[2]
        values = [dp - normal, squared * dr - dp, du, wave[3], dp + normal, vel_v, sound]
        for n, value in enumerate(values):
            turn_ref[n, i * chunks : (i + 1) * chunks, :] = value
    lane = lax.broadcasted_iota(jnp.int32, (cells, LANES), 1)
    group = lane // NZ

    def regroup(n):
        parts = [turn_ref[n, pl.ds(c, cells, stride=chunks), :] for c in range(chunks)]
        result = []
        for jj in range(steps):
            pieces = []
            for s in range(GROUPS):
                y = s * steps + jj
                piece = parts[y // GROUPS]
                shift = (s - y % GROUPS) * NZ % LANES
                pieces.append(pltpu.roll(piece, shift, 1) if shift else piece)
            value = pieces[0]
            for s in range(1, GROUPS):
                value = jnp.where(group == s, pieces[s], value)
            result.append(value)
        return result

    fields = [regroup(n) for n in range(7)]
    rights = [[fields[f][jj] for f in range(5)] for jj in range(steps)]
    speeds = [three_speeds(fields[5][jj], fields[6][jj]) for jj in range(steps)]
    lows, highs = zip(*[y_halos(flow_ref, one_ref, two_ref, f) for f in range(5)])
    low_prim, high_prim = primitives(lows), primitives(highs)
    low_speed = three_speeds(low_prim[2], low_prim[6])
    high_speed = three_speeds(high_prim[2], high_prim[6])
    before = tuple(
        pltpu.roll(jnp.where(group == GROUPS - 1, low_speed[k], speeds[-1][k]), NZ, 1) for k in range(3)
    )
    after = tuple(
        pltpu.roll(jnp.where(group == 0, high_speed[k], speeds[0][k]), LANES - NZ, 1) for k in range(3)
    )
    owns, lefts, right_terms = sweep(
        [before] + speeds + [after], rights, (edge_ref[0], edge_ref[1]), (edge_ref[2], edge_ref[3])
    )
    for i in range(steps):
        for f in range(5):
            yown_ref[f, i] = owns[i][f]
        for k in range(3):
            yleft_ref[k, i] = lefts[i][k]
            yright_ref[k, i] = right_terms[i][k]
    ends = ends_of(owns, lefts, right_terms)
    low = group % 2 == 0
    other = [jnp.where(low, pltpu.roll(v, LANES - NZ, 1), pltpu.roll(v, NZ, 1)) for v in ends]
    ends, side = merge(low, ends, other, SPEED_OF)
    for n, value in enumerate(side):
        s0_ref[n] = value
    low = group // 2 == 0
    other = [pltpu.roll(v, LANES // 2, 1) for v in ends]
    ends, side = merge(low, ends, other, SPEED_OF)
    for n, value in enumerate(side):
        s1_ref[n] = value
    for n, value in enumerate(pack_groups(group, ends)):
        out_ref[n] = value


def pack_groups(group, ends):
    a_f, a_e, b_f, c_f, b_e, c_e = unpack(ends)

    def four(a, b, c, d):
        return jnp.where(group == 0, a, jnp.where(group == 1, b, jnp.where(group == 2, c, d)))

    firsts = [four(a_f[0], a_f[1], a_f[4], a_f[2]), a_f[3]]
    lasts = [four(a_e[0], a_e[1], a_e[4], a_e[2]), a_e[3]]
    factors = [four(t[0], t[1], t[2], t[1]) for t in (b_f, c_f, b_e, c_e)]
    return firsts + lasts + factors


def spread(group, value, source):
    half = jnp.where(group // 2 == source // 2, value, pltpu.roll(value, LANES // 2, 1))
    down, up = pltpu.roll(half, NZ, 1), pltpu.roll(half, LANES - NZ, 1)
    if source % 2 == 0:
        return jnp.where(group % 2 == 0, half, down)
    return jnp.where(group % 2 == 1, half, up)


def final_kernel(levels, *refs):
    (flow_ref, yown_ref, yleft_ref, yright_ref, s0_ref, s1_ref, mine_ref, other_ref) = refs[:8]
    sides = refs[8 : 8 + levels - 1]
    out_ref = refs[8 + levels - 1]
    cells = flow_ref.shape[1]
    chunks = flow_ref.shape[2] // LANES
    steps = chunks
    lane = lax.broadcasted_iota(jnp.int32, (cells, LANES), 1)
    group = lane // NZ
    outer = outer_values("gy", levels, PACKED_SPEED, mine_ref, other_ref, sides)
    outer = tuple(
        [spread(group, v[0], 0), spread(group, v[0], 1), spread(group, v[0], 3),
         spread(group, v[1], 1), spread(group, v[0], 2)]
        for v in outer
    )
    outer = step_down(group // 2 == 0, [s1_ref[n] for n in range(11)], outer, SPEED_OF)
    outer_l, outer_r = step_down(group % 2 == 0, [s0_ref[n] for n in range(11)], outer, SPEED_OF)
    solved = [
        [
            yown_ref[f, j] + yleft_ref[SPEED_OF[f], j] * outer_l[f] + yright_ref[SPEED_OF[f], j] * outer_r[f]
            for f in range(5)
        ]
        for j in range(steps)
    ]
    for c in range(chunks):
        wave = []
        for f in range(5):
            value = None
            for g in range(GROUPS):
                y = c * GROUPS + g
                piece = solved[y % steps][f]
                shift = (g - y // steps) * NZ % LANES
                piece = pltpu.roll(piece, shift, 1) if shift else piece
                value = piece if g == 0 else jnp.where(group == g, piece, value)
            wave.append(value)
        q = [flow_ref[f, :, c * LANES : (c + 1) * LANES] for f in range(5)]
        inverse, vel_u, vel_v, vel_w, kinetic, pressure, sound = primitives(q)
        dp = 0.5 * (wave[0] + wave[4])
        dv = (wave[4] - wave[0]) / (2.0 * q[0] * sound)
        dr = (wave[1] + dp) / (sound * sound)
        du, dw = wave[2], wave[3]
        energy = (
            kinetic * dr + q[0] * (vel_u * du + vel_v * dv + vel_w * dw) + dp * (1.0 / (GAMMA - 1.0))
        )
        result = [dr, vel_u * dr + q[0] * du, vel_v * dr + q[0] * dv, vel_w * dr + q[0] * dw, energy]
        for f in range(5):
            out_ref[f, :, c * LANES : (c + 1) * LANES] = result[f]


def call(kernel, name, args, outs, scratch=()):
    vmem = pl.BlockSpec(memory_space=pltpu.VMEM)
    return pl.pallas_call(
        kernel,
        out_shape=[jax.ShapeDtypeStruct(shape, jnp.float32) for shape in outs],
        in_specs=[vmem] * len(args),
        out_specs=[vmem] * len(outs),
        scratch_shapes=[pltpu.VMEM(shape, jnp.float32) for shape in scratch],
        compiler_params=pltpu.CompilerParams(vmem_limit_bytes=16 * 1024 * 1024),
        name=name,
    )(*args)


def pairs_at(count, level):
    return [(i, i ^ (1 << level)) for i in range(count)]


def pairs_far(count):
    steps = [(i, i + 1) for i in range(1, count - 1, 2)]
    return steps + [(b, a) for a, b in steps]


def levels_of(count):
    levels = count.bit_length() - 1
    assert count == 1 << levels and levels >= 1
    return levels


def edges(codes, axis):
    at, count = lax.axis_index(axis), lax.axis_size(axis)
    start = (at == 0).astype(jnp.float32)
    end = (at == count - 1).astype(jnp.float32)
    ones = jnp.ones_like(codes[0], jnp.float32)
    is_one = (codes == 1).astype(jnp.float32)
    return jnp.stack([(1.0 - start) * ones, start * is_one[0], (1.0 - end) * ones, end * is_one[1]])


def local(flow, x_codes, y_codes):
    cells = flow.shape[1]
    columns = flow.shape[2]
    chunks = columns // LANES
    count_x, count_y = lax.axis_size("gx"), lax.axis_size("gy")
    levels_x, levels_y = levels_of(count_x), levels_of(count_y)
    tile_x, tile_y = (chunks, LANES), (cells, LANES)

    qx, near, far, one, two = call(
        pack_kernel, "pack", [flow],
        [(5, cells * chunks, LANES), (5,) + tile_x, (5,) + tile_x, (5,) + tile_y, (5,) + tile_y],
    )
    one = lax.ppermute(one, "gy", pairs_at(count_y, 0))
    two = lax.ppermute(two, "gy", pairs_far(count_y))
    far = lax.ppermute(far, "gx", pairs_far(count_x))
    near = lax.ppermute(near, "gx", pairs_at(count_x, 0))

    codes_x = jnp.broadcast_to(x_codes[:, :, None], x_codes.shape + (NZ,)).reshape((2,) + tile_x)
    edge_x = edges(codes_x, "gx")
    lane_group = lax.broadcasted_iota(jnp.int32, (4,) + tile_y, 2) // NZ
    edge_y = edges(jnp.broadcast_to(y_codes[:, :, None], (2,) + tile_y), "gy")
    side = lax.broadcasted_iota(jnp.int32, (4,) + tile_y, 0)
    inner = jnp.where(side < 2, lane_group != 0, lane_group != GROUPS - 1)
    edge_y = jnp.where(inner, jnp.where(side % 2 == 0, 1.0, 0.0), edge_y)

    rows, own, left, right = call(
        x_kernel, "xsweep", [flow, qx, near, far, one, two, edge_x],
        [(ROWS,) + tile_x, (5, cells) + tile_x, (3, cells) + tile_x, (3, cells) + tile_x],
        [(7,) + tile_y, (7,) + tile_y],
    )
    sides = []
    for level in range(levels_x - 1):
        other = lax.ppermute(rows, "gx", pairs_at(count_x, level))
        final = level == levels_x - 2
        rows, side_rows = call(
            functools.partial(merge_kernel, "gx", level, final, SPEED_OF), f"xmerge{level}",
            [rows, other], [(8 if final else ROWS,) + tile_x, (11,) + tile_x],
        )
        sides.append(side_rows)
    other = lax.ppermute(rows, "gx", pairs_at(count_x, levels_x - 1))
    packed, yown, yleft, yright, side_0, side_1 = call(
        functools.partial(y_kernel, levels_x), "ysweep",
        [flow, qx, one, two, edge_y, own, left, right, rows, other] + sides,
        [(8,) + tile_y, (5, chunks) + tile_y, (3, chunks) + tile_y, (3, chunks) + tile_y,
         (11,) + tile_y, (11,) + tile_y],
        [(7, cells * chunks, LANES)],
    )
    sides = []
    for level in range(levels_y - 1):
        other = lax.ppermute(packed, "gy", pairs_at(count_y, level))
        final = level == levels_y - 2
        packed, side_rows = call(
            functools.partial(merge_kernel, "gy", level, final, PACKED_SPEED), f"ymerge{level}",
            [packed, other], [(3 if final else 8,) + tile_y, (4,) + tile_y],
        )
        sides.append(side_rows)
    other = lax.ppermute(packed, "gy", pairs_at(count_y, levels_y - 1))
    (result,) = call(
        functools.partial(final_kernel, levels_y), "final",
        [flow, yown, yleft, yright, side_0, side_1, packed, other] + sides,
        [(5, cells, columns)],
    )
    return result


def solution(mesh):
    in_specs = (P(None, "gx", "gy"), P(None, "gy"), P(None, "gx"))
    out_specs = P(None, "gx", "gy")
    return jax.shard_map(local, mesh=mesh, in_specs=in_specs, out_specs=out_specs, check_vma=False)
```

```python
import functools

import jax
import jax.numpy as jnp
from jax import lax
from jax.experimental import pallas as pl
from jax.experimental.pallas import tpu as pltpu
from jax.sharding import PartitionSpec as P

NZ = 32
GAMMA = 1.4
SIGMA = 0.5
DIFFUSE = 400.0
LANES = 128
GROUPS = LANES // NZ
SPEED_OF = (0, 1, 1, 1, 2)
COEFS = 12


def primitives(q):
    inverse = 1.0 / q[0]
    vel_u, vel_v, vel_w = q[1] * inverse, q[2] * inverse, q[3] * inverse
    kinetic = 0.5 * (vel_u * vel_u + vel_v * vel_v + vel_w * vel_w)
    pressure = (GAMMA - 1.0) * (q[4] - q[0] * kinetic)
    sound = jnp.sqrt(GAMMA * pressure * inverse)
    return inverse, vel_u, vel_v, vel_w, kinetic, pressure, sound


def flux_of(q, normal, speed, pressure):
    return [q[normal]] + [
        q[f] * speed + pressure if f == normal else q[f] * speed for f in (1, 2, 3)
    ] + [speed * (q[4] + pressure)]


def three_speeds(velocity, sound):
    return (velocity - sound, velocity, velocity + sound)


def x_characteristics(res, density, prim):
    inverse, vel_u, vel_v, vel_w, kinetic, pressure, sound = prim
    du = (res[1] - vel_u * res[0]) * inverse
    dv = (res[2] - vel_v * res[0]) * inverse
    dw = (res[3] - vel_w * res[0]) * inverse
    dp = (GAMMA - 1.0) * (
        res[4] - vel_u * res[1] - vel_v * res[2] - vel_w * res[3] + kinetic * res[0]
    )
    normal = density * sound * du
    return [dp - normal, sound * sound * res[0] - dp, dv, dw, dp + normal]


def factor(speeds, first, last, forced=False):
    cells = len(speeds) - 2
    inverses, lowers, ups, lefts = [], [], [], []
    for i in range(cells):
        parts = []
        for k in range(3):
            lower = -0.5 * SIGMA * speeds[i][k] - DIFFUSE
            upper = 0.5 * SIGMA * speeds[i + 2][k] - DIFFUSE
            main = 1.0 + 2.0 * DIFFUSE
            if i == 0:
                main = main + lower * first[1]
                lower = None if forced else lower * first[0]
            if i == cells - 1:
                main = main + upper * last[1]
                upper = None if forced else upper * last[0]
            pivot = main if i == 0 else main - lower * ups[-1][k]
            inverse = 1.0 / pivot
            scaled = -inverse if lower is None else lower * inverse
            left = -scaled if i == 0 else -scaled * lefts[-1][k]
            parts.append((inverse, scaled, -inverse if upper is None else upper * inverse, left))
        for out, values in zip((inverses, lowers, ups, lefts), zip(*parts)):
            out.append(list(values))
    rights = [None] * cells
    rights[-1] = [-u for u in ups[-1]]
    for i in range(cells - 2, -1, -1):
        lefts[i] = [lefts[i][k] - ups[i][k] * lefts[i + 1][k] for k in range(3)]
        rights[i] = [-ups[i][k] * rights[i + 1][k] for k in range(3)]
    return inverses, lowers, ups, lefts, rights


def substitute(inverses, lowers, ups, sources):
    cells = len(sources)
    owns = []
    for i in range(cells):
        own = [sources[i][f] * inverses[i][SPEED_OF[f]] for f in range(5)]
        if i:
            own = [own[f] - lowers[i][SPEED_OF[f]] * owns[-1][f] for f in range(5)]
        owns.append(own)
    for i in range(cells - 2, -1, -1):
        owns[i] = [owns[i][f] - ups[i][SPEED_OF[f]] * owns[i + 1][f] for f in range(5)]
    return owns


def unpack(rows, fields=5, speeds=3):
    out, at = [], 0
    for n in (fields, fields, speeds, speeds, speeds, speeds):
        out.append(rows[at : at + n])
        at += n
    return out


def join(before, after, speed_of):
    fields = len(speed_of)
    a_f, a_e, b_f, c_f, b_e, c_e = before
    speeds = len(b_f)
    a_g, a_h, b_g, c_g, b_h, c_h = after
    inv = [1.0 / (1.0 - c_e[k] * b_g[k]) for k in range(speeds)]
    e_1 = [b_e[k] * inv[k] for k in range(speeds)]
    f_2 = [c_g[k] * inv[k] for k in range(speeds)]
    e_2 = [c_e[k] * f_2[k] for k in range(speeds)]
    f_1 = [b_g[k] * e_1[k] for k in range(speeds)]
    e_0 = [(a_e[f] + c_e[speed_of[f]] * a_g[f]) * inv[speed_of[f]] for f in range(fields)]
    f_0 = [(a_g[f] + b_g[speed_of[f]] * a_e[f]) * inv[speed_of[f]] for f in range(fields)]
    joined = (
        [a_f[f] + c_f[speed_of[f]] * f_0[f] for f in range(fields)]
        + [a_h[f] + b_h[speed_of[f]] * e_0[f] for f in range(fields)]
        + [b_f[k] + c_f[k] * f_1[k] for k in range(speeds)]
        + [c_f[k] * f_2[k] for k in range(speeds)]
        + [b_h[k] * e_1[k] for k in range(speeds)]
        + [c_h[k] + b_h[k] * e_2[k] for k in range(speeds)]
    )
    return joined, e_0 + e_1 + e_2, f_0 + f_1 + f_2


def merge(low, own, other, speed_of):
    fields = len(speed_of)
    speeds = max(speed_of) + 1
    before = [jnp.where(low, a, b) for a, b in zip(own, other)]
    after = [jnp.where(low, b, a) for a, b in zip(own, other)]
    joined, e, f = join(unpack(before, fields, speeds), unpack(after, fields, speeds), speed_of)
    return joined, [jnp.where(low, b, a) for a, b in zip(e, f)]


def facing(low, rows, fields=5, speeds=3):
    a_f, a_e, b_f, c_f, b_e, c_e = unpack(rows, fields, speeds)
    return [jnp.where(low, e, f) for e, f in zip(a_e + c_e, a_f + b_f)]


def join_factors(q_before, q_after):
    prim_b, prim_a = primitives(q_before), primitives(q_after)
    flux_b = flux_of(q_before, 1, prim_b[1], prim_b[5])
    flux_a = flux_of(q_after, 1, prim_a[1], prim_a[5])
    change = [-0.5 * SIGMA * (a - b) for a, b in zip(flux_a, flux_b)]
    smooth = [DIFFUSE * (a - b) for a, b in zip(q_after, q_before)]
    h_b = x_characteristics([c + d for c, d in zip(change, smooth)], q_before[0], prim_b)
    h_a = x_characteristics([c - d for c, d in zip(change, smooth)], q_after[0], prim_a)
    u_b = [DIFFUSE - 0.5 * SIGMA * v for v in three_speeds(prim_a[1], prim_a[6])]
    l_a = [DIFFUSE + 0.5 * SIGMA * v for v in three_speeds(prim_b[1], prim_b[6])]
    return h_b, u_b, h_a, l_a


def merge_forced(low, own, other):
    before = [jnp.where(low, a, b) for a, b in zip(own, other)]
    after = [jnp.where(low, b, a) for a, b in zip(own, other)]
    q_before, q_after = before[-5:], after[-10:-5]
    h_b, u_b, h_a, l_a = join_factors(q_before, q_after)
    a_f, a_e, b_f, c_f, b_e, c_e = unpack(before)
    a_g, a_h, b_g, c_g, b_h, c_h = unpack(after)
    a_f, a_e = ([a[f] + c[SPEED_OF[f]] * h_b[f] for f in range(5)] for a, c in ((a_f, c_f), (a_e, c_e)))
    a_g, a_h = ([a[f] + b[SPEED_OF[f]] * h_a[f] for f in range(5)] for a, b in ((a_g, b_g), (a_h, b_h)))
    c_f, c_e = ([c[k] * u_b[k] for k in range(3)] for c in (c_f, c_e))
    b_g, b_h = ([b[k] * l_a[k] for k in range(3)] for b in (b_g, b_h))
    joined, e, f = join(
        (a_f, a_e, b_f, c_f, b_e, c_e), (a_g, a_h, b_g, c_g, b_h, c_h), SPEED_OF
    )
    to_low = [h_b[n] + u_b[SPEED_OF[n]] * f[n] for n in range(5)]
    to_low += [u_b[k] * f[5 + 3 * t + k] for t in range(2) for k in range(3)]
    to_high = [h_a[n] + l_a[SPEED_OF[n]] * e[n] for n in range(5)]
    to_high += [l_a[k] * e[5 + 3 * t + k] for t in range(2) for k in range(3)]
    return joined, [jnp.where(low, a, b) for a, b in zip(to_low, to_high)]


def merge_factors(low, own, other):
    before = [jnp.where(low, a, b) for a, b in zip(own, other)]
    after = [jnp.where(low, b, a) for a, b in zip(own, other)]
    prim_b, prim_a = (primitives(q) for q in (before[-5:], after[-10:-5]))
    u_b = [DIFFUSE - 0.5 * SIGMA * v for v in three_speeds(prim_a[1], prim_a[6])]
    l_a = [DIFFUSE + 0.5 * SIGMA * v for v in three_speeds(prim_b[1], prim_b[6])]
    b_f, c_f, b_e, c_e = (before[3 * n : 3 * n + 3] for n in range(4))
    b_g, c_g, b_h, c_h = (after[3 * n : 3 * n + 3] for n in range(4))
    c_f, c_e = ([c[k] * u_b[k] for k in range(3)] for c in (c_f, c_e))
    b_g, b_h = ([b[k] * l_a[k] for k in range(3)] for b in (b_g, b_h))
    joined, _, _ = join(([], [], b_f, c_f, b_e, c_e), ([], [], b_g, c_g, b_h, c_h), ())
    return joined, before[-10:-5], after[-5:]


def last_join(low, own, other, speed_of):
    fields = len(speed_of)
    result = []
    for f in range(fields):
        k = fields + speed_of[f]
        result.append((other[f] + other[k] * own[f]) / (1.0 - own[k] * other[k]))
    return result


def last_join_forced(low, own, other):
    before = [jnp.where(low, a, b) for a, b in zip(own, other)]
    after = [jnp.where(low, b, a) for a, b in zip(own, other)]
    h_b, u_b, h_a, l_a = join_factors(before[8:], after[8:])
    h_own = [jnp.where(low, a, b) for a, b in zip(h_b, h_a)]
    h_other = [jnp.where(low, b, a) for a, b in zip(h_b, h_a)]
    k_own = [jnp.where(low, a, b) for a, b in zip(u_b, l_a)]
    k_other = [jnp.where(low, b, a) for a, b in zip(u_b, l_a)]
    mine, theirs = [], []
    for rows, h, k, out in ((own, h_own, k_own, mine), (other, h_other, k_other, theirs)):
        out.extend(rows[f] + rows[5 + SPEED_OF[f]] * h[f] for f in range(5))
        out.extend(rows[5 + n] * k[n] for n in range(3))
    value = last_join(low, mine, theirs, SPEED_OF)
    return [h_own[f] + k_own[SPEED_OF[f]] * value[f] for f in range(5)]


def step_down(low, side, outer, speed_of):
    fields = len(speed_of)
    speeds = max(speed_of) + 1
    left, right = outer
    new = [
        side[f] + side[fields + speed_of[f]] * left[f] + side[fields + speeds + speed_of[f]] * right[f]
        for f in range(fields)
    ]
    return (
        [jnp.where(low, a, b) for a, b in zip(left, new)],
        [jnp.where(low, b, a) for a, b in zip(right, new)],
    )


def from_last(low, new):
    zero = jnp.zeros_like(new[0])
    return [jnp.where(low, zero, x) for x in new], [jnp.where(low, x, zero) for x in new]


def bit_low(axis, level):
    return (lax.axis_index(axis) >> level) % 2 == 0


def x_edges(codes_ref, shape):
    at, count = lax.axis_index("gx"), lax.axis_size("gx")
    lane = lax.broadcasted_iota(jnp.int32, shape, 1)
    sub = lax.broadcasted_iota(jnp.int32, shape, 0)
    width = codes_ref.shape[1]
    result = []
    place = lax.broadcasted_iota(jnp.int32, (shape[0], width), 1)
    row = lax.broadcasted_iota(jnp.int32, (shape[0], width), 0)
    for side, outer in ((0, at == 0), (1, at == count - 1)):
        codes = jnp.broadcast_to(codes_ref[side : side + 1, :], (shape[0], width))
        is_one = jnp.where(codes == 1, 1.0, 0.0)
        value = jnp.zeros(shape, jnp.float32)
        for g in range(GROUPS):
            mine = jnp.where(place == row * GROUPS + g, is_one, 0.0)
            column = jnp.sum(mine, axis=1, keepdims=True)
            value = jnp.where(lane // NZ == g, column, value)
        result.append(jnp.where(outer, value, 0.0))
    return result


def y_edges(codes_ref, shape):
    at, count = lax.axis_index("gy"), lax.axis_size("gy")
    group = lax.broadcasted_iota(jnp.int32, shape, 1) // NZ
    cells = shape[0]
    result = []
    place = lax.broadcasted_iota(jnp.int32, (cells, cells), 1)
    row = lax.broadcasted_iota(jnp.int32, (cells, cells), 0)
    for side, outer, face in ((0, at == 0, 0), (1, at == count - 1, GROUPS - 1)):
        codes = jnp.broadcast_to(codes_ref[side : side + 1, :], (cells, cells))
        mine = jnp.where(jnp.logical_and(codes == 1, place == row), 1.0, 0.0)
        value = jnp.broadcast_to(jnp.sum(mine, axis=1, keepdims=True), shape)
        at_face = jnp.logical_and(outer, group == face)
        result.append((jnp.where(at_face, 0.0, 1.0), jnp.where(at_face, value, 0.0)))
    return result


def pack_kernel(flow_ref, qx_ref, one_ref, two_ref):
    cells = flow_ref.shape[1]
    chunks = flow_ref.shape[2] // LANES
    even = bit_low("gx", 0)
    for f in range(5):
        down = flow_ref[f, :, 0:LANES]
        up = flow_ref[f, :, (chunks - 1) * LANES : chunks * LANES]
        one_ref[f] = jnp.where(even, up, down)
        two_ref[f] = jnp.where(even, down, up)
        for c in range(chunks):
            qx_ref[f, pl.ds(c, cells, stride=chunks), :] = flow_ref[f, :, c * LANES : (c + 1) * LANES]


def y_halos(flow_ref, one_ref, two_ref, f):
    chunks = flow_ref.shape[2] // LANES
    at, count = lax.axis_index("gy"), lax.axis_size("gy")
    even = bit_low("gx", 0)
    low = jnp.where(even, one_ref[f], two_ref[f])
    high = jnp.where(even, two_ref[f], one_ref[f])
    own_low = pltpu.roll(flow_ref[f, :, 0:LANES], LANES - NZ, 1)
    own_high = pltpu.roll(flow_ref[f, :, (chunks - 1) * LANES : chunks * LANES], NZ, 1)
    return jnp.where(at == 0, own_low, low), jnp.where(at == count - 1, own_high, high)


def x_factor_kernel(qx_ref, codes_ref, out_ref, inverse_ref, lower_ref, up_ref, left_ref, right_ref):
    cells = inverse_ref.shape[0]
    chunks = inverse_ref.shape[2]
    rows = [[qx_ref[f, i * chunks : (i + 1) * chunks, :] for f in range(5)] for i in range(cells)]
    speeds = []
    for q in rows:
        prim = primitives(q)
        speeds.append(three_speeds(prim[1], prim[6]))
    neumann = x_edges(codes_ref, (chunks, LANES))
    parts = factor(
        speeds[:1] + speeds + speeds[-1:], (None, neumann[0]), (None, neumann[1]), forced=True
    )
    for ref, values in zip((inverse_ref, lower_ref, up_ref, left_ref, right_ref), parts):
        for i in range(cells):
            store(ref.at[i], values[i])
    lefts, rights = parts[3:]
    store(out_ref, lefts[0] + rights[0] + lefts[-1] + rights[-1] + rows[0] + rows[-1])


def x_source_kernel(qx_ref, out_ref):
    cells = out_ref.shape[0]
    chunks = out_ref.shape[2]
    lane = lax.broadcasted_iota(jnp.int32, (chunks, LANES), 1)
    sub = lax.broadcasted_iota(jnp.int32, (chunks, LANES), 0)
    z_of = lane % NZ
    rows = [[qx_ref[f, i * chunks : (i + 1) * chunks, :] for f in range(5)] for i in range(cells)]
    prims = [primitives(q) for q in rows]
    fluxes = [flux_of(q, 1, p[1], p[5]) for q, p in zip(rows, prims)]
    rows, fluxes = (v[:1] + v + v[-1:] for v in (rows, fluxes))
    up_edge = jnp.logical_and(sub == chunks - 1, lane >= LANES - NZ)
    down_edge = jnp.logical_and(sub == 0, lane < NZ)

    def y_next(value):
        turned = pltpu.roll(value, LANES - NZ, 1)
        turned = jnp.where(lane >= LANES - NZ, pltpu.roll(turned, chunks - 1, 0), turned)
        return jnp.where(up_edge, value, turned)

    def y_before(value):
        turned = pltpu.roll(value, NZ, 1)
        turned = jnp.where(lane < NZ, pltpu.roll(turned, 1, 0), turned)
        return jnp.where(down_edge, value, turned)

    def z_change(value):
        after = jnp.where(z_of == NZ - 1, pltpu.roll(value, NZ - 1, 1), pltpu.roll(value, LANES - 1, 1))
        before = jnp.where(z_of == 0, pltpu.roll(value, LANES - NZ + 1, 1), pltpu.roll(value, 1, 1))
        return after - before

    for i in range(cells):
        q = rows[i + 1]
        inverse, vel_u, vel_v, vel_w, kinetic, pressure, sound = prims[i]
        after = [y_next(v) for v in list(q) + [vel_v, pressure]]
        before = [y_before(v) for v in list(q) + [vel_v, pressure]]
        flux_after = flux_of(after, 2, after[5], after[6])
        flux_before = flux_of(before, 2, before[5], before[6])
        flux_z = flux_of(q, 3, vel_w, pressure)
        res = []
        for f in range(5):
            change = (
                (fluxes[i + 2][f] - fluxes[i][f])
                + (flux_after[f] - flux_before[f])
                + z_change(flux_z[f])
            )
            smooth = rows[i + 2][f] + rows[i][f] + after[f] + before[f] - 4.0 * q[f]
            res.append(-0.5 * SIGMA * change + DIFFUSE * smooth)
        store(out_ref.at[i], x_characteristics(res, q[0], prims[i]))


def x_kernel(
    flow_ref, one_ref, two_ref, source_ref, inverse_ref, lower_ref, up_ref,
    rows_ref, own_ref, low_ref, high_ref,
):
    cells = flow_ref.shape[1]
    chunks = flow_ref.shape[2] // LANES
    lane = lax.broadcasted_iota(jnp.int32, (chunks, LANES), 1)
    sub = lax.broadcasted_iota(jnp.int32, (chunks, LANES), 0)
    up_edge = jnp.logical_and(sub == chunks - 1, lane >= LANES - NZ)
    down_edge = jnp.logical_and(sub == 0, lane < NZ)
    lows, highs = zip(*[y_halos(flow_ref, one_ref, two_ref, f) for f in range(5)])
    for ghosts, at, turn, sign, ref in (
        (lows, 0, NZ, 1.0, low_ref), (highs, chunks - 1, LANES - NZ, -1.0, high_ref)
    ):
        ghosts = [pltpu.roll(g, turn, 1) for g in ghosts]
        inner = [flow_ref[f, :, at * LANES : (at + 1) * LANES] for f in range(5)]
        ghost_prim, prim = primitives(ghosts), primitives(inner)
        ghost_flux = flux_of(ghosts, 2, ghost_prim[2], ghost_prim[5])
        inner_flux = flux_of(inner, 2, prim[2], prim[5])
        res = [
            sign * 0.5 * SIGMA * (ghost_flux[f] - inner_flux[f]) + DIFFUSE * (ghosts[f] - inner[f])
            for f in range(5)
        ]
        store(ref, x_characteristics(res, inner[0], prim))
    sources = []
    for i in range(cells):
        source = []
        for f in range(5):
            low = jnp.broadcast_to(low_ref[f, i : i + 1, :], (chunks, LANES))
            high = jnp.broadcast_to(high_ref[f, i : i + 1, :], (chunks, LANES))
            extra = jnp.where(down_edge, low, 0.0) + jnp.where(up_edge, high, 0.0)
            source.append(source_ref[i, f] + extra)
        sources.append(source)
    owns = substitute(*([load(ref.at[i]) for i in range(cells)] for ref in (inverse_ref, lower_ref, up_ref)), sources)
    for i in range(cells):
        store(own_ref.at[i], owns[i])
    store(rows_ref, owns[0] + owns[-1])


def load(ref):
    return [ref[n] for n in range(ref.shape[0])]


def store(ref, values):
    for n, value in enumerate(values):
        ref[n] = value


def x_merge_factor_kernel(level, final, own_ref, other_ref, out_ref):
    joined, q_first, q_last = merge_factors(bit_low("gx", level), load(own_ref), load(other_ref))
    if final:
        low = bit_low("gx", level + 1)
        b_f, c_f, b_e, c_e = (joined[3 * n : 3 * n + 3] for n in range(4))
        pairs = list(zip(c_e, b_f)) + list(zip(q_last, q_first))
        store(out_ref, [jnp.where(low, e, f) for e, f in pairs])
    else:
        store(out_ref, joined + q_first + q_last)


def x_merge_kernel(level, final, own_ref, other_ref, own_factor_ref, other_factor_ref, out_ref, side_ref):
    joined, side = merge_forced(
        bit_low("gx", level), load(own_ref) + load(own_factor_ref), load(other_ref) + load(other_factor_ref)
    )
    a_f, a_e = joined[:5], joined[5:10]
    if final:
        low = bit_low("gx", level + 1)
        store(out_ref, [jnp.where(low, e, f) for e, f in zip(a_e, a_f)])
    else:
        store(out_ref, a_f + a_e)
    store(side_ref, side)


def y_merge_kernel(level, final, own_ref, other_ref, out_ref, side_ref):
    joined, side = merge(bit_low("gy", level), load(own_ref), load(other_ref), PACKED_SPEED)
    if final:
        joined = facing(bit_low("gy", level + 1), joined, 2, 1)
    store(out_ref, joined)
    store(side_ref, side)


def outer_values(axis, levels, speed_of, own, other, side_refs):
    low = bit_low(axis, levels - 1)
    if axis == "gx":
        new = last_join_forced(low, own, other)
    else:
        new = last_join(low, own, other, speed_of)
    outer = from_last(low, new)
    for level in range(levels - 2, -1, -1):
        outer = step_down(bit_low(axis, level), load(side_refs[level]), outer, speed_of)
    return outer


PACKED_SPEED = (0, 0)


def regroup(parts, group):
    steps = len(parts)
    result = []
    for jj in range(steps):
        value = None
        for s in range(GROUPS):
            y = s * steps + jj
            piece = parts[y // GROUPS]
            shift = (s - y % GROUPS) * NZ % LANES
            piece = pltpu.roll(piece, shift, 1) if shift else piece
            value = piece if s == 0 else jnp.where(group == s, piece, value)
        result.append(value)
    return result


def lane_partner(values, group, level):
    if level == 0:
        return [
            jnp.where(group % 2 == 0, pltpu.roll(v, LANES - NZ, 1), pltpu.roll(v, NZ, 1)) for v in values
        ]
    return [pltpu.roll(v, LANES // 2, 1) for v in values]


def lane_low(group, level):
    return (group // 2 ** level) % 2 == 0


def y_factor_kernel(
    flow_ref, one_ref, two_ref, codes_ref,
    packed_ref, inverse_ref, lower_ref, up_ref, left_ref, right_ref, join_ref, side_ref,
):
    cells = flow_ref.shape[1]
    chunks = flow_ref.shape[2] // LANES
    lane = lax.broadcasted_iota(jnp.int32, (cells, LANES), 1)
    group = lane // NZ
    vels, sounds = [], []
    for c in range(chunks):
        prim = primitives([flow_ref[f, :, c * LANES : (c + 1) * LANES] for f in range(5)])
        vels.append(prim[2])
        sounds.append(prim[6])
    speeds = [three_speeds(v, c) for v, c in zip(regroup(vels, group), regroup(sounds, group))]
    lows, highs = zip(*[y_halos(flow_ref, one_ref, two_ref, f) for f in range(5)])
    low_prim, high_prim = primitives(lows), primitives(highs)
    low_speed = three_speeds(low_prim[2], low_prim[6])
    high_speed = three_speeds(high_prim[2], high_prim[6])
    before = tuple(
        pltpu.roll(jnp.where(group == GROUPS - 1, low_speed[k], speeds[-1][k]), NZ, 1) for k in range(3)
    )
    after = tuple(
        pltpu.roll(jnp.where(group == 0, high_speed[k], speeds[0][k]), LANES - NZ, 1) for k in range(3)
    )
    parts = factor([before] + speeds + [after], *y_edges(codes_ref, (cells, LANES)))
    for ref, values in zip((inverse_ref, lower_ref, up_ref, left_ref, right_ref), parts):
        for i in range(chunks):
            store(ref.at[i], values[i])
    lefts, rights = parts[3:]
    ends = lefts[0] + rights[0] + lefts[-1] + rights[-1]
    for level in range(2):
        low = lane_low(group, level)
        other = lane_partner(ends, group, level)
        before = [jnp.where(low, a, b) for a, b in zip(ends, other)]
        after = [jnp.where(low, b, a) for a, b in zip(ends, other)]
        b_f, c_f, b_e, c_e = (before[3 * n : 3 * n + 3] for n in range(4))
        b_g, c_g, b_h, c_h = (after[3 * n : 3 * n + 3] for n in range(4))
        inv = [1.0 / (1.0 - c_e[k] * b_g[k]) for k in range(3)]
        store(join_ref.at[level], inv + c_e + b_g + c_f + b_h)
        ends, e, f = join(([], [], b_f, c_f, b_e, c_e), ([], [], b_g, c_g, b_h, c_h), ())
        store(side_ref.at[level], [jnp.where(low, b, a) for a, b in zip(e, f)])
    store(packed_ref, [four(group, t[0], t[1], t[2], t[1]) for t in (ends[3 * n : 3 * n + 3] for n in range(4))])


def y_kernel(levels, *refs):
    (qx_ref, own_ref, left_ref, right_ref, mine_ref, other_ref, mine_factor_ref, other_factor_ref,
     packed_ref, inverse_ref, lower_ref, up_ref, join_ref) = refs[:13]
    sides = refs[13 : 13 + levels - 1]
    out_ref, yown_ref, side_ref, turn_ref = refs[13 + levels - 1 :]
    chunks = qx_ref.shape[1] // own_ref.shape[0]
    cells = own_ref.shape[0]
    steps = chunks
    mine, other = load(mine_ref) + load(mine_factor_ref), load(other_ref) + load(other_factor_ref)
    outer_l, outer_r = outer_values("gx", levels, SPEED_OF, mine, other, sides)
    for i in range(cells):
        q = [qx_ref[f, i * chunks : (i + 1) * chunks, :] for f in range(5)]
        sound = primitives(q)[6]
        wave = [
            own_ref[i, f] + left_ref[i, SPEED_OF[f]] * outer_l[f] + right_ref[i, SPEED_OF[f]] * outer_r[f]
            for f in range(5)
        ]
        impedance = q[0] * sound
        squared = sound * sound
        dp = 0.5 * (wave[0] + wave[4])
        du = (wave[4] - wave[0]) / (2.0 * impedance)
        dr = (wave[1] + dp) / squared
        normal = impedance * wave[2]
        values = [dp - normal, squared * dr - dp, du, wave[3], dp + normal]
        for n, value in enumerate(values):
            turn_ref[n, i * chunks : (i + 1) * chunks, :] = value
    lane = lax.broadcasted_iota(jnp.int32, (cells, LANES), 1)
    group = lane // NZ
    fields = [
        regroup([turn_ref[n, pl.ds(c, cells, stride=chunks), :] for c in range(chunks)], group)
        for n in range(5)
    ]
    sources = [[fields[f][jj] for f in range(5)] for jj in range(steps)]
    owns = substitute(*([load(ref.at[i]) for i in range(steps)] for ref in (inverse_ref, lower_ref, up_ref)), sources)
    for i in range(steps):
        store(yown_ref.at[i], owns[i])
    a_f, a_e = owns[0], owns[-1]
    for level in range(2):
        low = lane_low(group, level)
        other = lane_partner(a_f + a_e, group, level)
        parts = load(join_ref.at[level])
        inv, c_e, b_g, c_f, b_h = (parts[3 * n : 3 * n + 3] for n in range(5))
        before = [jnp.where(low, a, b) for a, b in zip(a_f + a_e, other)]
        after = [jnp.where(low, b, a) for a, b in zip(a_f + a_e, other)]
        e, f, new_f, new_e = [], [], [], []
        for n in range(5):
            k = SPEED_OF[n]
            e.append((before[5 + n] + c_e[k] * after[n]) * inv[k])
            f.append((after[n] + b_g[k] * before[5 + n]) * inv[k])
            new_f.append(before[n] + c_f[k] * f[n])
            new_e.append(after[5 + n] + b_h[k] * e[n])
        a_f, a_e = new_f, new_e
        store(side_ref.at[level], [jnp.where(low, b, a) for a, b in zip(e, f)])
    rows = []
    for a in (a_f, a_e):
        rows += [four(group, a[0], a[1], a[4], a[2]), a[3]]
    store(out_ref, rows + load(packed_ref))


def four(group, a, b, c, d):
    return jnp.where(group == 0, a, jnp.where(group == 1, b, jnp.where(group == 2, c, d)))


def spread(group, value, source):
    half = jnp.where(group // 2 == source // 2, value, pltpu.roll(value, LANES // 2, 1))
    down, up = pltpu.roll(half, NZ, 1), pltpu.roll(half, LANES - NZ, 1)
    if source % 2 == 0:
        return jnp.where(group % 2 == 0, half, down)
    return jnp.where(group % 2 == 1, half, up)


def final_kernel(levels, *refs):
    (flow_ref, yown_ref, yleft_ref, yright_ref, ends_ref, side_ref, mine_ref, other_ref) = refs[:8]
    sides = refs[8 : 8 + levels - 1]
    out_hbm, out_ref, sems = refs[8 + levels - 1 :]
    cells = flow_ref.shape[1]
    chunks = flow_ref.shape[2] // LANES
    steps = chunks
    lane = lax.broadcasted_iota(jnp.int32, (cells, LANES), 1)
    group = lane // NZ
    outer = outer_values("gy", levels, PACKED_SPEED, load(mine_ref), load(other_ref), sides)
    outer = tuple(
        [spread(group, v[0], 0), spread(group, v[0], 1), spread(group, v[0], 3),
         spread(group, v[1], 1), spread(group, v[0], 2)]
        for v in outer
    )
    for level in (1, 0):
        side = load(ends_ref.at[level]) + load(side_ref.at[level])
        outer = step_down(lane_low(group, level), side, outer, SPEED_OF)
    outer_l, outer_r = outer
    solved = [
        [
            yown_ref[j, f] + yleft_ref[j, SPEED_OF[f]] * outer_l[f] + yright_ref[j, SPEED_OF[f]] * outer_r[f]
            for f in range(5)
        ]
        for j in range(steps)
    ]
    copies = []
    for c in range(chunks):
        wave = []
        for f in range(5):
            value = None
            for g in range(GROUPS):
                y = c * GROUPS + g
                piece = solved[y % steps][f]
                shift = (g - y // steps) * NZ % LANES
                piece = pltpu.roll(piece, shift, 1) if shift else piece
                value = piece if g == 0 else jnp.where(group == g, piece, value)
            wave.append(value)
        q = [flow_ref[f, :, c * LANES : (c + 1) * LANES] for f in range(5)]
        inverse, vel_u, vel_v, vel_w, kinetic, pressure, sound = primitives(q)
        dp = 0.5 * (wave[0] + wave[4])
        dv = (wave[4] - wave[0]) / (2.0 * q[0] * sound)
        dr = (wave[1] + dp) / (sound * sound)
        du, dw = wave[2], wave[3]
        energy = (
            kinetic * dr + q[0] * (vel_u * du + vel_v * dv + vel_w * dw) + dp * (1.0 / (GAMMA - 1.0))
        )
        result = [dr, vel_u * dr + q[0] * du, vel_v * dr + q[0] * dv, vel_w * dr + q[0] * dw, energy]
        for f in range(5):
            out_ref[f, :, c * LANES : (c + 1) * LANES] = result[f]
        part = (slice(None), slice(None), slice(c * LANES, (c + 1) * LANES))
        copies.append(pltpu.make_async_copy(out_ref.at[part], out_hbm.at[part], sems.at[c]))
        copies[-1].start()
    for copy in copies:
        copy.wait()


def call(kernel, name, args, outs, scratch=(), out_hbm=False):
    vmem, hbm = (pl.BlockSpec(memory_space=space) for space in (pltpu.VMEM, pltpu.HBM))
    return pl.pallas_call(
        kernel,
        out_shape=[jax.ShapeDtypeStruct(shape, jnp.float32) for shape in outs],
        in_specs=[vmem] * len(args),
        out_specs=[hbm if out_hbm else vmem] * len(outs),
        scratch_shapes=list(scratch),
        compiler_params=pltpu.CompilerParams(vmem_limit_bytes=16 * 1024 * 1024),
        name=name,
    )(*args)


def pairs_at(count, level):
    return [(i, i ^ (1 << level)) for i in range(count)]


def pairs_across(count, level):
    return [(i, i ^ (1 << level) ^ (1 if level else 0)) for i in range(count)]


def snake(count_x, count_y):
    pairs = []
    for x in range(count_x):
        for y in range(count_y):
            to = y + 1 if x % 2 == 0 else y - 1
            inside = 0 <= to < count_y
            pairs.append((x * count_y + y, x * count_y + to if inside else (x ^ 1) * count_y + y))
    return pairs


def levels_of(count):
    levels = count.bit_length() - 1
    assert count == 1 << levels and levels >= 2
    return levels


def local(flow, x_codes, y_codes):
    cells = flow.shape[1]
    columns = flow.shape[2]
    chunks = columns // LANES
    count_x, count_y = lax.axis_size("gx"), lax.axis_size("gy")
    levels_x, levels_y = levels_of(count_x), levels_of(count_y)
    tile_x, tile_y = (chunks, LANES), (cells, LANES)

    qx, one, two = call(
        pack_kernel, "pack", [flow], [(5, cells * chunks, LANES), (5,) + tile_y, (5,) + tile_y]
    )
    round_trip = snake(count_x, count_y)
    one = lax.ppermute(one, ("gx", "gy"), round_trip)
    two = lax.ppermute(two, ("gx", "gy"), [(b, a) for a, b in round_trip])

    factors, inverse, lower, upper, left, right = call(
        x_factor_kernel, "xfactor", [qx, x_codes], [(COEFS + 10,) + tile_x] + [(cells, 3) + tile_x] * 5
    )
    (source,) = call(x_source_kernel, "xsource", [qx], [(cells, 5) + tile_x])
    all_factors = []
    for level in range(levels_x):
        other = lax.ppermute(factors, "gx", pairs_across(count_x, level))
        all_factors.append((factors, other))
        if level < levels_x - 1:
            final = level == levels_x - 2
            (factors,) = call(
                functools.partial(x_merge_factor_kernel, level, final), f"xfactor{level}",
                [factors, other], [(8 if final else COEFS + 10,) + tile_x],
            )
    rows, own = call(
        x_kernel, "xsweep", [flow, one, two, source, inverse, lower, upper],
        [(10,) + tile_x, (cells, 5) + tile_x],
        [pltpu.VMEM((5,) + tile_y, jnp.float32), pltpu.VMEM((5,) + tile_y, jnp.float32)],
    )
    sides = []
    for level in range(levels_x - 1):
        other = lax.ppermute(rows, "gx", pairs_across(count_x, level))
        final = level == levels_x - 2
        rows, side_rows = call(
            functools.partial(x_merge_kernel, level, final), f"xmerge{level}",
            [rows, other, *all_factors[level]], [(5 if final else 10,) + tile_x, (11,) + tile_x],
        )
        sides.append(side_rows)
    other = lax.ppermute(rows, "gx", pairs_across(count_x, levels_x - 1))
    y_factors, yinverse, ylower, yup, yleft, yright, yjoin, yside = call(
        y_factor_kernel, "yfactor", [flow, one, two, y_codes],
        [(4,) + tile_y] + [(chunks, 3) + tile_y] * 5 + [(2, 15) + tile_y, (2, 6) + tile_y],
    )
    packed, yown, yends = call(
        functools.partial(y_kernel, levels_x), "ysweep",
        [qx, own, left, right, rows, other, *all_factors[-1], y_factors, yinverse, ylower, yup, yjoin] + sides,
        [(8,) + tile_y, (chunks, 5) + tile_y, (2, 5) + tile_y],
        [pltpu.VMEM((5, cells * chunks, LANES), jnp.float32)],
    )
    sides = []
    for level in range(levels_y - 1):
        other = lax.ppermute(packed, "gy", pairs_at(count_y, level))
        final = level == levels_y - 2
        packed, side_rows = call(
            functools.partial(y_merge_kernel, level, final), f"ymerge{level}",
            [packed, other], [(3 if final else 8,) + tile_y, (4,) + tile_y],
        )
        sides.append(side_rows)
    other = lax.ppermute(packed, "gy", pairs_at(count_y, levels_y - 1))
    (result,) = call(
        functools.partial(final_kernel, levels_y), "final",
        [flow, yown, yleft, yright, yends, yside, packed, other] + sides,
        [(5, cells, columns)],
        [pltpu.VMEM((5, cells, columns), jnp.float32), pltpu.SemaphoreType.DMA((chunks,))],
        out_hbm=True,
    )
    return result


def solution(mesh):
    in_specs = (P(None, "gx", "gy"), P(None, "gy"), P(None, "gx"))
    out_specs = P(None, "gx", "gy")
    return jax.shard_map(local, mesh=mesh, in_specs=in_specs, out_specs=out_specs, check_vma=False)
```

```python
import functools

import jax
import jax.numpy as jnp
from jax import lax
from jax.experimental import pallas as pl
from jax.experimental.pallas import tpu as pltpu
from jax.sharding import PartitionSpec as P


NZ = 32
GAMMA = 1.4
SIGMA = 0.5
DIFFUSE = 400.0
LANES = 128
GROUPS = LANES // NZ
SPEED_OF = (0, 1, 1, 1, 2)
COEFS = 12


def primitives(q):
    inverse = 1.0 / q[0]
    vel_u, vel_v, vel_w = q[1] * inverse, q[2] * inverse, q[3] * inverse
    kinetic = 0.5 * (vel_u * vel_u + vel_v * vel_v + vel_w * vel_w)
    pressure = (GAMMA - 1.0) * (q[4] - q[0] * kinetic)
    sound = jnp.sqrt(GAMMA * pressure * inverse)
    return inverse, vel_u, vel_v, vel_w, kinetic, pressure, sound


def flux_of(q, normal, speed, pressure):
    return [q[normal]] + [
        q[f] * speed + pressure if f == normal else q[f] * speed for f in (1, 2, 3)
    ] + [speed * (q[4] + pressure)]


def three_speeds(velocity, sound):
    return (velocity - sound, velocity, velocity + sound)


def x_characteristics(res, density, prim):
    inverse, vel_u, vel_v, vel_w, kinetic, _, sound = prim
    du = (res[1] - vel_u * res[0]) * inverse
    dv = (res[2] - vel_v * res[0]) * inverse
    dw = (res[3] - vel_w * res[0]) * inverse
    dp = (GAMMA - 1.0) * (
        res[4] - vel_u * res[1] - vel_v * res[2] - vel_w * res[3] + kinetic * res[0]
    )
    normal = density * sound * du
    return [dp - normal, sound * sound * res[0] - dp, dv, dw, dp + normal]


def factor(speeds, first, last, forced=False):
    cells = len(speeds) - 2
    inverses, lowers, ups, lefts = [], [], [], []
    for i in range(cells):
        parts = []
        for k in range(3):
            lower = -0.5 * SIGMA * speeds[i][k] - DIFFUSE
            upper = 0.5 * SIGMA * speeds[i + 2][k] - DIFFUSE
            main = 1.0 + 2.0 * DIFFUSE
            if i == 0:
                main = main + lower * first[1]
                lower = None if forced else lower * first[0]
            if i == cells - 1:
                main = main + upper * last[1]
                upper = None if forced else upper * last[0]
            pivot = main if i == 0 else main - lower * ups[-1][k]
            inverse = 1.0 / pivot
            scaled = -inverse if lower is None else lower * inverse
            left = -scaled if i == 0 else -scaled * lefts[-1][k]
            parts.append((inverse, scaled, -inverse if upper is None else upper * inverse, left))
        for out, values in zip((inverses, lowers, ups, lefts), zip(*parts)):
            out.append(list(values))
    rights = [None] * cells
    rights[-1] = [-u for u in ups[-1]]
    for i in range(cells - 2, -1, -1):
        lefts[i] = [lefts[i][k] - ups[i][k] * lefts[i + 1][k] for k in range(3)]
        rights[i] = [-ups[i][k] * rights[i + 1][k] for k in range(3)]
    return inverses, lowers, ups, lefts, rights


def substitute(inverses, lowers, ups, sources):
    cells = len(sources)
    owns = []
    for i in range(cells):
        own = [sources[i][f] * inverses[i][SPEED_OF[f]] for f in range(5)]
        if i:
            own = [own[f] - lowers[i][SPEED_OF[f]] * owns[-1][f] for f in range(5)]
        owns.append(own)
    for i in range(cells - 2, -1, -1):
        owns[i] = [owns[i][f] - ups[i][SPEED_OF[f]] * owns[i + 1][f] for f in range(5)]
    return owns


def unpack(rows, fields=5, speeds=3):
    out, at = [], 0
    for n in (fields, fields, speeds, speeds, speeds, speeds):
        out.append(rows[at : at + n])
        at += n
    return out


def join(before, after, speed_of):
    fields = len(speed_of)
    a_f, a_e, b_f, c_f, b_e, c_e = before
    speeds = len(b_f)
    a_g, a_h, b_g, c_g, b_h, c_h = after
    inv = [1.0 / (1.0 - c_e[k] * b_g[k]) for k in range(speeds)]
    e_1 = [b_e[k] * inv[k] for k in range(speeds)]
    f_2 = [c_g[k] * inv[k] for k in range(speeds)]
    e_2 = [c_e[k] * f_2[k] for k in range(speeds)]
    f_1 = [b_g[k] * e_1[k] for k in range(speeds)]
    e_0 = [(a_e[f] + c_e[speed_of[f]] * a_g[f]) * inv[speed_of[f]] for f in range(fields)]
    f_0 = [(a_g[f] + b_g[speed_of[f]] * a_e[f]) * inv[speed_of[f]] for f in range(fields)]
    joined = (
        [a_f[f] + c_f[speed_of[f]] * f_0[f] for f in range(fields)]
        + [a_h[f] + b_h[speed_of[f]] * e_0[f] for f in range(fields)]
        + [b_f[k] + c_f[k] * f_1[k] for k in range(speeds)]
        + [c_f[k] * f_2[k] for k in range(speeds)]
        + [b_h[k] * e_1[k] for k in range(speeds)]
        + [c_h[k] + b_h[k] * e_2[k] for k in range(speeds)]
    )
    return joined, e_0 + e_1 + e_2, f_0 + f_1 + f_2


def merge(low, own, other, speed_of):
    fields = len(speed_of)
    speeds = max(speed_of) + 1
    before = [jnp.where(low, a, b) for a, b in zip(own, other)]
    after = [jnp.where(low, b, a) for a, b in zip(own, other)]
    joined, e, f = join(unpack(before, fields, speeds), unpack(after, fields, speeds), speed_of)
    return joined, [jnp.where(low, b, a) for a, b in zip(e, f)]


def facing(low, rows, fields=5, speeds=3):
    a_f, a_e, b_f, _, _, c_e = unpack(rows, fields, speeds)
    return [jnp.where(low, e, f) for e, f in zip(a_e + c_e, a_f + b_f)]


def join_factors(q_before, q_after):
    prim_b, prim_a = primitives(q_before), primitives(q_after)
    flux_b = flux_of(q_before, 1, prim_b[1], prim_b[5])
    flux_a = flux_of(q_after, 1, prim_a[1], prim_a[5])
    change = [-0.5 * SIGMA * (a - b) for a, b in zip(flux_a, flux_b)]
    smooth = [DIFFUSE * (a - b) for a, b in zip(q_after, q_before)]
    h_b = x_characteristics([c + d for c, d in zip(change, smooth)], q_before[0], prim_b)
    h_a = x_characteristics([c - d for c, d in zip(change, smooth)], q_after[0], prim_a)
    u_b = [DIFFUSE - 0.5 * SIGMA * v for v in three_speeds(prim_a[1], prim_a[6])]
    l_a = [DIFFUSE + 0.5 * SIGMA * v for v in three_speeds(prim_b[1], prim_b[6])]
    return h_b, u_b, h_a, l_a


def merge_forced(low, own, other):
    before = [jnp.where(low, a, b) for a, b in zip(own, other)]
    after = [jnp.where(low, b, a) for a, b in zip(own, other)]
    q_before, q_after = before[-5:], after[-10:-5]
    h_b, u_b, h_a, l_a = join_factors(q_before, q_after)
    a_f, a_e, b_f, c_f, b_e, c_e = unpack(before)
    a_g, a_h, b_g, c_g, b_h, c_h = unpack(after)
    a_f, a_e = ([a[f] + c[SPEED_OF[f]] * h_b[f] for f in range(5)] for a, c in ((a_f, c_f), (a_e, c_e)))
    a_g, a_h = ([a[f] + b[SPEED_OF[f]] * h_a[f] for f in range(5)] for a, b in ((a_g, b_g), (a_h, b_h)))
    c_f, c_e = ([c[k] * u_b[k] for k in range(3)] for c in (c_f, c_e))
    b_g, b_h = ([b[k] * l_a[k] for k in range(3)] for b in (b_g, b_h))
    joined, e, f = join(
        (a_f, a_e, b_f, c_f, b_e, c_e), (a_g, a_h, b_g, c_g, b_h, c_h), SPEED_OF
    )
    to_low = [h_b[n] + u_b[SPEED_OF[n]] * f[n] for n in range(5)]
    to_low += [u_b[k] * f[5 + 3 * t + k] for t in range(2) for k in range(3)]
    to_high = [h_a[n] + l_a[SPEED_OF[n]] * e[n] for n in range(5)]
    to_high += [l_a[k] * e[5 + 3 * t + k] for t in range(2) for k in range(3)]
    return joined, [jnp.where(low, a, b) for a, b in zip(to_low, to_high)]


def merge_factors(low, own, other):
    before = [jnp.where(low, a, b) for a, b in zip(own, other)]
    after = [jnp.where(low, b, a) for a, b in zip(own, other)]
    prim_b, prim_a = (primitives(q) for q in (before[-5:], after[-10:-5]))
    u_b = [DIFFUSE - 0.5 * SIGMA * v for v in three_speeds(prim_a[1], prim_a[6])]
    l_a = [DIFFUSE + 0.5 * SIGMA * v for v in three_speeds(prim_b[1], prim_b[6])]
    b_f, c_f, b_e, c_e = (before[3 * n : 3 * n + 3] for n in range(4))
    b_g, c_g, b_h, c_h = (after[3 * n : 3 * n + 3] for n in range(4))
    c_f, c_e = ([c[k] * u_b[k] for k in range(3)] for c in (c_f, c_e))
    b_g, b_h = ([b[k] * l_a[k] for k in range(3)] for b in (b_g, b_h))
    joined, _, _ = join(([], [], b_f, c_f, b_e, c_e), ([], [], b_g, c_g, b_h, c_h), ())
    return joined, before[-10:-5], after[-5:]


def last_join(own, other, speed_of):
    fields = len(speed_of)
    result = []
    for f in range(fields):
        k = fields + speed_of[f]
        result.append((other[f] + other[k] * own[f]) / (1.0 - own[k] * other[k]))
    return result


def last_join_forced(low, own, other):
    before = [jnp.where(low, a, b) for a, b in zip(own, other)]
    after = [jnp.where(low, b, a) for a, b in zip(own, other)]
    h_b, u_b, h_a, l_a = join_factors(before[8:], after[8:])
    h_own = [jnp.where(low, a, b) for a, b in zip(h_b, h_a)]
    h_other = [jnp.where(low, b, a) for a, b in zip(h_b, h_a)]
    k_own = [jnp.where(low, a, b) for a, b in zip(u_b, l_a)]
    k_other = [jnp.where(low, b, a) for a, b in zip(u_b, l_a)]
    mine, theirs = [], []
    for rows, h, k, out in ((own, h_own, k_own, mine), (other, h_other, k_other, theirs)):
        out.extend(rows[f] + rows[5 + SPEED_OF[f]] * h[f] for f in range(5))
        out.extend(rows[5 + n] * k[n] for n in range(3))
    value = last_join(mine, theirs, SPEED_OF)
    return [h_own[f] + k_own[SPEED_OF[f]] * value[f] for f in range(5)]


def step_down(low, side, outer, speed_of):
    fields = len(speed_of)
    speeds = max(speed_of) + 1
    left, right = outer
    new = [
        side[f] + side[fields + speed_of[f]] * left[f] + side[fields + speeds + speed_of[f]] * right[f]
        for f in range(fields)
    ]
    if isinstance(low, bool):
        return (left, new) if low else (new, right)
    return (
        [jnp.where(low, a, b) for a, b in zip(left, new)],
        [jnp.where(low, b, a) for a, b in zip(right, new)],
    )


def from_last(low, new):
    zero = jnp.zeros_like(new[0])
    return [jnp.where(low, zero, x) for x in new], [jnp.where(low, x, zero) for x in new]


def bit_low(axis, level):
    return (lax.axis_index(axis) >> level) % 2 == 0


def x_edges(codes_ref, shape):
    at, count = lax.axis_index("gx"), lax.axis_size("gx")
    lane = lax.broadcasted_iota(jnp.int32, shape, 1)
    sub = lax.broadcasted_iota(jnp.int32, shape, 0)
    width = codes_ref.shape[1]
    result = []
    place = lax.broadcasted_iota(jnp.int32, (shape[0], width), 1)
    row = lax.broadcasted_iota(jnp.int32, (shape[0], width), 0)
    for side, outer in ((0, at == 0), (1, at == count - 1)):
        codes = jnp.broadcast_to(codes_ref[side : side + 1, :], (shape[0], width))
        is_one = jnp.where(codes == 1, 1.0, 0.0)
        value = jnp.zeros(shape, jnp.float32)
        for g in range(GROUPS):
            mine = jnp.where(place == row * GROUPS + g, is_one, 0.0)
            column = jnp.sum(mine, axis=1, keepdims=True)
            value = jnp.where(lane // NZ == g, column, value)
        result.append(jnp.where(outer, value, 0.0))
    return result


def y_edges(codes_ref, shape):
    at, count = lax.axis_index("gy"), lax.axis_size("gy")
    group = lax.broadcasted_iota(jnp.int32, shape, 1) // NZ
    cells = shape[0]
    result = []
    place = lax.broadcasted_iota(jnp.int32, (cells, cells), 1)
    row = lax.broadcasted_iota(jnp.int32, (cells, cells), 0)
    for side, outer, face in ((0, at == 0, 0), (1, at == count - 1, GROUPS - 1)):
        codes = jnp.broadcast_to(codes_ref[side : side + 1, :], (cells, cells))
        mine = jnp.where(jnp.logical_and(codes == 1, place == row), 1.0, 0.0)
        value = jnp.broadcast_to(jnp.sum(mine, axis=1, keepdims=True), shape)
        at_face = jnp.logical_and(outer, group == face)
        result.append((jnp.where(at_face, 0.0, 1.0), jnp.where(at_face, value, 0.0)))
    return result


def to_group(value, source, target):
    shift = (target - source) * NZ % LANES
    return pltpu.roll(value, shift, 1) if shift else value


def pack_kernel(flow_ref, qx_ref, one_ref, two_ref):
    cells = flow_ref.shape[1]
    chunks = flow_ref.shape[2] // LANES
    even = bit_low("gx", 0)
    group = lax.broadcasted_iota(jnp.int32, (cells, LANES), 1) // NZ
    downs, ups = [], []
    for f in range(5):
        down = to_group(flow_ref[f, :, 0:LANES], 0, f % GROUPS)
        up = to_group(flow_ref[f, :, (chunks - 1) * LANES : chunks * LANES], GROUPS - 1, f % GROUPS)
        for rows, value in ((downs, down), (ups, up)):
            if f % GROUPS:
                rows[-1] = jnp.where(group == f % GROUPS, value, rows[-1])
            else:
                rows.append(value)
    for n, (down, up) in enumerate(zip(downs, ups)):
        one_ref[n] = jnp.where(even, up, down)
        two_ref[n] = jnp.where(even, down, up)
    for f in range(5):
        for c in range(chunks):
            qx_ref[f, pl.ds(c, cells, stride=chunks), :] = flow_ref[f, :, c * LANES : (c + 1) * LANES]


def y_halos(flow_ref, one_ref, two_ref, f):
    chunks = flow_ref.shape[2] // LANES
    at, count = lax.axis_index("gy"), lax.axis_size("gy")
    even = bit_low("gx", 0)
    low = jnp.where(even, one_ref[f // GROUPS], two_ref[f // GROUPS])
    high = jnp.where(even, two_ref[f // GROUPS], one_ref[f // GROUPS])
    low, high = to_group(low, f % GROUPS, GROUPS - 1), to_group(high, f % GROUPS, 0)
    own_low = to_group(flow_ref[f, :, 0:LANES], 0, GROUPS - 1)
    own_high = to_group(flow_ref[f, :, (chunks - 1) * LANES : chunks * LANES], GROUPS - 1, 0)
    return jnp.where(at == 0, own_low, low), jnp.where(at == count - 1, own_high, high)


def x_factor_kernel(
    qx_ref, codes_ref, out_ref, inverse_ref, lower_ref, up_ref, left_ref, right_ref, points_ref
):
    cells = inverse_ref.shape[0]
    chunks = inverse_ref.shape[2]
    rows = [[qx_ref[f, i * chunks : (i + 1) * chunks, :] for f in range(5)] for i in range(cells)]
    speeds, points = [], []
    for q in rows:
        prim = primitives(q)
        speeds.append(three_speeds(prim[1], prim[6]))
        impedance = q[0] * prim[6]
        points.append([impedance, 0.5 / impedance])
    for i in range(cells):
        store(points_ref.at[i], points[i])
    neumann = x_edges(codes_ref, (chunks, LANES))
    parts = factor(
        speeds[:1] + speeds + speeds[-1:], (None, neumann[0]), (None, neumann[1]), forced=True
    )
    for ref, values in zip((inverse_ref, lower_ref, up_ref, left_ref, right_ref), parts):
        for i in range(cells):
            store(ref.at[i], values[i])
    lefts, rights = parts[3:]
    store(out_ref, lefts[0] + rights[0] + lefts[-1] + rights[-1] + rows[0] + rows[-1])


def x_source_kernel(qx_ref, out_ref):
    cells = out_ref.shape[0]
    chunks = out_ref.shape[2]
    lane = lax.broadcasted_iota(jnp.int32, (chunks, LANES), 1)
    sub = lax.broadcasted_iota(jnp.int32, (chunks, LANES), 0)
    z_of = lane % NZ
    rows = [[qx_ref[f, i * chunks : (i + 1) * chunks, :] for f in range(5)] for i in range(cells)]
    prims = [primitives(q) for q in rows]
    fluxes = [flux_of(q, 1, p[1], p[5]) for q, p in zip(rows, prims)]
    rows, fluxes = (v[:1] + v + v[-1:] for v in (rows, fluxes))
    up_edge = jnp.logical_and(sub == chunks - 1, lane >= LANES - NZ)
    down_edge = jnp.logical_and(sub == 0, lane < NZ)

    def y_next(value):
        turned = pltpu.roll(value, LANES - NZ, 1)
        turned = jnp.where(lane >= LANES - NZ, pltpu.roll(turned, chunks - 1, 0), turned)
        return jnp.where(up_edge, value, turned)

    def y_before(value):
        turned = pltpu.roll(value, NZ, 1)
        turned = jnp.where(lane < NZ, pltpu.roll(turned, 1, 0), turned)
        return jnp.where(down_edge, value, turned)

    def z_change(value):
        after = jnp.where(z_of == NZ - 1, pltpu.roll(value, NZ - 1, 1), pltpu.roll(value, LANES - 1, 1))
        before = jnp.where(z_of == 0, pltpu.roll(value, LANES - NZ + 1, 1), pltpu.roll(value, 1, 1))
        return after - before

    for i in range(cells):
        q = rows[i + 1]
        _, _, vel_v, vel_w, _, pressure, _ = prims[i]
        after = [y_next(v) for v in list(q) + [vel_v, pressure]]
        before = [y_before(v) for v in list(q) + [vel_v, pressure]]
        flux_after = flux_of(after, 2, after[5], after[6])
        flux_before = flux_of(before, 2, before[5], before[6])
        flux_z = flux_of(q, 3, vel_w, pressure)
        res = []
        for f in range(5):
            change = (
                (fluxes[i + 2][f] - fluxes[i][f])
                + (flux_after[f] - flux_before[f])
                + z_change(flux_z[f])
            )
            smooth = rows[i + 2][f] + rows[i][f] + after[f] + before[f] - 4.0 * q[f]
            res.append(-0.5 * SIGMA * change + DIFFUSE * smooth)
        store(out_ref.at[i], x_characteristics(res, q[0], prims[i]))


def x_kernel(
    flow_ref, one_ref, two_ref, source_ref, inverse_ref, lower_ref, up_ref,
    rows_ref, own_ref, low_ref, high_ref,
):
    cells = flow_ref.shape[1]
    chunks = flow_ref.shape[2] // LANES
    lane = lax.broadcasted_iota(jnp.int32, (chunks, LANES), 1)
    sub = lax.broadcasted_iota(jnp.int32, (chunks, LANES), 0)
    up_edge = jnp.logical_and(sub == chunks - 1, lane >= LANES - NZ)
    down_edge = jnp.logical_and(sub == 0, lane < NZ)
    lows, highs = zip(*[y_halos(flow_ref, one_ref, two_ref, f) for f in range(5)])
    for ghosts, at, turn, sign, ref in (
        (lows, 0, NZ, 1.0, low_ref), (highs, chunks - 1, LANES - NZ, -1.0, high_ref)
    ):
        ghosts = [pltpu.roll(g, turn, 1) for g in ghosts]
        inner = [flow_ref[f, :, at * LANES : (at + 1) * LANES] for f in range(5)]
        ghost_prim, prim = primitives(ghosts), primitives(inner)
        ghost_flux = flux_of(ghosts, 2, ghost_prim[2], ghost_prim[5])
        inner_flux = flux_of(inner, 2, prim[2], prim[5])
        res = [
            sign * 0.5 * SIGMA * (ghost_flux[f] - inner_flux[f]) + DIFFUSE * (ghosts[f] - inner[f])
            for f in range(5)
        ]
        store(ref, x_characteristics(res, inner[0], prim))
    sources = []
    for i in range(cells):
        source = []
        for f in range(5):
            low = jnp.broadcast_to(low_ref[f, i : i + 1, :], (chunks, LANES))
            high = jnp.broadcast_to(high_ref[f, i : i + 1, :], (chunks, LANES))
            extra = jnp.where(down_edge, low, 0.0) + jnp.where(up_edge, high, 0.0)
            source.append(source_ref[i, f] + extra)
        sources.append(source)
    owns = substitute(*([load(ref.at[i]) for i in range(cells)] for ref in (inverse_ref, lower_ref, up_ref)), sources)
    for i in range(cells):
        store(own_ref.at[i], owns[i])
    store(rows_ref, owns[0] + owns[-1])


def load(ref):
    return [ref[n] for n in range(ref.shape[0])]


def store(ref, values):
    for n, value in enumerate(values):
        ref[n] = value


def x_merge_factor_kernel(level, final, own_ref, other_ref, out_ref):
    joined, q_first, q_last = merge_factors(bit_low("gx", level), load(own_ref), load(other_ref))
    if final:
        low = bit_low("gx", level + 1)
        b_f, _, _, c_e = (joined[3 * n : 3 * n + 3] for n in range(4))
        pairs = list(zip(c_e, b_f)) + list(zip(q_last, q_first))
        store(out_ref, [jnp.where(low, e, f) for e, f in pairs])
    else:
        store(out_ref, joined + q_first + q_last)


def x_merge_kernel(level, final, own_ref, other_ref, own_factor_ref, other_factor_ref, out_ref, side_ref):
    joined, side = merge_forced(
        bit_low("gx", level), load(own_ref) + load(own_factor_ref), load(other_ref) + load(other_factor_ref)
    )
    a_f, a_e = joined[:5], joined[5:10]
    if final:
        low = bit_low("gx", level + 1)
        store(out_ref, [jnp.where(low, e, f) for e, f in zip(a_e, a_f)])
    else:
        store(out_ref, a_f + a_e)
    store(side_ref, side)


def y_merge_kernel(level, final, own_ref, other_ref, out_ref, side_ref):
    joined, side = merge(bit_low("gy", level), load(own_ref), load(other_ref), PACKED_SPEED)
    if final:
        joined = facing(bit_low("gy", level + 1), joined, 2, 1)
    store(out_ref, joined)
    store(side_ref, side)


def outer_values(axis, levels, speed_of, own, other, side_refs):
    low = bit_low(axis, levels - 1)
    if axis == "gx":
        new = last_join_forced(low, own, other)
    else:
        new = last_join(own, other, speed_of)
    outer = from_last(low, new)
    for level in range(levels - 2, -1, -1):
        outer = step_down(bit_low(axis, level), load(side_refs[level]), outer, speed_of)
    return outer


PACKED_SPEED = (0, 0)


def regroup(parts, group):
    steps = len(parts)
    result = []
    for jj in range(steps):
        value = None
        for s in range(GROUPS):
            y = s * steps + jj
            piece = parts[y // GROUPS]
            shift = (s - y % GROUPS) * NZ % LANES
            piece = pltpu.roll(piece, shift, 1) if shift else piece
            value = piece if s == 0 else jnp.where(group == s, piece, value)
        result.append(value)
    return result


def lane_partner(values, group, level):
    if level == 0:
        return [
            jnp.where(group % 2 == 0, pltpu.roll(v, LANES - NZ, 1), pltpu.roll(v, NZ, 1)) for v in values
        ]
    return [pltpu.roll(v, LANES // 2, 1) for v in values]


def lane_low(group, level):
    return (group // 2 ** level) % 2 == 0


def y_factor_kernel(
    flow_ref, one_ref, two_ref, codes_ref,
    packed_ref, inverse_ref, lower_ref, up_ref, left_ref, right_ref, join_ref, side_ref,
):
    cells = flow_ref.shape[1]
    chunks = flow_ref.shape[2] // LANES
    lane = lax.broadcasted_iota(jnp.int32, (cells, LANES), 1)
    group = lane // NZ
    vels, sounds = [], []
    for c in range(chunks):
        prim = primitives([flow_ref[f, :, c * LANES : (c + 1) * LANES] for f in range(5)])
        vels.append(prim[2])
        sounds.append(prim[6])
    speeds = [three_speeds(v, c) for v, c in zip(regroup(vels, group), regroup(sounds, group))]
    lows, highs = zip(*[y_halos(flow_ref, one_ref, two_ref, f) for f in range(5)])
    low_prim, high_prim = primitives(lows), primitives(highs)
    low_speed = three_speeds(low_prim[2], low_prim[6])
    high_speed = three_speeds(high_prim[2], high_prim[6])
    before = tuple(
        pltpu.roll(jnp.where(group == GROUPS - 1, low_speed[k], speeds[-1][k]), NZ, 1) for k in range(3)
    )
    after = tuple(
        pltpu.roll(jnp.where(group == 0, high_speed[k], speeds[0][k]), LANES - NZ, 1) for k in range(3)
    )
    parts = factor([before] + speeds + [after], *y_edges(codes_ref, (cells, LANES)))
    for ref, values in zip((inverse_ref, lower_ref, up_ref, left_ref, right_ref), parts):
        for i in range(chunks):
            store(ref.at[i], values[i])
    lefts, rights = parts[3:]
    ends = lefts[0] + rights[0] + lefts[-1] + rights[-1]
    for level in range(2):
        low = lane_low(group, level)
        other = lane_partner(ends, group, level)
        before = [jnp.where(low, a, b) for a, b in zip(ends, other)]
        after = [jnp.where(low, b, a) for a, b in zip(ends, other)]
        b_f, c_f, b_e, c_e = (before[3 * n : 3 * n + 3] for n in range(4))
        b_g, c_g, b_h, c_h = (after[3 * n : 3 * n + 3] for n in range(4))
        inv = [1.0 / (1.0 - c_e[k] * b_g[k]) for k in range(3)]
        store(join_ref.at[level], inv + c_e + b_g + c_f + b_h)
        ends, e, f = join(([], [], b_f, c_f, b_e, c_e), ([], [], b_g, c_g, b_h, c_h), ())
        store(side_ref.at[level], [jnp.where(low, b, a) for a, b in zip(e, f)])
    store(packed_ref, [four(group, t[0], t[1], t[2], t[1]) for t in (ends[3 * n : 3 * n + 3] for n in range(4))])


def y_kernel(levels, *refs):
    (points_ref, own_ref, left_ref, right_ref, mine_ref, other_ref, mine_factor_ref, other_factor_ref,
     packed_ref, inverse_ref, lower_ref, up_ref, join_ref) = refs[:13]
    sides = refs[13 : 13 + levels - 1]
    out_ref, yown_ref, side_ref, turn_ref = refs[13 + levels - 1 :]
    chunks = own_ref.shape[2]
    cells = own_ref.shape[0]
    steps = chunks
    mine, other = load(mine_ref) + load(mine_factor_ref), load(other_ref) + load(other_factor_ref)
    outer_l, outer_r = outer_values("gx", levels, SPEED_OF, mine, other, sides)
    for i in range(cells):
        impedance, half_admittance = load(points_ref.at[i])
        wave = [
            own_ref[i, f] + left_ref[i, SPEED_OF[f]] * outer_l[f] + right_ref[i, SPEED_OF[f]] * outer_r[f]
            for f in range(5)
        ]
        dp = 0.5 * (wave[0] + wave[4])
        du = (wave[4] - wave[0]) * half_admittance
        normal = impedance * wave[2]
        values = [dp - normal, wave[1], du, wave[3], dp + normal]
        for n, value in enumerate(values):
            turn_ref[n, i * chunks : (i + 1) * chunks, :] = value
    lane = lax.broadcasted_iota(jnp.int32, (cells, LANES), 1)
    group = lane // NZ
    fields = [
        regroup([turn_ref[n, pl.ds(c, cells, stride=chunks), :] for c in range(chunks)], group)
        for n in range(5)
    ]
    sources = [[fields[f][jj] for f in range(5)] for jj in range(steps)]
    owns = substitute(*([load(ref.at[i]) for i in range(steps)] for ref in (inverse_ref, lower_ref, up_ref)), sources)
    for i in range(steps):
        store(yown_ref.at[i], owns[i])
    a_f, a_e = owns[0], owns[-1]
    for level in range(2):
        low = lane_low(group, level)
        other = lane_partner(a_f + a_e, group, level)
        parts = load(join_ref.at[level])
        inv, c_e, b_g, c_f, b_h = (parts[3 * n : 3 * n + 3] for n in range(5))
        before = [jnp.where(low, a, b) for a, b in zip(a_f + a_e, other)]
        after = [jnp.where(low, b, a) for a, b in zip(a_f + a_e, other)]
        e, f, new_f, new_e = [], [], [], []
        for n in range(5):
            k = SPEED_OF[n]
            e.append((before[5 + n] + c_e[k] * after[n]) * inv[k])
            f.append((after[n] + b_g[k] * before[5 + n]) * inv[k])
            new_f.append(before[n] + c_f[k] * f[n])
            new_e.append(after[5 + n] + b_h[k] * e[n])
        a_f, a_e = new_f, new_e
        store(side_ref.at[level], [jnp.where(low, b, a) for a, b in zip(e, f)])
    rows = []
    for a in (a_f, a_e):
        rows += [four(group, a[0], a[1], a[4], a[2]), a[3]]
    store(out_ref, rows + load(packed_ref))


def four(group, a, b, c, d):
    return jnp.where(group == 0, a, jnp.where(group == 1, b, jnp.where(group == 2, c, d)))


def spread(group, value, source):
    half = jnp.where(group // 2 == source // 2, value, pltpu.roll(value, LANES // 2, 1))
    down, up = pltpu.roll(half, NZ, 1), pltpu.roll(half, LANES - NZ, 1)
    if source % 2 == 0:
        return jnp.where(group % 2 == 0, half, down)
    return jnp.where(group % 2 == 1, half, up)


def ungroup(values, c, group):
    steps = len(values)
    result = None
    for g in range(GROUPS):
        y = c * GROUPS + g
        piece = to_group(values[y % steps], y // steps, g)
        result = piece if g == 0 else jnp.where(group == g, piece, result)
    return result


def prepare_kernel(
    flow_ref, yown_ref, yleft_ref, yright_ref, ends_ref, side_ref,
    terms_ref, points_ref, half_ref, quarter_ref,
):
    cells = flow_ref.shape[1]
    chunks = flow_ref.shape[2] // LANES
    group = lax.broadcasted_iota(jnp.int32, (cells, LANES), 1) // NZ
    columns = [
        [ref[j, n] for j in range(chunks)]
        for ref in (yown_ref, yleft_ref, yright_ref) for n in range(ref.shape[1])
    ]
    for c in range(chunks):
        store(terms_ref.at[c], [ungroup(column, c, group) for column in columns])
        q = [flow_ref[f, :, c * LANES : (c + 1) * LANES] for f in range(5)]
        _, vel_u, vel_v, vel_w, kinetic, _, sound = primitives(q)
        store(
            points_ref.at[c],
            [vel_u, vel_v, vel_w, kinetic, 1.0 / (2.0 * q[0] * sound), 1.0 / (sound * sound)],
        )
    for level, ref, count in ((1, half_ref, 2), (0, quarter_ref, GROUPS)):
        rows = load(ends_ref.at[level]) + load(side_ref.at[level])
        for n in range(count):
            store(ref.at[n], [spread(group, row, n * GROUPS // count) for row in rows])


def final_kernel(levels, *refs):
    (flow_ref, terms_ref, points_ref, half_ref, quarter_ref, mine_ref, other_ref) = refs[:7]
    sides = refs[7 : 7 + levels - 1]
    out_hbm, out_ref, sems = refs[7 + levels - 1 :]
    cells = flow_ref.shape[1]
    chunks = flow_ref.shape[2] // LANES
    group = lax.broadcasted_iota(jnp.int32, (cells, LANES), 1) // NZ
    outer = outer_values("gy", levels, PACKED_SPEED, load(mine_ref), load(other_ref), sides)
    outer = tuple(
        [spread(group, v[0], 0), spread(group, v[0], 1), spread(group, v[0], 3),
         spread(group, v[1], 1), spread(group, v[0], 2)]
        for v in outer
    )
    copies = []
    for s in range(GROUPS):
        half = step_down(s < GROUPS // 2, load(half_ref.at[s * 2 // GROUPS]), outer, SPEED_OF)
        outer_l, outer_r = step_down(s % 2 == 0, load(quarter_ref.at[s]), half, SPEED_OF)
        for c in range(s * chunks // GROUPS, (s + 1) * chunks // GROUPS):
            wave = [
                terms_ref[c, f] + terms_ref[c, 5 + SPEED_OF[f]] * outer_l[f]
                + terms_ref[c, 8 + SPEED_OF[f]] * outer_r[f]
                for f in range(5)
            ]
            density = flow_ref[0, :, c * LANES : (c + 1) * LANES]
            vel_u, vel_v, vel_w, kinetic, half_admittance, inverse_squared = load(points_ref.at[c])
            dp = 0.5 * (wave[0] + wave[4])
            dv = (wave[4] - wave[0]) * half_admittance
            dr = (wave[1] + dp) * inverse_squared
            du, dw = wave[2], wave[3]
            energy = (
                kinetic * dr + density * (vel_u * du + vel_v * dv + vel_w * dw)
                + dp * (1.0 / (GAMMA - 1.0))
            )
            result = [dr, vel_u * dr + density * du, vel_v * dr + density * dv, vel_w * dr + density * dw, energy]
            for f in range(5):
                out_ref[f, :, c * LANES : (c + 1) * LANES] = result[f]
        width = chunks // GROUPS * LANES
        part = (slice(None), slice(None), slice(s * width, (s + 1) * width))
        copies.append(pltpu.make_async_copy(out_ref.at[part], out_hbm.at[part], sems.at[s]))
        copies[-1].start()
    for copy in copies:
        copy.wait()


def call(kernel, args, outs, scratch=(), out_hbm=False):
    vmem, hbm = (pl.BlockSpec(memory_space=space) for space in (pltpu.VMEM, pltpu.HBM))
    return pl.pallas_call(
        kernel,
        out_shape=[jax.ShapeDtypeStruct(shape, jnp.float32) for shape in outs],
        in_specs=[vmem] * len(args),
        out_specs=[hbm if out_hbm else vmem] * len(outs),
        scratch_shapes=list(scratch),
        compiler_params=pltpu.CompilerParams(vmem_limit_bytes=16 * 1024 * 1024),
    )(*args)


def pairs_at(count, level):
    return [(i, i ^ (1 << level)) for i in range(count)]


def pairs_across(count, level):
    return [(i, i ^ (1 << level) ^ (1 if level else 0)) for i in range(count)]


def snake(count_x, count_y):
    pairs = []
    for x in range(count_x):
        for y in range(count_y):
            to = y + 1 if x % 2 == 0 else y - 1
            inside = 0 <= to < count_y
            pairs.append((x * count_y + y, x * count_y + to if inside else (x ^ 1) * count_y + y))
    return pairs


def levels_of(count):
    levels = count.bit_length() - 1
    assert count == 1 << levels and levels >= 2
    return levels


def local(flow, x_codes, y_codes):
    cells = flow.shape[1]
    columns = flow.shape[2]
    chunks = columns // LANES
    count_x, count_y = lax.axis_size("gx"), lax.axis_size("gy")
    levels_x, levels_y = levels_of(count_x), levels_of(count_y)
    tile_x, tile_y = (chunks, LANES), (cells, LANES)

    qx, one, two = call(pack_kernel, [flow], [(5, cells * chunks, LANES), (2,) + tile_y, (2,) + tile_y])
    round_trip = snake(count_x, count_y)
    one = lax.ppermute(one, ("gx", "gy"), round_trip)
    two = lax.ppermute(two, ("gx", "gy"), [(b, a) for a, b in round_trip])

    factors, inverse, lower, upper, left, right, xpoints = call(
        x_factor_kernel, [qx, x_codes],
        [(COEFS + 10,) + tile_x] + [(cells, 3) + tile_x] * 5 + [(cells, 2) + tile_x],
    )
    (source,) = call(x_source_kernel, [qx], [(cells, 5) + tile_x])
    all_factors = []
    for level in range(levels_x):
        other = lax.ppermute(factors, "gx", pairs_across(count_x, level))
        all_factors.append((factors, other))
        if level < levels_x - 1:
            final = level == levels_x - 2
            (factors,) = call(
                functools.partial(x_merge_factor_kernel, level, final),
                [factors, other], [(8 if final else COEFS + 10,) + tile_x],
            )
    rows, own = call(
        x_kernel, [flow, one, two, source, inverse, lower, upper],
        [(10,) + tile_x, (cells, 5) + tile_x],
        [pltpu.VMEM((5,) + tile_y, jnp.float32), pltpu.VMEM((5,) + tile_y, jnp.float32)],
    )
    sides = []
    for level in range(levels_x - 1):
        other = lax.ppermute(rows, "gx", pairs_across(count_x, level))
        final = level == levels_x - 2
        rows, side_rows = call(
            functools.partial(x_merge_kernel, level, final),
            [rows, other, *all_factors[level]], [(5 if final else 10,) + tile_x, (11,) + tile_x],
        )
        sides.append(side_rows)
    other = lax.ppermute(rows, "gx", pairs_across(count_x, levels_x - 1))
    y_factors, yinverse, ylower, yup, yleft, yright, yjoin, yside = call(
        y_factor_kernel, [flow, one, two, y_codes],
        [(4,) + tile_y] + [(chunks, 3) + tile_y] * 5 + [(2, 15) + tile_y, (2, 6) + tile_y],
    )
    packed, yown, yends = call(
        functools.partial(y_kernel, levels_x),
        [xpoints, own, left, right, rows, other, *all_factors[-1], y_factors, yinverse, ylower, yup, yjoin] + sides,
        [(8,) + tile_y, (chunks, 5) + tile_y, (2, 5) + tile_y],
        [pltpu.VMEM((5, cells * chunks, LANES), jnp.float32)],
    )
    prepared = call(
        prepare_kernel, [flow, yown, yleft, yright, yends, yside],
        [(chunks, 11) + tile_y, (chunks, 6) + tile_y, (2, 11) + tile_y, (GROUPS, 11) + tile_y],
    )
    sides = []
    for level in range(levels_y - 1):
        other = lax.ppermute(packed, "gy", pairs_at(count_y, level))
        final = level == levels_y - 2
        packed, side_rows = call(
            functools.partial(y_merge_kernel, level, final),
            [packed, other], [(3 if final else 8,) + tile_y, (4,) + tile_y],
        )
        sides.append(side_rows)
    other = lax.ppermute(packed, "gy", pairs_at(count_y, levels_y - 1))
    (result,) = call(
        functools.partial(final_kernel, levels_y),
        [flow, *prepared, packed, other] + sides,
        [(5, cells, columns)],
        [pltpu.VMEM((5, cells, columns), jnp.float32), pltpu.SemaphoreType.DMA((GROUPS,))],
        out_hbm=True,
    )
    return result


def solution(mesh):
    in_specs = (P(None, "gx", "gy"), P(None, "gy"), P(None, "gx"))
    out_specs = P(None, "gx", "gy")
    return jax.shard_map(local, mesh=mesh, in_specs=in_specs, out_specs=out_specs, check_vma=False)
```

```python
import functools

import jax
import jax.numpy as jnp
from jax import lax
from jax.experimental import pallas as pl
from jax.experimental.pallas import tpu as pltpu
from jax.sharding import PartitionSpec as P


NZ = 32
GAMMA = 1.4
SIGMA = 0.5
DIFFUSE = 400.0
LANES = 128
GROUPS = LANES // NZ
SPEED_OF = (0, 1, 1, 1, 2)
COEFS = 12


def primitives(q):
    inverse = 1.0 / q[0]
    vel_u, vel_v, vel_w = q[1] * inverse, q[2] * inverse, q[3] * inverse
    kinetic = 0.5 * (vel_u * vel_u + vel_v * vel_v + vel_w * vel_w)
    pressure = (GAMMA - 1.0) * (q[4] - q[0] * kinetic)
    sound = jnp.sqrt(GAMMA * pressure * inverse)
    return inverse, vel_u, vel_v, vel_w, kinetic, pressure, sound


def flux_of(q, normal, speed, pressure):
    return [q[normal]] + [
        q[f] * speed + pressure if f == normal else q[f] * speed for f in (1, 2, 3)
    ] + [speed * (q[4] + pressure)]


def three_speeds(velocity, sound):
    return (velocity - sound, velocity, velocity + sound)


def x_characteristics(res, density, prim):
    inverse, vel_u, vel_v, vel_w, kinetic, _, sound = prim
    du = (res[1] - vel_u * res[0]) * inverse
    dv = (res[2] - vel_v * res[0]) * inverse
    dw = (res[3] - vel_w * res[0]) * inverse
    dp = (GAMMA - 1.0) * (
        res[4] - vel_u * res[1] - vel_v * res[2] - vel_w * res[3] + kinetic * res[0]
    )
    normal = density * sound * du
    return [dp - normal, sound * sound * res[0] - dp, dv, dw, dp + normal]


def factor(speeds, first, last, forced=False):
    cells = len(speeds) - 2
    inverses, lowers, ups, lefts = [], [], [], []
    for i in range(cells):
        parts = []
        for k in range(3):
            lower = -0.5 * SIGMA * speeds[i][k] - DIFFUSE
            upper = 0.5 * SIGMA * speeds[i + 2][k] - DIFFUSE
            main = 1.0 + 2.0 * DIFFUSE
            if i == 0:
                main = main + lower * first[1]
                lower = None if forced else lower * first[0]
            if i == cells - 1:
                main = main + upper * last[1]
                upper = None if forced else upper * last[0]
            pivot = main if i == 0 else main - lower * ups[-1][k]
            inverse = 1.0 / pivot
            scaled = -inverse if lower is None else lower * inverse
            left = -scaled if i == 0 else -scaled * lefts[-1][k]
            parts.append((inverse, scaled, -inverse if upper is None else upper * inverse, left))
        for out, values in zip((inverses, lowers, ups, lefts), zip(*parts)):
            out.append(list(values))
    rights = [None] * cells
    rights[-1] = [-u for u in ups[-1]]
    for i in range(cells - 2, -1, -1):
        lefts[i] = [lefts[i][k] - ups[i][k] * lefts[i + 1][k] for k in range(3)]
        rights[i] = [-ups[i][k] * rights[i + 1][k] for k in range(3)]
    return inverses, lowers, ups, lefts, rights


def substitute(inverses, lowers, ups, sources):
    cells = len(sources)
    owns = []
    for i in range(cells):
        own = [sources[i][f] * inverses[i][SPEED_OF[f]] for f in range(5)]
        if i:
            own = [own[f] - lowers[i][SPEED_OF[f]] * owns[-1][f] for f in range(5)]
        owns.append(own)
    for i in range(cells - 2, -1, -1):
        owns[i] = [owns[i][f] - ups[i][SPEED_OF[f]] * owns[i + 1][f] for f in range(5)]
    return owns


def unpack(rows, fields=5, speeds=3):
    out, at = [], 0
    for n in (fields, fields, speeds, speeds, speeds, speeds):
        out.append(rows[at : at + n])
        at += n
    return out


def join(before, after, speed_of):
    fields = len(speed_of)
    a_f, a_e, b_f, c_f, b_e, c_e = before
    speeds = len(b_f)
    a_g, a_h, b_g, c_g, b_h, c_h = after
    inv = [1.0 / (1.0 - c_e[k] * b_g[k]) for k in range(speeds)]
    e_1 = [b_e[k] * inv[k] for k in range(speeds)]
    f_2 = [c_g[k] * inv[k] for k in range(speeds)]
    e_2 = [c_e[k] * f_2[k] for k in range(speeds)]
    f_1 = [b_g[k] * e_1[k] for k in range(speeds)]
    e_0 = [(a_e[f] + c_e[speed_of[f]] * a_g[f]) * inv[speed_of[f]] for f in range(fields)]
    f_0 = [(a_g[f] + b_g[speed_of[f]] * a_e[f]) * inv[speed_of[f]] for f in range(fields)]
    joined = (
        [a_f[f] + c_f[speed_of[f]] * f_0[f] for f in range(fields)]
        + [a_h[f] + b_h[speed_of[f]] * e_0[f] for f in range(fields)]
        + [b_f[k] + c_f[k] * f_1[k] for k in range(speeds)]
        + [c_f[k] * f_2[k] for k in range(speeds)]
        + [b_h[k] * e_1[k] for k in range(speeds)]
        + [c_h[k] + b_h[k] * e_2[k] for k in range(speeds)]
    )
    return joined, e_0 + e_1 + e_2, f_0 + f_1 + f_2


def merge(low, own, other, speed_of):
    fields = len(speed_of)
    speeds = max(speed_of) + 1
    before = [jnp.where(low, a, b) for a, b in zip(own, other)]
    after = [jnp.where(low, b, a) for a, b in zip(own, other)]
    joined, e, f = join(unpack(before, fields, speeds), unpack(after, fields, speeds), speed_of)
    return joined, [jnp.where(low, b, a) for a, b in zip(e, f)]


def join_factors(q_before, q_after):
    prim_b, prim_a = primitives(q_before), primitives(q_after)
    flux_b = flux_of(q_before, 1, prim_b[1], prim_b[5])
    flux_a = flux_of(q_after, 1, prim_a[1], prim_a[5])
    change = [-0.5 * SIGMA * (a - b) for a, b in zip(flux_a, flux_b)]
    smooth = [DIFFUSE * (a - b) for a, b in zip(q_after, q_before)]
    h_b = x_characteristics([c + d for c, d in zip(change, smooth)], q_before[0], prim_b)
    h_a = x_characteristics([c - d for c, d in zip(change, smooth)], q_after[0], prim_a)
    u_b = [DIFFUSE - 0.5 * SIGMA * v for v in three_speeds(prim_a[1], prim_a[6])]
    l_a = [DIFFUSE + 0.5 * SIGMA * v for v in three_speeds(prim_b[1], prim_b[6])]
    return h_b, u_b, h_a, l_a


def merge_forced(low, own, other):
    before = [jnp.where(low, a, b) for a, b in zip(own, other)]
    after = [jnp.where(low, b, a) for a, b in zip(own, other)]
    q_before, q_after = before[-5:], after[-10:-5]
    h_b, u_b, h_a, l_a = join_factors(q_before, q_after)
    a_f, a_e, b_f, c_f, b_e, c_e = unpack(before)
    a_g, a_h, b_g, c_g, b_h, c_h = unpack(after)
    a_f, a_e = ([a[f] + c[SPEED_OF[f]] * h_b[f] for f in range(5)] for a, c in ((a_f, c_f), (a_e, c_e)))
    a_g, a_h = ([a[f] + b[SPEED_OF[f]] * h_a[f] for f in range(5)] for a, b in ((a_g, b_g), (a_h, b_h)))
    c_f, c_e = ([c[k] * u_b[k] for k in range(3)] for c in (c_f, c_e))
    b_g, b_h = ([b[k] * l_a[k] for k in range(3)] for b in (b_g, b_h))
    joined, e, f = join(
        (a_f, a_e, b_f, c_f, b_e, c_e), (a_g, a_h, b_g, c_g, b_h, c_h), SPEED_OF
    )
    to_low = [h_b[n] + u_b[SPEED_OF[n]] * f[n] for n in range(5)]
    to_low += [u_b[k] * f[5 + 3 * t + k] for t in range(2) for k in range(3)]
    to_high = [h_a[n] + l_a[SPEED_OF[n]] * e[n] for n in range(5)]
    to_high += [l_a[k] * e[5 + 3 * t + k] for t in range(2) for k in range(3)]
    return joined, [jnp.where(low, a, b) for a, b in zip(to_low, to_high)]


def merge_factors(low, own, other):
    before = [jnp.where(low, a, b) for a, b in zip(own, other)]
    after = [jnp.where(low, b, a) for a, b in zip(own, other)]
    prim_b, prim_a = (primitives(q) for q in (before[-5:], after[-10:-5]))
    u_b = [DIFFUSE - 0.5 * SIGMA * v for v in three_speeds(prim_a[1], prim_a[6])]
    l_a = [DIFFUSE + 0.5 * SIGMA * v for v in three_speeds(prim_b[1], prim_b[6])]
    b_f, c_f, b_e, c_e = (before[3 * n : 3 * n + 3] for n in range(4))
    b_g, c_g, b_h, c_h = (after[3 * n : 3 * n + 3] for n in range(4))
    c_f, c_e = ([c[k] * u_b[k] for k in range(3)] for c in (c_f, c_e))
    b_g, b_h = ([b[k] * l_a[k] for k in range(3)] for b in (b_g, b_h))
    joined, _, _ = join(([], [], b_f, c_f, b_e, c_e), ([], [], b_g, c_g, b_h, c_h), ())
    return joined, before[-10:-5], after[-5:]


def last_join(own, other, speed_of):
    fields = len(speed_of)
    result = []
    for f in range(fields):
        k = fields + speed_of[f]
        result.append((other[f] + other[k] * own[f]) / (1.0 - own[k] * other[k]))
    return result


def last_join_forced(low, own, other):
    before = [jnp.where(low, a, b) for a, b in zip(own, other)]
    after = [jnp.where(low, b, a) for a, b in zip(own, other)]
    h_b, u_b, h_a, l_a = join_factors(before[8:], after[8:])
    h_own = [jnp.where(low, a, b) for a, b in zip(h_b, h_a)]
    h_other = [jnp.where(low, b, a) for a, b in zip(h_b, h_a)]
    k_own = [jnp.where(low, a, b) for a, b in zip(u_b, l_a)]
    k_other = [jnp.where(low, b, a) for a, b in zip(u_b, l_a)]
    mine, theirs = [], []
    for rows, h, k, out in ((own, h_own, k_own, mine), (other, h_other, k_other, theirs)):
        out.extend(rows[f] + rows[5 + SPEED_OF[f]] * h[f] for f in range(5))
        out.extend(rows[5 + n] * k[n] for n in range(3))
    value = last_join(mine, theirs, SPEED_OF)
    return [h_own[f] + k_own[SPEED_OF[f]] * value[f] for f in range(5)]


def step_down(low, side, outer, speed_of):
    fields = len(speed_of)
    speeds = max(speed_of) + 1
    left, right = outer
    new = [
        side[f] + side[fields + speed_of[f]] * left[f] + side[fields + speeds + speed_of[f]] * right[f]
        for f in range(fields)
    ]
    if isinstance(low, bool):
        return (left, new) if low else (new, right)
    return (
        [jnp.where(low, a, b) for a, b in zip(left, new)],
        [jnp.where(low, b, a) for a, b in zip(right, new)],
    )


def from_last(low, new):
    zero = jnp.zeros_like(new[0])
    return [jnp.where(low, zero, x) for x in new], [jnp.where(low, x, zero) for x in new]


def bit_low(axis, level):
    return (lax.axis_index(axis) >> level) % 2 == 0


def x_edges(codes_ref, shape):
    at, count = lax.axis_index("gx"), lax.axis_size("gx")
    lane = lax.broadcasted_iota(jnp.int32, shape, 1)
    sub = lax.broadcasted_iota(jnp.int32, shape, 0)
    width = codes_ref.shape[1]
    result = []
    place = lax.broadcasted_iota(jnp.int32, (shape[0], width), 1)
    row = lax.broadcasted_iota(jnp.int32, (shape[0], width), 0)
    for side, outer in ((0, at == 0), (1, at == count - 1)):
        codes = jnp.broadcast_to(codes_ref[side : side + 1, :], (shape[0], width))
        is_one = jnp.where(codes == 1, 1.0, 0.0)
        value = jnp.zeros(shape, jnp.float32)
        for g in range(GROUPS):
            mine = jnp.where(place == row * GROUPS + g, is_one, 0.0)
            column = jnp.sum(mine, axis=1, keepdims=True)
            value = jnp.where(lane // NZ == g, column, value)
        result.append(jnp.where(outer, value, 0.0))
    return result


def y_edges(codes_ref, shape):
    at, count = lax.axis_index("gy"), lax.axis_size("gy")
    group = lax.broadcasted_iota(jnp.int32, shape, 1) // NZ
    cells = shape[0]
    result = []
    place = lax.broadcasted_iota(jnp.int32, (cells, cells), 1)
    row = lax.broadcasted_iota(jnp.int32, (cells, cells), 0)
    for side, outer, face in ((0, at == 0, 0), (1, at == count - 1, GROUPS - 1)):
        codes = jnp.broadcast_to(codes_ref[side : side + 1, :], (cells, cells))
        mine = jnp.where(jnp.logical_and(codes == 1, place == row), 1.0, 0.0)
        value = jnp.broadcast_to(jnp.sum(mine, axis=1, keepdims=True), shape)
        at_face = jnp.logical_and(outer, group == face)
        result.append((jnp.where(at_face, 0.0, 1.0), jnp.where(at_face, value, 0.0)))
    return result


def to_group(value, source, target):
    shift = (target - source) * NZ % LANES
    return pltpu.roll(value, shift, 1) if shift else value


def pack_kernel(flow_ref, qx_ref, one_ref, two_ref):
    cells = flow_ref.shape[1]
    chunks = flow_ref.shape[2] // LANES
    even = bit_low("gx", 0)
    group = lax.broadcasted_iota(jnp.int32, (cells, LANES), 1) // NZ
    downs, ups = [], []
    for f in range(5):
        down = to_group(flow_ref[f, :, 0:LANES], 0, f % GROUPS)
        up = to_group(flow_ref[f, :, (chunks - 1) * LANES : chunks * LANES], GROUPS - 1, f % GROUPS)
        for rows, value in ((downs, down), (ups, up)):
            if f % GROUPS:
                rows[-1] = jnp.where(group == f % GROUPS, value, rows[-1])
            else:
                rows.append(value)
    for n, (down, up) in enumerate(zip(downs, ups)):
        one_ref[n] = jnp.where(even, up, down)
        two_ref[n] = jnp.where(even, down, up)
    for f in range(5):
        for c in range(chunks):
            qx_ref[f, pl.ds(c, cells, stride=chunks), :] = flow_ref[f, :, c * LANES : (c + 1) * LANES]


def y_halos(flow_ref, one_ref, two_ref, f):
    chunks = flow_ref.shape[2] // LANES
    at, count = lax.axis_index("gy"), lax.axis_size("gy")
    even = bit_low("gx", 0)
    low = jnp.where(even, one_ref[f // GROUPS], two_ref[f // GROUPS])
    high = jnp.where(even, two_ref[f // GROUPS], one_ref[f // GROUPS])
    low, high = to_group(low, f % GROUPS, GROUPS - 1), to_group(high, f % GROUPS, 0)
    own_low = to_group(flow_ref[f, :, 0:LANES], 0, GROUPS - 1)
    own_high = to_group(flow_ref[f, :, (chunks - 1) * LANES : chunks * LANES], GROUPS - 1, 0)
    return jnp.where(at == 0, own_low, low), jnp.where(at == count - 1, own_high, high)


def x_factor_kernel(
    qx_ref, codes_ref, out_ref, inverse_ref, lower_ref, up_ref, left_ref, right_ref, points_ref
):
    cells = inverse_ref.shape[0]
    chunks = inverse_ref.shape[2]
    rows = [[qx_ref[f, i * chunks : (i + 1) * chunks, :] for f in range(5)] for i in range(cells)]
    speeds, points = [], []
    for q in rows:
        prim = primitives(q)
        speeds.append(three_speeds(prim[1], prim[6]))
        impedance = q[0] * prim[6]
        points.append([impedance, 0.5 / impedance])
    for i in range(cells):
        store(points_ref.at[i], points[i])
    neumann = x_edges(codes_ref, (chunks, LANES))
    parts = factor(
        speeds[:1] + speeds + speeds[-1:], (None, neumann[0]), (None, neumann[1]), forced=True
    )
    for ref, values in zip((inverse_ref, lower_ref, up_ref, left_ref, right_ref), parts):
        for i in range(cells):
            store(ref.at[i], values[i])
    lefts, rights = parts[3:]
    store(out_ref, lefts[0] + rights[0] + lefts[-1] + rights[-1] + rows[0] + rows[-1])


def x_source_kernel(qx_ref, out_ref):
    cells = out_ref.shape[0]
    chunks = out_ref.shape[2]
    lane = lax.broadcasted_iota(jnp.int32, (chunks, LANES), 1)
    sub = lax.broadcasted_iota(jnp.int32, (chunks, LANES), 0)
    z_of = lane % NZ
    rows = [[qx_ref[f, i * chunks : (i + 1) * chunks, :] for f in range(5)] for i in range(cells)]
    prims = [primitives(q) for q in rows]
    fluxes = [flux_of(q, 1, p[1], p[5]) for q, p in zip(rows, prims)]
    rows, fluxes = (v[:1] + v + v[-1:] for v in (rows, fluxes))
    up_edge = jnp.logical_and(sub == chunks - 1, lane >= LANES - NZ)
    down_edge = jnp.logical_and(sub == 0, lane < NZ)

    def y_next(value):
        turned = pltpu.roll(value, LANES - NZ, 1)
        turned = jnp.where(lane >= LANES - NZ, pltpu.roll(turned, chunks - 1, 0), turned)
        return jnp.where(up_edge, value, turned)

    def y_before(value):
        turned = pltpu.roll(value, NZ, 1)
        turned = jnp.where(lane < NZ, pltpu.roll(turned, 1, 0), turned)
        return jnp.where(down_edge, value, turned)

    def z_change(value):
        after = jnp.where(z_of == NZ - 1, pltpu.roll(value, NZ - 1, 1), pltpu.roll(value, LANES - 1, 1))
        before = jnp.where(z_of == 0, pltpu.roll(value, LANES - NZ + 1, 1), pltpu.roll(value, 1, 1))
        return after - before

    for i in range(cells):
        q = rows[i + 1]
        _, _, vel_v, vel_w, _, pressure, _ = prims[i]
        after = [y_next(v) for v in list(q) + [vel_v, pressure]]
        before = [y_before(v) for v in list(q) + [vel_v, pressure]]
        flux_after = flux_of(after, 2, after[5], after[6])
        flux_before = flux_of(before, 2, before[5], before[6])
        flux_z = flux_of(q, 3, vel_w, pressure)
        res = []
        for f in range(5):
            change = (
                (fluxes[i + 2][f] - fluxes[i][f])
                + (flux_after[f] - flux_before[f])
                + z_change(flux_z[f])
            )
            smooth = rows[i + 2][f] + rows[i][f] + after[f] + before[f] - 4.0 * q[f]
            res.append(-0.5 * SIGMA * change + DIFFUSE * smooth)
        store(out_ref.at[i], x_characteristics(res, q[0], prims[i]))


def x_kernel(
    flow_ref, one_ref, two_ref, source_ref, inverse_ref, lower_ref, up_ref,
    rows_ref, own_ref, low_ref, high_ref,
):
    cells = flow_ref.shape[1]
    chunks = flow_ref.shape[2] // LANES
    lane = lax.broadcasted_iota(jnp.int32, (chunks, LANES), 1)
    sub = lax.broadcasted_iota(jnp.int32, (chunks, LANES), 0)
    up_edge = jnp.logical_and(sub == chunks - 1, lane >= LANES - NZ)
    down_edge = jnp.logical_and(sub == 0, lane < NZ)
    lows, highs = zip(*[y_halos(flow_ref, one_ref, two_ref, f) for f in range(5)])
    for ghosts, at, turn, sign, ref in (
        (lows, 0, NZ, 1.0, low_ref), (highs, chunks - 1, LANES - NZ, -1.0, high_ref)
    ):
        ghosts = [pltpu.roll(g, turn, 1) for g in ghosts]
        inner = [flow_ref[f, :, at * LANES : (at + 1) * LANES] for f in range(5)]
        ghost_prim, prim = primitives(ghosts), primitives(inner)
        ghost_flux = flux_of(ghosts, 2, ghost_prim[2], ghost_prim[5])
        inner_flux = flux_of(inner, 2, prim[2], prim[5])
        res = [
            sign * 0.5 * SIGMA * (ghost_flux[f] - inner_flux[f]) + DIFFUSE * (ghosts[f] - inner[f])
            for f in range(5)
        ]
        store(ref, x_characteristics(res, inner[0], prim))
    sources = []
    for i in range(cells):
        source = []
        for f in range(5):
            low = jnp.broadcast_to(low_ref[f, i : i + 1, :], (chunks, LANES))
            high = jnp.broadcast_to(high_ref[f, i : i + 1, :], (chunks, LANES))
            extra = jnp.where(down_edge, low, 0.0) + jnp.where(up_edge, high, 0.0)
            source.append(source_ref[i, f] + extra)
        sources.append(source)
    owns = substitute(*([load(ref.at[i]) for i in range(cells)] for ref in (inverse_ref, lower_ref, up_ref)), sources)
    for i in range(cells):
        store(own_ref.at[i], owns[i])
    store(rows_ref, owns[0] + owns[-1])


def load(ref):
    return [ref[n] for n in range(ref.shape[0])]


def store(ref, values):
    for n, value in enumerate(values):
        ref[n] = value


def x_merge_factor_kernel(level, final, own_ref, other_ref, out_ref):
    joined, q_first, q_last = merge_factors(bit_low("gx", level), load(own_ref), load(other_ref))
    if final:
        low = bit_low("gx", level + 1)
        b_f, _, _, c_e = (joined[3 * n : 3 * n + 3] for n in range(4))
        pairs = list(zip(c_e, b_f)) + list(zip(q_last, q_first))
        store(out_ref, [jnp.where(low, e, f) for e, f in pairs])
    else:
        store(out_ref, joined + q_first + q_last)


def x_merge_kernel(level, final, own_ref, other_ref, own_factor_ref, other_factor_ref, out_ref, side_ref):
    joined, side = merge_forced(
        bit_low("gx", level), load(own_ref) + load(own_factor_ref), load(other_ref) + load(other_factor_ref)
    )
    a_f, a_e = joined[:5], joined[5:10]
    if final:
        low = bit_low("gx", level + 1)
        store(out_ref, [jnp.where(low, e, f) for e, f in zip(a_e, a_f)])
    else:
        store(out_ref, a_f + a_e)
    store(side_ref, side)


def y_merge_kernel(level, own_ref, other_ref, out_ref, side_ref):
    joined, side = merge(bit_low("gy", level), load(own_ref), load(other_ref), PACKED_SPEED)
    store(out_ref, joined)
    store(side_ref, side)


def outer_values(levels, own, other, side_refs):
    low = bit_low("gx", levels - 1)
    outer = from_last(low, last_join_forced(low, own, other))
    for level in range(levels - 2, -1, -1):
        outer = step_down(bit_low("gx", level), load(side_refs[level]), outer, SPEED_OF)
    return outer


def pick(place, values):
    return [
        functools.reduce(lambda old, n: jnp.where(place == n, items[n], old), range(1, len(items)), items[0])
        for items in zip(*values)
    ]


def outer_of_four(place, own, arrived, speed_of):
    fields, speeds = len(speed_of), max(speed_of) + 1
    ring = [own] + arrived
    segments = [unpack(pick((place - n) % 4, ring), fields, speeds) for n in range(4)]
    left, e_left, f_left = join(segments[0], segments[1], speed_of)
    right, e_right, f_right = join(segments[2], segments[3], speed_of)
    a_e, c_e = (unpack(left, fields, speeds)[n] for n in (1, 5))
    a_f, b_f = (unpack(right, fields, speeds)[n] for n in (0, 2))
    e_mid, f_mid, zero = [], [], jnp.zeros_like(a_e[0])
    inverse = [1.0 / (1.0 - c_e[k] * b_f[k]) for k in range(speeds)]
    for n in range(fields):
        k = speed_of[n]
        e_mid.append((a_e[n] + c_e[k] * a_f[n]) * inverse[k])
        f_mid.append((a_f[n] + b_f[k] * a_e[n]) * inverse[k])

    def inner(terms, outer, side):
        return [terms[n] + terms[fields + side * speeds + speed_of[n]] * outer[n] for n in range(fields)]

    lefts = [[zero] * fields, inner(e_left, f_mid, 1), e_mid, inner(e_right, e_mid, 0)]
    rights = [inner(f_left, f_mid, 1), f_mid, inner(f_right, e_mid, 0), [zero] * fields]
    return pick(place, lefts), pick(place, rights)


PACKED_SPEED = (0, 0)


def regroup(parts, group):
    steps = len(parts)
    result = []
    for jj in range(steps):
        value = None
        for s in range(GROUPS):
            y = s * steps + jj
            piece = parts[y // GROUPS]
            shift = (s - y % GROUPS) * NZ % LANES
            piece = pltpu.roll(piece, shift, 1) if shift else piece
            value = piece if s == 0 else jnp.where(group == s, piece, value)
        result.append(value)
    return result


def lane_partner(values, group, level):
    if level == 0:
        return [
            jnp.where(group % 2 == 0, pltpu.roll(v, LANES - NZ, 1), pltpu.roll(v, NZ, 1)) for v in values
        ]
    return [pltpu.roll(v, LANES // 2, 1) for v in values]


def lane_low(group, level):
    return (group // 2 ** level) % 2 == 0


def y_factor_kernel(
    flow_ref, one_ref, two_ref, codes_ref,
    packed_ref, inverse_ref, lower_ref, up_ref, left_ref, right_ref, join_ref, side_ref,
):
    cells = flow_ref.shape[1]
    chunks = flow_ref.shape[2] // LANES
    lane = lax.broadcasted_iota(jnp.int32, (cells, LANES), 1)
    group = lane // NZ
    vels, sounds = [], []
    for c in range(chunks):
        prim = primitives([flow_ref[f, :, c * LANES : (c + 1) * LANES] for f in range(5)])
        vels.append(prim[2])
        sounds.append(prim[6])
    speeds = [three_speeds(v, c) for v, c in zip(regroup(vels, group), regroup(sounds, group))]
    lows, highs = zip(*[y_halos(flow_ref, one_ref, two_ref, f) for f in range(5)])
    low_prim, high_prim = primitives(lows), primitives(highs)
    low_speed = three_speeds(low_prim[2], low_prim[6])
    high_speed = three_speeds(high_prim[2], high_prim[6])
    before = tuple(
        pltpu.roll(jnp.where(group == GROUPS - 1, low_speed[k], speeds[-1][k]), NZ, 1) for k in range(3)
    )
    after = tuple(
        pltpu.roll(jnp.where(group == 0, high_speed[k], speeds[0][k]), LANES - NZ, 1) for k in range(3)
    )
    parts = factor([before] + speeds + [after], *y_edges(codes_ref, (cells, LANES)))
    for ref, values in zip((inverse_ref, lower_ref, up_ref, left_ref, right_ref), parts):
        for i in range(chunks):
            store(ref.at[i], values[i])
    lefts, rights = parts[3:]
    ends = lefts[0] + rights[0] + lefts[-1] + rights[-1]
    for level in range(2):
        low = lane_low(group, level)
        other = lane_partner(ends, group, level)
        before = [jnp.where(low, a, b) for a, b in zip(ends, other)]
        after = [jnp.where(low, b, a) for a, b in zip(ends, other)]
        b_f, c_f, b_e, c_e = (before[3 * n : 3 * n + 3] for n in range(4))
        b_g, c_g, b_h, c_h = (after[3 * n : 3 * n + 3] for n in range(4))
        inv = [1.0 / (1.0 - c_e[k] * b_g[k]) for k in range(3)]
        store(join_ref.at[level], inv + c_e + b_g + c_f + b_h)
        ends, e, f = join(([], [], b_f, c_f, b_e, c_e), ([], [], b_g, c_g, b_h, c_h), ())
        store(side_ref.at[level], [jnp.where(low, b, a) for a, b in zip(e, f)])
    store(packed_ref, [four(group, t[0], t[1], t[2], t[1]) for t in (ends[3 * n : 3 * n + 3] for n in range(4))])


def y_kernel(levels, *refs):
    (points_ref, own_ref, left_ref, right_ref, mine_ref, other_ref, mine_factor_ref, other_factor_ref,
     packed_ref, inverse_ref, lower_ref, up_ref, join_ref) = refs[:13]
    sides = refs[13 : 13 + levels - 1]
    out_ref, yown_ref, side_ref, turn_ref = refs[13 + levels - 1 :]
    chunks = own_ref.shape[2]
    cells = own_ref.shape[0]
    steps = chunks
    mine, other = load(mine_ref) + load(mine_factor_ref), load(other_ref) + load(other_factor_ref)
    outer_l, outer_r = outer_values(levels, mine, other, sides)
    for i in range(cells):
        impedance, half_admittance = load(points_ref.at[i])
        wave = [
            own_ref[i, f] + left_ref[i, SPEED_OF[f]] * outer_l[f] + right_ref[i, SPEED_OF[f]] * outer_r[f]
            for f in range(5)
        ]
        dp = 0.5 * (wave[0] + wave[4])
        du = (wave[4] - wave[0]) * half_admittance
        normal = impedance * wave[2]
        values = [dp - normal, wave[1], du, wave[3], dp + normal]
        for n, value in enumerate(values):
            turn_ref[n, i * chunks : (i + 1) * chunks, :] = value
    lane = lax.broadcasted_iota(jnp.int32, (cells, LANES), 1)
    group = lane // NZ
    fields = [
        regroup([turn_ref[n, pl.ds(c, cells, stride=chunks), :] for c in range(chunks)], group)
        for n in range(5)
    ]
    sources = [[fields[f][jj] for f in range(5)] for jj in range(steps)]
    owns = substitute(*([load(ref.at[i]) for i in range(steps)] for ref in (inverse_ref, lower_ref, up_ref)), sources)
    for i in range(steps):
        store(yown_ref.at[i], owns[i])
    a_f, a_e = owns[0], owns[-1]
    for level in range(2):
        low = lane_low(group, level)
        other = lane_partner(a_f + a_e, group, level)
        parts = load(join_ref.at[level])
        inv, c_e, b_g, c_f, b_h = (parts[3 * n : 3 * n + 3] for n in range(5))
        before = [jnp.where(low, a, b) for a, b in zip(a_f + a_e, other)]
        after = [jnp.where(low, b, a) for a, b in zip(a_f + a_e, other)]
        e, f, new_f, new_e = [], [], [], []
        for n in range(5):
            k = SPEED_OF[n]
            e.append((before[5 + n] + c_e[k] * after[n]) * inv[k])
            f.append((after[n] + b_g[k] * before[5 + n]) * inv[k])
            new_f.append(before[n] + c_f[k] * f[n])
            new_e.append(after[5 + n] + b_h[k] * e[n])
        a_f, a_e = new_f, new_e
        store(side_ref.at[level], [jnp.where(low, b, a) for a, b in zip(e, f)])
    rows = []
    for a in (a_f, a_e):
        rows += [four(group, a[0], a[1], a[4], a[2]), a[3]]
    store(out_ref, rows + load(packed_ref))


def four(group, a, b, c, d):
    return jnp.where(group == 0, a, jnp.where(group == 1, b, jnp.where(group == 2, c, d)))


def spread(group, value, source):
    half = jnp.where(group // 2 == source // 2, value, pltpu.roll(value, LANES // 2, 1))
    down, up = pltpu.roll(half, NZ, 1), pltpu.roll(half, LANES - NZ, 1)
    if source % 2 == 0:
        return jnp.where(group % 2 == 0, half, down)
    return jnp.where(group % 2 == 1, half, up)


def ungroup(values, c, group):
    steps = len(values)
    result = None
    for g in range(GROUPS):
        y = c * GROUPS + g
        piece = to_group(values[y % steps], y // steps, g)
        result = piece if g == 0 else jnp.where(group == g, piece, result)
    return result


def prepare_kernel(
    flow_ref, yown_ref, yleft_ref, yright_ref, ends_ref, side_ref,
    terms_ref, points_ref, half_ref, quarter_ref,
):
    cells = flow_ref.shape[1]
    chunks = flow_ref.shape[2] // LANES
    group = lax.broadcasted_iota(jnp.int32, (cells, LANES), 1) // NZ
    columns = [
        [ref[j, n] for j in range(chunks)]
        for ref in (yown_ref, yleft_ref, yright_ref) for n in range(ref.shape[1])
    ]
    for c in range(chunks):
        store(terms_ref.at[c], [ungroup(column, c, group) for column in columns])
        q = [flow_ref[f, :, c * LANES : (c + 1) * LANES] for f in range(5)]
        _, vel_u, vel_v, vel_w, kinetic, _, sound = primitives(q)
        store(
            points_ref.at[c],
            [vel_u, vel_v, vel_w, kinetic, 1.0 / (2.0 * q[0] * sound), 1.0 / (sound * sound)],
        )
    for level, ref, count in ((1, half_ref, 2), (0, quarter_ref, GROUPS)):
        rows = load(ends_ref.at[level]) + load(side_ref.at[level])
        for n in range(count):
            store(ref.at[n], [spread(group, row, n * GROUPS // count) for row in rows])


def final_kernel(levels, *refs):
    (flow_ref, terms_ref, points_ref, half_ref, quarter_ref, mine_ref) = refs[:6]
    arrived, sides = refs[6:9], refs[9 : 9 + levels]
    out_hbm, out_ref, sems = refs[9 + levels :]
    cells = flow_ref.shape[1]
    chunks = flow_ref.shape[2] // LANES
    group = lax.broadcasted_iota(jnp.int32, (cells, LANES), 1) // NZ
    place = (lax.axis_index("gy") >> levels) % 4
    outer = outer_of_four(place, load(mine_ref), [load(ref) for ref in arrived], PACKED_SPEED)
    for level in range(levels - 1, -1, -1):
        outer = step_down(bit_low("gy", level), load(sides[level]), outer, PACKED_SPEED)
    outer = tuple(
        [spread(group, v[0], 0), spread(group, v[0], 1), spread(group, v[0], 3),
         spread(group, v[1], 1), spread(group, v[0], 2)]
        for v in outer
    )
    copies = []
    for s in range(GROUPS):
        half = step_down(s < GROUPS // 2, load(half_ref.at[s * 2 // GROUPS]), outer, SPEED_OF)
        outer_l, outer_r = step_down(s % 2 == 0, load(quarter_ref.at[s]), half, SPEED_OF)
        for c in range(s * chunks // GROUPS, (s + 1) * chunks // GROUPS):
            wave = [
                terms_ref[c, f] + terms_ref[c, 5 + SPEED_OF[f]] * outer_l[f]
                + terms_ref[c, 8 + SPEED_OF[f]] * outer_r[f]
                for f in range(5)
            ]
            density = flow_ref[0, :, c * LANES : (c + 1) * LANES]
            vel_u, vel_v, vel_w, kinetic, half_admittance, inverse_squared = load(points_ref.at[c])
            dp = 0.5 * (wave[0] + wave[4])
            dv = (wave[4] - wave[0]) * half_admittance
            dr = (wave[1] + dp) * inverse_squared
            du, dw = wave[2], wave[3]
            energy = (
                kinetic * dr + density * (vel_u * du + vel_v * dv + vel_w * dw)
                + dp * (1.0 / (GAMMA - 1.0))
            )
            result = [dr, vel_u * dr + density * du, vel_v * dr + density * dv, vel_w * dr + density * dw, energy]
            for f in range(5):
                out_ref[f, :, c * LANES : (c + 1) * LANES] = result[f]
        width = chunks // GROUPS * LANES
        part = (slice(None), slice(None), slice(s * width, (s + 1) * width))
        copies.append(pltpu.make_async_copy(out_ref.at[part], out_hbm.at[part], sems.at[s]))
        copies[-1].start()
    for copy in copies:
        copy.wait()


def call(kernel, args, outs, scratch=(), out_hbm=False):
    vmem, hbm = (pl.BlockSpec(memory_space=space) for space in (pltpu.VMEM, pltpu.HBM))
    return pl.pallas_call(
        kernel,
        out_shape=[jax.ShapeDtypeStruct(shape, jnp.float32) for shape in outs],
        in_specs=[vmem] * len(args),
        out_specs=[hbm if out_hbm else vmem] * len(outs),
        scratch_shapes=list(scratch),
        compiler_params=pltpu.CompilerParams(vmem_limit_bytes=16 * 1024 * 1024),
    )(*args)


def pairs_at(count, level):
    return [(i, i ^ (1 << level)) for i in range(count)]


def pairs_across(count, level):
    return [(i, i ^ (1 << level) ^ (1 if level else 0)) for i in range(count)]


def snake(count_x, count_y):
    pairs = []
    for x in range(count_x):
        for y in range(count_y):
            to = y + 1 if x % 2 == 0 else y - 1
            inside = 0 <= to < count_y
            pairs.append((x * count_y + y, x * count_y + to if inside else (x ^ 1) * count_y + y))
    return pairs


def ring_of_four(count, step):
    width = count // 4
    return [(i, (i + step * width) % count) for i in range(count)]


def levels_of(count):
    levels = count.bit_length() - 1
    assert count == 1 << levels and levels >= 2
    return levels


def local(flow, x_codes, y_codes):
    cells = flow.shape[1]
    columns = flow.shape[2]
    chunks = columns // LANES
    count_x, count_y = lax.axis_size("gx"), lax.axis_size("gy")
    levels_x, levels_y = levels_of(count_x), levels_of(count_y)
    tile_x, tile_y = (chunks, LANES), (cells, LANES)

    qx, one, two = call(pack_kernel, [flow], [(5, cells * chunks, LANES), (2,) + tile_y, (2,) + tile_y])
    round_trip = snake(count_x, count_y)
    one = lax.ppermute(one, ("gx", "gy"), round_trip)
    two = lax.ppermute(two, ("gx", "gy"), [(b, a) for a, b in round_trip])

    factors, inverse, lower, upper, left, right, xpoints = call(
        x_factor_kernel, [qx, x_codes],
        [(COEFS + 10,) + tile_x] + [(cells, 3) + tile_x] * 5 + [(cells, 2) + tile_x],
    )
    (source,) = call(x_source_kernel, [qx], [(cells, 5) + tile_x])
    all_factors = []
    for level in range(levels_x):
        other = lax.ppermute(factors, "gx", pairs_across(count_x, level))
        all_factors.append((factors, other))
        if level < levels_x - 1:
            final = level == levels_x - 2
            (factors,) = call(
                functools.partial(x_merge_factor_kernel, level, final),
                [factors, other], [(8 if final else COEFS + 10,) + tile_x],
            )
    rows, own = call(
        x_kernel, [flow, one, two, source, inverse, lower, upper],
        [(10,) + tile_x, (cells, 5) + tile_x],
        [pltpu.VMEM((5,) + tile_y, jnp.float32), pltpu.VMEM((5,) + tile_y, jnp.float32)],
    )
    sides = []
    for level in range(levels_x - 1):
        other = lax.ppermute(rows, "gx", pairs_across(count_x, level))
        final = level == levels_x - 2
        rows, side_rows = call(
            functools.partial(x_merge_kernel, level, final),
            [rows, other, *all_factors[level]], [(5 if final else 10,) + tile_x, (11,) + tile_x],
        )
        sides.append(side_rows)
    other = lax.ppermute(rows, "gx", pairs_across(count_x, levels_x - 1))
    y_factors, yinverse, ylower, yup, yleft, yright, yjoin, yside = call(
        y_factor_kernel, [flow, one, two, y_codes],
        [(4,) + tile_y] + [(chunks, 3) + tile_y] * 5 + [(2, 15) + tile_y, (2, 6) + tile_y],
    )
    packed, yown, yends = call(
        functools.partial(y_kernel, levels_x),
        [xpoints, own, left, right, rows, other, *all_factors[-1], y_factors, yinverse, ylower, yup, yjoin] + sides,
        [(8,) + tile_y, (chunks, 5) + tile_y, (2, 5) + tile_y],
        [pltpu.VMEM((5, cells * chunks, LANES), jnp.float32)],
    )
    prepared = call(
        prepare_kernel, [flow, yown, yleft, yright, yends, yside],
        [(chunks, 11) + tile_y, (chunks, 6) + tile_y, (2, 11) + tile_y, (GROUPS, 11) + tile_y],
    )
    sides = []
    for level in range(levels_y - 2):
        other = lax.ppermute(packed, "gy", pairs_at(count_y, level))
        packed, side_rows = call(
            functools.partial(y_merge_kernel, level),
            [packed, other], [(8,) + tile_y, (4,) + tile_y],
        )
        sides.append(side_rows)
    arrived = []
    for step in range(1, 4):
        arrived.append(lax.ppermute(packed, "gy", ring_of_four(count_y, step)))
    (result,) = call(
        functools.partial(final_kernel, levels_y - 2),
        [flow, *prepared, packed, *arrived] + sides,
        [(5, cells, columns)],
        [pltpu.VMEM((5, cells, columns), jnp.float32), pltpu.SemaphoreType.DMA((GROUPS,))],
        out_hbm=True,
    )
    return result


def solution(mesh):
    in_specs = (P(None, "gx", "gy"), P(None, "gy"), P(None, "gx"))
    out_specs = P(None, "gx", "gy")
    return jax.shard_map(local, mesh=mesh, in_specs=in_specs, out_specs=out_specs, check_vma=False)
```

```python
import functools

import jax
import jax.numpy as jnp
from jax import lax
from jax.experimental import pallas as pl
from jax.experimental.pallas import tpu as pltpu
from jax.sharding import PartitionSpec as P


NZ = 32
GAMMA = 1.4
SIGMA = 0.5
DIFFUSE = 400.0
LANES = 128
GROUPS = LANES // NZ
SPEED_OF = (0, 1, 1, 1, 2)
COEFS = 12


def primitives(q):
    inverse = 1.0 / q[0]
    vel_u, vel_v, vel_w = q[1] * inverse, q[2] * inverse, q[3] * inverse
    kinetic = 0.5 * (vel_u * vel_u + vel_v * vel_v + vel_w * vel_w)
    pressure = (GAMMA - 1.0) * (q[4] - q[0] * kinetic)
    sound = jnp.sqrt(GAMMA * pressure * inverse)
    return inverse, vel_u, vel_v, vel_w, kinetic, pressure, sound


def flux_of(q, normal, speed, pressure):
    return [q[normal]] + [
        q[f] * speed + pressure if f == normal else q[f] * speed for f in (1, 2, 3)
    ] + [speed * (q[4] + pressure)]


def three_speeds(velocity, sound):
    return (velocity - sound, velocity, velocity + sound)


def x_characteristics(res, density, prim):
    inverse, vel_u, vel_v, vel_w, kinetic, _, sound = prim
    du = (res[1] - vel_u * res[0]) * inverse
    dv = (res[2] - vel_v * res[0]) * inverse
    dw = (res[3] - vel_w * res[0]) * inverse
    dp = (GAMMA - 1.0) * (
        res[4] - vel_u * res[1] - vel_v * res[2] - vel_w * res[3] + kinetic * res[0]
    )
    normal = density * sound * du
    return [dp - normal, sound * sound * res[0] - dp, dv, dw, dp + normal]


def factor(speeds, first, last, forced=False):
    cells = len(speeds) - 2
    inverses, lowers, ups, lefts = [], [], [], []
    for i in range(cells):
        parts = []
        for k in range(3):
            lower = -0.5 * SIGMA * speeds[i][k] - DIFFUSE
            upper = 0.5 * SIGMA * speeds[i + 2][k] - DIFFUSE
            main = 1.0 + 2.0 * DIFFUSE
            if i == 0:
                main = main + lower * first[1]
                lower = None if forced else lower * first[0]
            if i == cells - 1:
                main = main + upper * last[1]
                upper = None if forced else upper * last[0]
            pivot = main if i == 0 else main - lower * ups[-1][k]
            inverse = 1.0 / pivot
            scaled = -inverse if lower is None else lower * inverse
            left = -scaled if i == 0 else -scaled * lefts[-1][k]
            parts.append((inverse, scaled, -inverse if upper is None else upper * inverse, left))
        for out, values in zip((inverses, lowers, ups, lefts), zip(*parts)):
            out.append(list(values))
    rights = [None] * cells
    rights[-1] = [-u for u in ups[-1]]
    for i in range(cells - 2, -1, -1):
        lefts[i] = [lefts[i][k] - ups[i][k] * lefts[i + 1][k] for k in range(3)]
        rights[i] = [-ups[i][k] * rights[i + 1][k] for k in range(3)]
    return inverses, lowers, ups, lefts, rights


def substitute(inverses, lowers, ups, sources):
    cells = len(sources)
    owns = []
    for i in range(cells):
        own = [sources[i][f] * inverses[i][SPEED_OF[f]] for f in range(5)]
        if i:
            own = [own[f] - lowers[i][SPEED_OF[f]] * owns[-1][f] for f in range(5)]
        owns.append(own)
    for i in range(cells - 2, -1, -1):
        owns[i] = [owns[i][f] - ups[i][SPEED_OF[f]] * owns[i + 1][f] for f in range(5)]
    return owns


def unpack(rows, fields=5, speeds=3):
    out, at = [], 0
    for n in (fields, fields, speeds, speeds, speeds, speeds):
        out.append(rows[at : at + n])
        at += n
    return out


def join(before, after, speed_of):
    fields = len(speed_of)
    a_f, a_e, b_f, c_f, b_e, c_e = before
    speeds = len(b_f)
    a_g, a_h, b_g, c_g, b_h, c_h = after
    inv = [1.0 / (1.0 - c_e[k] * b_g[k]) for k in range(speeds)]
    e_1 = [b_e[k] * inv[k] for k in range(speeds)]
    f_2 = [c_g[k] * inv[k] for k in range(speeds)]
    e_2 = [c_e[k] * f_2[k] for k in range(speeds)]
    f_1 = [b_g[k] * e_1[k] for k in range(speeds)]
    e_0 = [(a_e[f] + c_e[speed_of[f]] * a_g[f]) * inv[speed_of[f]] for f in range(fields)]
    f_0 = [(a_g[f] + b_g[speed_of[f]] * a_e[f]) * inv[speed_of[f]] for f in range(fields)]
    joined = (
        [a_f[f] + c_f[speed_of[f]] * f_0[f] for f in range(fields)]
        + [a_h[f] + b_h[speed_of[f]] * e_0[f] for f in range(fields)]
        + [b_f[k] + c_f[k] * f_1[k] for k in range(speeds)]
        + [c_f[k] * f_2[k] for k in range(speeds)]
        + [b_h[k] * e_1[k] for k in range(speeds)]
        + [c_h[k] + b_h[k] * e_2[k] for k in range(speeds)]
    )
    return joined, e_0 + e_1 + e_2, f_0 + f_1 + f_2


def merge(low, own, other, speed_of):
    fields = len(speed_of)
    speeds = max(speed_of) + 1
    before = [jnp.where(low, a, b) for a, b in zip(own, other)]
    after = [jnp.where(low, b, a) for a, b in zip(own, other)]
    joined, e, f = join(unpack(before, fields, speeds), unpack(after, fields, speeds), speed_of)
    return joined, [jnp.where(low, b, a) for a, b in zip(e, f)]


def join_factors(q_before, q_after):
    prim_b, prim_a = primitives(q_before), primitives(q_after)
    flux_b = flux_of(q_before, 1, prim_b[1], prim_b[5])
    flux_a = flux_of(q_after, 1, prim_a[1], prim_a[5])
    change = [-0.5 * SIGMA * (a - b) for a, b in zip(flux_a, flux_b)]
    smooth = [DIFFUSE * (a - b) for a, b in zip(q_after, q_before)]
    h_b = x_characteristics([c + d for c, d in zip(change, smooth)], q_before[0], prim_b)
    h_a = x_characteristics([c - d for c, d in zip(change, smooth)], q_after[0], prim_a)
    u_b = [DIFFUSE - 0.5 * SIGMA * v for v in three_speeds(prim_a[1], prim_a[6])]
    l_a = [DIFFUSE + 0.5 * SIGMA * v for v in three_speeds(prim_b[1], prim_b[6])]
    return h_b, u_b, h_a, l_a


def merge_forced(low, own, other):
    before = [jnp.where(low, a, b) for a, b in zip(own, other)]
    after = [jnp.where(low, b, a) for a, b in zip(own, other)]
    q_before, q_after = before[-5:], after[-10:-5]
    h_b, u_b, h_a, l_a = join_factors(q_before, q_after)
    a_f, a_e, b_f, c_f, b_e, c_e = unpack(before)
    a_g, a_h, b_g, c_g, b_h, c_h = unpack(after)
    a_f, a_e = ([a[f] + c[SPEED_OF[f]] * h_b[f] for f in range(5)] for a, c in ((a_f, c_f), (a_e, c_e)))
    a_g, a_h = ([a[f] + b[SPEED_OF[f]] * h_a[f] for f in range(5)] for a, b in ((a_g, b_g), (a_h, b_h)))
    c_f, c_e = ([c[k] * u_b[k] for k in range(3)] for c in (c_f, c_e))
    b_g, b_h = ([b[k] * l_a[k] for k in range(3)] for b in (b_g, b_h))
    joined, e, f = join(
        (a_f, a_e, b_f, c_f, b_e, c_e), (a_g, a_h, b_g, c_g, b_h, c_h), SPEED_OF
    )
    to_low = [h_b[n] + u_b[SPEED_OF[n]] * f[n] for n in range(5)]
    to_low += [u_b[k] * f[5 + 3 * t + k] for t in range(2) for k in range(3)]
    to_high = [h_a[n] + l_a[SPEED_OF[n]] * e[n] for n in range(5)]
    to_high += [l_a[k] * e[5 + 3 * t + k] for t in range(2) for k in range(3)]
    return joined, [jnp.where(low, a, b) for a, b in zip(to_low, to_high)]


def merge_factors(low, own, other):
    before = [jnp.where(low, a, b) for a, b in zip(own, other)]
    after = [jnp.where(low, b, a) for a, b in zip(own, other)]
    prim_b, prim_a = (primitives(q) for q in (before[-5:], after[-10:-5]))
    u_b = [DIFFUSE - 0.5 * SIGMA * v for v in three_speeds(prim_a[1], prim_a[6])]
    l_a = [DIFFUSE + 0.5 * SIGMA * v for v in three_speeds(prim_b[1], prim_b[6])]
    b_f, c_f, b_e, c_e = (before[3 * n : 3 * n + 3] for n in range(4))
    b_g, c_g, b_h, c_h = (after[3 * n : 3 * n + 3] for n in range(4))
    c_f, c_e = ([c[k] * u_b[k] for k in range(3)] for c in (c_f, c_e))
    b_g, b_h = ([b[k] * l_a[k] for k in range(3)] for b in (b_g, b_h))
    joined, _, _ = join(([], [], b_f, c_f, b_e, c_e), ([], [], b_g, c_g, b_h, c_h), ())
    return joined, before[-10:-5], after[-5:]


def last_factors_kernel(level, own_ref, other_ref, out_ref):
    low = bit_low("gx", level)
    own, other = load(own_ref), load(other_ref)
    before = [jnp.where(low, a, b) for a, b in zip(own, other)]
    after = [jnp.where(low, b, a) for a, b in zip(own, other)]
    h_b, u_b, h_a, l_a = join_factors(before[3:], after[3:])
    h_own = [jnp.where(low, a, b) for a, b in zip(h_b, h_a)]
    h_other = [jnp.where(low, b, a) for a, b in zip(h_b, h_a)]
    k_own = [jnp.where(low, a, b) for a, b in zip(u_b, l_a)]
    k_other = [jnp.where(low, b, a) for a, b in zip(u_b, l_a)]
    mine = [own[k] * k_own[k] for k in range(3)]
    theirs = [other[k] * k_other[k] for k in range(3)]
    of_other = [k_own[k] / (1.0 - mine[k] * theirs[k]) for k in range(3)]
    of_own = [of_other[k] * theirs[k] for k in range(3)]
    constant = []
    for f in range(5):
        k = SPEED_OF[f]
        constant.append(h_own[f] + of_other[k] * (other[k] * h_other[f]) + of_own[k] * (own[k] * h_own[f]))
    store(out_ref, constant + of_other + of_own)


def step_down(low, side, outer, speed_of):
    fields = len(speed_of)
    speeds = max(speed_of) + 1
    left, right = outer
    new = [
        side[f] + side[fields + speed_of[f]] * left[f] + side[fields + speeds + speed_of[f]] * right[f]
        for f in range(fields)
    ]
    if isinstance(low, bool):
        return (left, new) if low else (new, right)
    return (
        [jnp.where(low, a, b) for a, b in zip(left, new)],
        [jnp.where(low, b, a) for a, b in zip(right, new)],
    )


def from_last(low, new):
    zero = jnp.zeros_like(new[0])
    return [jnp.where(low, zero, x) for x in new], [jnp.where(low, x, zero) for x in new]


def bit_low(axis, level):
    return (lax.axis_index(axis) >> level) % 2 == 0


def x_edges(codes_ref, shape):
    at, count = lax.axis_index("gx"), lax.axis_size("gx")
    lane = lax.broadcasted_iota(jnp.int32, shape, 1)
    sub = lax.broadcasted_iota(jnp.int32, shape, 0)
    width = codes_ref.shape[1]
    result = []
    place = lax.broadcasted_iota(jnp.int32, (shape[0], width), 1)
    row = lax.broadcasted_iota(jnp.int32, (shape[0], width), 0)
    for side, outer in ((0, at == 0), (1, at == count - 1)):
        codes = jnp.broadcast_to(codes_ref[side : side + 1, :], (shape[0], width))
        is_one = jnp.where(codes == 1, 1.0, 0.0)
        value = jnp.zeros(shape, jnp.float32)
        for g in range(GROUPS):
            mine = jnp.where(place == row * GROUPS + g, is_one, 0.0)
            column = jnp.sum(mine, axis=1, keepdims=True)
            value = jnp.where(lane // NZ == g, column, value)
        result.append(jnp.where(outer, value, 0.0))
    return result


def y_edges(codes_ref, shape):
    at, count = lax.axis_index("gy"), lax.axis_size("gy")
    group = lax.broadcasted_iota(jnp.int32, shape, 1) // NZ
    cells = shape[0]
    result = []
    place = lax.broadcasted_iota(jnp.int32, (cells, cells), 1)
    row = lax.broadcasted_iota(jnp.int32, (cells, cells), 0)
    for side, outer, face in ((0, at == 0, 0), (1, at == count - 1, GROUPS - 1)):
        codes = jnp.broadcast_to(codes_ref[side : side + 1, :], (cells, cells))
        mine = jnp.where(jnp.logical_and(codes == 1, place == row), 1.0, 0.0)
        value = jnp.broadcast_to(jnp.sum(mine, axis=1, keepdims=True), shape)
        at_face = jnp.logical_and(outer, group == face)
        result.append((jnp.where(at_face, 0.0, 1.0), jnp.where(at_face, value, 0.0)))
    return result


def to_group(value, source, target):
    shift = (target - source) * NZ % LANES
    return pltpu.roll(value, shift, 1) if shift else value


def pack_kernel(flow_ref, qx_ref, one_ref, two_ref):
    cells = flow_ref.shape[1]
    chunks = flow_ref.shape[2] // LANES
    even = bit_low("gx", 0)
    group = lax.broadcasted_iota(jnp.int32, (cells, LANES), 1) // NZ
    downs, ups = [], []
    for f in range(5):
        down = to_group(flow_ref[f, :, 0:LANES], 0, f % GROUPS)
        up = to_group(flow_ref[f, :, (chunks - 1) * LANES : chunks * LANES], GROUPS - 1, f % GROUPS)
        for rows, value in ((downs, down), (ups, up)):
            if f % GROUPS:
                rows[-1] = jnp.where(group == f % GROUPS, value, rows[-1])
            else:
                rows.append(value)
    for n, (down, up) in enumerate(zip(downs, ups)):
        one_ref[n] = jnp.where(even, up, down)
        two_ref[n] = jnp.where(even, down, up)
    for f in range(5):
        for c in range(chunks):
            qx_ref[f, pl.ds(c, cells, stride=chunks), :] = flow_ref[f, :, c * LANES : (c + 1) * LANES]


def y_halos(flow_ref, one_ref, two_ref, f):
    chunks = flow_ref.shape[2] // LANES
    at, count = lax.axis_index("gy"), lax.axis_size("gy")
    even = bit_low("gx", 0)
    low = jnp.where(even, one_ref[f // GROUPS], two_ref[f // GROUPS])
    high = jnp.where(even, two_ref[f // GROUPS], one_ref[f // GROUPS])
    low, high = to_group(low, f % GROUPS, GROUPS - 1), to_group(high, f % GROUPS, 0)
    own_low = to_group(flow_ref[f, :, 0:LANES], 0, GROUPS - 1)
    own_high = to_group(flow_ref[f, :, (chunks - 1) * LANES : chunks * LANES], GROUPS - 1, 0)
    return jnp.where(at == 0, own_low, low), jnp.where(at == count - 1, own_high, high)


def x_factor_kernel(
    qx_ref, codes_ref, out_ref, inverse_ref, lower_ref, up_ref, left_ref, right_ref, points_ref, weight_ref
):
    cells = inverse_ref.shape[0]
    chunks = inverse_ref.shape[2]
    rows = [[qx_ref[f, i * chunks : (i + 1) * chunks, :] for f in range(5)] for i in range(cells)]
    speeds, points = [], []
    for q in rows:
        prim = primitives(q)
        speeds.append(three_speeds(prim[1], prim[6]))
        impedance = q[0] * prim[6]
        points.append([impedance, 0.5 / impedance])
    for i in range(cells):
        store(points_ref.at[i], points[i])
    neumann = x_edges(codes_ref, (chunks, LANES))
    parts = factor(
        speeds[:1] + speeds + speeds[-1:], (None, neumann[0]), (None, neumann[1]), forced=True
    )
    for ref, values in zip((inverse_ref, lower_ref, up_ref, left_ref, right_ref), parts):
        for i in range(cells):
            store(ref.at[i], values[i])
    weights = [part_weights(*parts[:3], k) for k in range(3)]
    for i in range(cells):
        store(weight_ref.at[i], [weights[k][side][i] for side in range(2) for k in range(3)])
    lefts, rights = parts[3:]
    store(out_ref, lefts[0] + rights[0] + lefts[-1] + rights[-1] + rows[0] + rows[-1])


def x_source_kernel(qx_ref, weight_ref, out_ref, ends_ref):
    cells = out_ref.shape[0]
    chunks = out_ref.shape[2]
    lane = lax.broadcasted_iota(jnp.int32, (chunks, LANES), 1)
    sub = lax.broadcasted_iota(jnp.int32, (chunks, LANES), 0)
    z_of = lane % NZ
    rows = [[qx_ref[f, i * chunks : (i + 1) * chunks, :] for f in range(5)] for i in range(cells)]
    prims = [primitives(q) for q in rows]
    fluxes = [flux_of(q, 1, p[1], p[5]) for q, p in zip(rows, prims)]
    rows, fluxes = (v[:1] + v + v[-1:] for v in (rows, fluxes))
    up_edge = jnp.logical_and(sub == chunks - 1, lane >= LANES - NZ)
    down_edge = jnp.logical_and(sub == 0, lane < NZ)

    def y_next(value):
        turned = pltpu.roll(value, LANES - NZ, 1)
        turned = jnp.where(lane >= LANES - NZ, pltpu.roll(turned, chunks - 1, 0), turned)
        return jnp.where(up_edge, value, turned)

    def y_before(value):
        turned = pltpu.roll(value, NZ, 1)
        turned = jnp.where(lane < NZ, pltpu.roll(turned, 1, 0), turned)
        return jnp.where(down_edge, value, turned)

    def z_change(value):
        after = jnp.where(z_of == NZ - 1, pltpu.roll(value, NZ - 1, 1), pltpu.roll(value, LANES - 1, 1))
        before = jnp.where(z_of == 0, pltpu.roll(value, LANES - NZ + 1, 1), pltpu.roll(value, 1, 1))
        return after - before

    ends = None
    for i in range(cells):
        q = rows[i + 1]
        _, _, vel_v, vel_w, _, pressure, _ = prims[i]
        after = [y_next(v) for v in list(q) + [vel_v, pressure]]
        before = [y_before(v) for v in list(q) + [vel_v, pressure]]
        flux_after = flux_of(after, 2, after[5], after[6])
        flux_before = flux_of(before, 2, before[5], before[6])
        flux_z = flux_of(q, 3, vel_w, pressure)
        res = []
        for f in range(5):
            change = (
                (fluxes[i + 2][f] - fluxes[i][f])
                + (flux_after[f] - flux_before[f])
                + z_change(flux_z[f])
            )
            smooth = rows[i + 2][f] + rows[i][f] + after[f] + before[f] - 4.0 * q[f]
            res.append(-0.5 * SIGMA * change + DIFFUSE * smooth)
        source = x_characteristics(res, q[0], prims[i])
        store(out_ref.at[i], source)
        parts = [weight_ref[i, 3 * side + SPEED_OF[f]] * source[f] for side in range(2) for f in range(5)]
        ends = parts if ends is None else [a + b for a, b in zip(ends, parts)]
    store(ends_ref, ends)


def y_edge_mask(chunks):
    lane = lax.broadcasted_iota(jnp.int32, (chunks, LANES), 1)
    sub = lax.broadcasted_iota(jnp.int32, (chunks, LANES), 0)
    high = jnp.logical_and(sub == chunks - 1, lane >= LANES - NZ)
    return jnp.logical_or(high, jnp.logical_and(sub == 0, lane < NZ))


def x_kernel(flow_ref, one_ref, two_ref, weight_ref, ends_ref, rows_ref, extra_ref):
    cells = flow_ref.shape[1]
    chunks = flow_ref.shape[2] // LANES
    lows, highs = zip(*[y_halos(flow_ref, one_ref, two_ref, f) for f in range(5)])
    extras = []
    for ghosts, at, turn, sign in ((lows, 0, NZ, 1.0), (highs, chunks - 1, LANES - NZ, -1.0)):
        ghosts = [pltpu.roll(g, turn, 1) for g in ghosts]
        inner = [flow_ref[f, :, at * LANES : (at + 1) * LANES] for f in range(5)]
        ghost_prim, prim = primitives(ghosts), primitives(inner)
        ghost_flux = flux_of(ghosts, 2, ghost_prim[2], ghost_prim[5])
        inner_flux = flux_of(inner, 2, prim[2], prim[5])
        res = [
            sign * 0.5 * SIGMA * (ghost_flux[f] - inner_flux[f]) + DIFFUSE * (ghosts[f] - inner[f])
            for f in range(5)
        ]
        extras.append(x_characteristics(res, inner[0], prim))
    lane = lax.broadcasted_iota(jnp.int32, (cells, LANES), 1)
    store(extra_ref, [jnp.where(lane < LANES // 2, low, high) for low, high in zip(*extras)])
    edge = y_edge_mask(chunks)
    added = None
    for i in range(cells):
        extra = [jnp.broadcast_to(extra_ref[f, i : i + 1, :], (chunks, LANES)) for f in range(5)]
        parts = [weight_ref[i, 3 * side + SPEED_OF[f]] * extra[f] for side in range(2) for f in range(5)]
        added = parts if added is None else [a + b for a, b in zip(added, parts)]
    store(rows_ref, [ends_ref[n] + jnp.where(edge, value, 0.0) for n, value in enumerate(added)])


def x_own_kernel(source_ref, extra_ref, inverse_ref, lower_ref, up_ref, own_ref):
    cells, chunks = source_ref.shape[0], source_ref.shape[2]
    edge = y_edge_mask(chunks)
    sources = []
    for i in range(cells):
        extra = [jnp.broadcast_to(extra_ref[f, i : i + 1, :], (chunks, LANES)) for f in range(5)]
        sources.append([source_ref[i, f] + jnp.where(edge, extra[f], 0.0) for f in range(5)])
    owns = substitute(*([load(ref.at[i]) for i in range(cells)] for ref in (inverse_ref, lower_ref, up_ref)), sources)
    for i in range(cells):
        store(own_ref.at[i], owns[i])


def load(ref):
    return [ref[n] for n in range(ref.shape[0])]


def store(ref, values):
    for n, value in enumerate(values):
        ref[n] = value


def x_merge_factor_kernel(level, final, own_ref, other_ref, out_ref):
    joined, q_first, q_last = merge_factors(bit_low("gx", level), load(own_ref), load(other_ref))
    if final:
        low = bit_low("gx", level + 1)
        b_f, _, _, c_e = (joined[3 * n : 3 * n + 3] for n in range(4))
        pairs = list(zip(c_e, b_f)) + list(zip(q_last, q_first))
        store(out_ref, [jnp.where(low, e, f) for e, f in pairs])
    else:
        store(out_ref, joined + q_first + q_last)


def x_merge_kernel(level, final, own_ref, other_ref, own_factor_ref, other_factor_ref, out_ref, side_ref):
    joined, side = merge_forced(
        bit_low("gx", level), load(own_ref) + load(own_factor_ref), load(other_ref) + load(other_factor_ref)
    )
    a_f, a_e = joined[:5], joined[5:10]
    if final:
        low = bit_low("gx", level + 1)
        store(out_ref, [jnp.where(low, e, f) for e, f in zip(a_e, a_f)])
    else:
        store(out_ref, a_f + a_e)
    store(side_ref, side)


def y_merge_kernel(level, own_ref, other_ref, out_ref, side_ref):
    joined, side = merge(bit_low("gy", level), load(own_ref), load(other_ref), PACKED_SPEED)
    store(out_ref, joined)
    store(side_ref, side)


def outer_values(levels, own, other, factors, side_refs):
    low = bit_low("gx", levels - 1)
    new = [
        factors[f] + factors[5 + SPEED_OF[f]] * other[f] + factors[8 + SPEED_OF[f]] * own[f] for f in range(5)
    ]
    outer = from_last(low, new)
    for level in range(levels - 2, -1, -1):
        outer = step_down(bit_low("gx", level), load(side_refs[level]), outer, SPEED_OF)
    return outer


def pick(place, values):
    return [
        functools.reduce(lambda old, n: jnp.where(place == n, items[n], old), range(1, len(items)), items[0])
        for items in zip(*values)
    ]


def outer_of_four(place, own, arrived, speed_of):
    fields, speeds = len(speed_of), max(speed_of) + 1
    ring = [own] + arrived
    segments = [unpack(pick((place - n) % 4, ring), fields, speeds) for n in range(4)]
    left, e_left, f_left = join(segments[0], segments[1], speed_of)
    right, e_right, f_right = join(segments[2], segments[3], speed_of)
    a_e, c_e = (unpack(left, fields, speeds)[n] for n in (1, 5))
    a_f, b_f = (unpack(right, fields, speeds)[n] for n in (0, 2))
    e_mid, f_mid, zero = [], [], jnp.zeros_like(a_e[0])
    inverse = [1.0 / (1.0 - c_e[k] * b_f[k]) for k in range(speeds)]
    for n in range(fields):
        k = speed_of[n]
        e_mid.append((a_e[n] + c_e[k] * a_f[n]) * inverse[k])
        f_mid.append((a_f[n] + b_f[k] * a_e[n]) * inverse[k])

    def inner(terms, outer, side):
        return [terms[n] + terms[fields + side * speeds + speed_of[n]] * outer[n] for n in range(fields)]

    lefts = [[zero] * fields, inner(e_left, f_mid, 1), e_mid, inner(e_right, e_mid, 0)]
    rights = [inner(f_left, f_mid, 1), f_mid, inner(f_right, e_mid, 0), [zero] * fields]
    return pick(place, lefts), pick(place, rights)


PACKED_SPEED = (0, 0)


def regroup(parts, group):
    steps = len(parts)
    result = []
    for jj in range(steps):
        value = None
        for s in range(GROUPS):
            y = s * steps + jj
            piece = parts[y // GROUPS]
            shift = (s - y % GROUPS) * NZ % LANES
            piece = pltpu.roll(piece, shift, 1) if shift else piece
            value = piece if s == 0 else jnp.where(group == s, piece, value)
        result.append(value)
    return result


def lane_partner(values, group, level):
    if level == 0:
        return [
            jnp.where(group % 2 == 0, pltpu.roll(v, LANES - NZ, 1), pltpu.roll(v, NZ, 1)) for v in values
        ]
    return [pltpu.roll(v, LANES // 2, 1) for v in values]


def lane_low(group, level):
    return (group // 2 ** level) % 2 == 0


def y_factor_kernel(
    flow_ref, one_ref, two_ref, codes_ref,
    packed_ref, inverse_ref, lower_ref, up_ref, left_ref, right_ref, join_ref, side_ref, weight_ref,
):
    cells = flow_ref.shape[1]
    chunks = flow_ref.shape[2] // LANES
    lane = lax.broadcasted_iota(jnp.int32, (cells, LANES), 1)
    group = lane // NZ
    vels, sounds = [], []
    for c in range(chunks):
        prim = primitives([flow_ref[f, :, c * LANES : (c + 1) * LANES] for f in range(5)])
        vels.append(prim[2])
        sounds.append(prim[6])
    speeds = [three_speeds(v, c) for v, c in zip(regroup(vels, group), regroup(sounds, group))]
    lows, highs = zip(*[y_halos(flow_ref, one_ref, two_ref, f) for f in range(5)])
    low_prim, high_prim = primitives(lows), primitives(highs)
    low_speed = three_speeds(low_prim[2], low_prim[6])
    high_speed = three_speeds(high_prim[2], high_prim[6])
    before = tuple(
        pltpu.roll(jnp.where(group == GROUPS - 1, low_speed[k], speeds[-1][k]), NZ, 1) for k in range(3)
    )
    after = tuple(
        pltpu.roll(jnp.where(group == 0, high_speed[k], speeds[0][k]), LANES - NZ, 1) for k in range(3)
    )
    parts = factor([before] + speeds + [after], *y_edges(codes_ref, (cells, LANES)))
    for ref, values in zip((inverse_ref, lower_ref, up_ref, left_ref, right_ref), parts):
        for i in range(chunks):
            store(ref.at[i], values[i])
    lefts, rights = parts[3:]
    ends = lefts[0] + rights[0] + lefts[-1] + rights[-1]
    for level in range(2):
        low = lane_low(group, level)
        other = lane_partner(ends, group, level)
        before = [jnp.where(low, a, b) for a, b in zip(ends, other)]
        after = [jnp.where(low, b, a) for a, b in zip(ends, other)]
        b_f, c_f, b_e, c_e = (before[3 * n : 3 * n + 3] for n in range(4))
        b_g, c_g, b_h, c_h = (after[3 * n : 3 * n + 3] for n in range(4))
        inv = [1.0 / (1.0 - c_e[k] * b_g[k]) for k in range(3)]
        store(join_ref.at[level], inv + c_e + b_g + c_f + b_h)
        ends, e, f = join(([], [], b_f, c_f, b_e, c_e), ([], [], b_g, c_g, b_h, c_h), ())
        store(side_ref.at[level], [jnp.where(low, b, a) for a, b in zip(e, f)])
    store(packed_ref, [four(group, t[0], t[1], t[2], t[1]) for t in (ends[3 * n : 3 * n + 3] for n in range(4))])
    weights = end_weights(group, parts, [load(join_ref.at[level]) for level in range(2)])
    for c in range(chunks):
        store(weight_ref.at[c], [ungroup(column, c, group) for column in weights])


def part_weights(inverses, lowers, ups, k):
    steps = len(inverses)
    reach = [None] * steps
    passed = None
    for i in range(steps):
        reach[i] = passed
        passed = -ups[i][k] if passed is None else -passed * ups[i][k]
    first_w, last_w = [None] * steps, [None] * steps
    ahead_first, ahead_last = reach[-1], None
    for i in range(steps - 1, -1, -1):
        if i == steps - 1:
            last_w[i] = inverses[i][k]
        else:
            ahead_first = -lowers[i + 1][k] * ahead_first
            ahead_first = ahead_first + (1.0 if i == 0 else reach[i])
            ahead_last = -lowers[i + 1][k] if ahead_last is None else -lowers[i + 1][k] * ahead_last
            last_w[i] = ahead_last * inverses[i][k]
        first_w[i] = ahead_first * inverses[i][k]
    return first_w, last_w


def end_weights(group, parts, joins):
    columns = []
    for k in range(3):
        first_w, last_w = part_weights(*parts[:3], k)
        steps = len(first_w)
        shares = []
        for level in range(2):
            inv, c_e, b_g, c_f, b_h = (joins[level][3 * n + k] for n in range(5))
            low = lane_low(group, level)
            one, zero = jnp.ones_like(inv), jnp.zeros_like(inv)
            shares.append((
                jnp.where(low, one, c_f * inv),
                jnp.where(low, c_f * b_g * inv, zero),
                jnp.where(low, zero, b_h * c_e * inv),
                jnp.where(low, b_h * inv, one),
            ))
        (ff, lf, fl, ll), (top_ff, top_lf, top_fl, top_ll) = shares
        for top_first, top_last in ((top_ff, top_lf), (top_fl, top_ll)):
            share_first = top_first * ff + top_last * fl
            share_last = top_first * lf + top_last * ll
            columns.append([share_first * first_w[i] + share_last * last_w[i] for i in range(steps)])
    return columns[0::2] + columns[1::2]


def y_kernel(levels, *refs):
    (points_ref, own_ref, left_ref, right_ref, mine_ref, other_ref, last_ref, packed_ref, weight_ref) = refs[:9]
    sides = refs[9 : 9 + levels - 1]
    out_ref, turn_ref = refs[9 + levels - 1 :]
    chunks = own_ref.shape[2]
    cells = own_ref.shape[0]
    outer_l, outer_r = outer_values(levels, load(mine_ref), load(other_ref), load(last_ref), sides)
    for i in range(cells):
        impedance, half_admittance = load(points_ref.at[i])
        wave = [
            own_ref[i, f] + left_ref[i, SPEED_OF[f]] * outer_l[f] + right_ref[i, SPEED_OF[f]] * outer_r[f]
            for f in range(5)
        ]
        dp = 0.5 * (wave[0] + wave[4])
        du = (wave[4] - wave[0]) * half_admittance
        normal = impedance * wave[2]
        values = [dp - normal, wave[1], du, wave[3], dp + normal]
        for n, value in enumerate(values):
            turn_ref[n, i * chunks : (i + 1) * chunks, :] = value
    group = lax.broadcasted_iota(jnp.int32, (cells, LANES), 1) // NZ
    ends = []
    for side in range(2):
        for f in range(5):
            terms = [
                turn_ref[f, pl.ds(c, cells, stride=chunks), :] * weight_ref[c, 3 * side + SPEED_OF[f]]
                for c in range(chunks)
            ]
            while len(terms) > 1:
                terms = [a + b for a, b in zip(terms[0::2], terms[1::2])] + terms[len(terms) // 2 * 2 :]
            ends.append(terms[0])
    ends = [v + pltpu.roll(v, LANES // 2, 1) for v in ends]
    ends = [v + pltpu.roll(v, NZ, 1) for v in ends]
    rows = []
    for a in (ends[:5], ends[5:]):
        rows += [four(group, a[0], a[1], a[4], a[2]), a[3]]
    store(out_ref, rows + load(packed_ref))


def y_sweep(turn_ref, cells, group, factor_refs, join_ref):
    chunks = turn_ref.shape[1] // cells
    fields = [
        regroup([turn_ref[n, pl.ds(c, cells, stride=chunks), :] for c in range(chunks)], group)
        for n in range(5)
    ]
    sources = [[fields[f][jj] for f in range(5)] for jj in range(chunks)]
    owns = substitute(*([load(ref.at[i]) for i in range(chunks)] for ref in factor_refs), sources)
    a_f, a_e = owns[0], owns[-1]
    sides = []
    for level in range(2):
        low = lane_low(group, level)
        other = lane_partner(a_f + a_e, group, level)
        parts = load(join_ref.at[level])
        inv, c_e, b_g, c_f, b_h = (parts[3 * n : 3 * n + 3] for n in range(5))
        before = [jnp.where(low, a, b) for a, b in zip(a_f + a_e, other)]
        after = [jnp.where(low, b, a) for a, b in zip(a_f + a_e, other)]
        e, f, new_f, new_e = [], [], [], []
        for n in range(5):
            k = SPEED_OF[n]
            e.append((before[5 + n] + c_e[k] * after[n]) * inv[k])
            f.append((after[n] + b_g[k] * before[5 + n]) * inv[k])
            new_f.append(before[n] + c_f[k] * f[n])
            new_e.append(after[5 + n] + b_h[k] * e[n])
        a_f, a_e = new_f, new_e
        sides.append([jnp.where(low, b, a) for a, b in zip(e, f)])
    return owns, sides


def four(group, a, b, c, d):
    return jnp.where(group == 0, a, jnp.where(group == 1, b, jnp.where(group == 2, c, d)))


def spread(group, value, source):
    half = jnp.where(group // 2 == source // 2, value, pltpu.roll(value, LANES // 2, 1))
    down, up = pltpu.roll(half, NZ, 1), pltpu.roll(half, LANES - NZ, 1)
    if source % 2 == 0:
        return jnp.where(group % 2 == 0, half, down)
    return jnp.where(group % 2 == 1, half, up)


def ungroup(values, c, group):
    steps = len(values)
    result = None
    for g in range(GROUPS):
        y = c * GROUPS + g
        piece = to_group(values[y % steps], y // steps, g)
        result = piece if g == 0 else jnp.where(group == g, piece, result)
    return result


def prepare_kernel(
    flow_ref, turn_ref, inverse_ref, lower_ref, up_ref, join_ref, yleft_ref, yright_ref, side_ref,
    terms_ref, points_ref, half_ref, quarter_ref,
):
    cells = flow_ref.shape[1]
    chunks = flow_ref.shape[2] // LANES
    group = lax.broadcasted_iota(jnp.int32, (cells, LANES), 1) // NZ
    owns, ends = y_sweep(turn_ref, cells, group, (inverse_ref, lower_ref, up_ref), join_ref)
    columns = [[own[n] for own in owns] for n in range(5)] + [
        [ref[j, n] for j in range(chunks)] for ref in (yleft_ref, yright_ref) for n in range(3)
    ]
    for c in range(chunks):
        store(terms_ref.at[c], [ungroup(column, c, group) for column in columns])
        q = [flow_ref[f, :, c * LANES : (c + 1) * LANES] for f in range(5)]
        _, vel_u, vel_v, vel_w, kinetic, _, sound = primitives(q)
        store(
            points_ref.at[c],
            [vel_u, vel_v, vel_w, kinetic, 1.0 / (2.0 * q[0] * sound), 1.0 / (sound * sound)],
        )
    for level, ref, count in ((1, half_ref, 2), (0, quarter_ref, GROUPS)):
        rows = ends[level] + load(side_ref.at[level])
        for n in range(count):
            store(ref.at[n], [spread(group, row, n * GROUPS // count) for row in rows])


def final_kernel(levels, *refs):
    (flow_ref, terms_ref, points_ref, half_ref, quarter_ref, mine_ref) = refs[:6]
    arrived, sides = refs[6:9], refs[9 : 9 + levels]
    out_hbm, out_ref, sems = refs[9 + levels :]
    cells = flow_ref.shape[1]
    chunks = flow_ref.shape[2] // LANES
    group = lax.broadcasted_iota(jnp.int32, (cells, LANES), 1) // NZ
    place = (lax.axis_index("gy") >> levels) % 4
    outer = outer_of_four(place, load(mine_ref), [load(ref) for ref in arrived], PACKED_SPEED)
    for level in range(levels - 1, -1, -1):
        outer = step_down(bit_low("gy", level), load(sides[level]), outer, PACKED_SPEED)
    outer = tuple(
        [spread(group, v[0], 0), spread(group, v[0], 1), spread(group, v[0], 3),
         spread(group, v[1], 1), spread(group, v[0], 2)]
        for v in outer
    )
    copies = []
    for s in range(GROUPS):
        half = step_down(s < GROUPS // 2, load(half_ref.at[s * 2 // GROUPS]), outer, SPEED_OF)
        outer_l, outer_r = step_down(s % 2 == 0, load(quarter_ref.at[s]), half, SPEED_OF)
        for c in range(s * chunks // GROUPS, (s + 1) * chunks // GROUPS):
            wave = [
                terms_ref[c, f] + terms_ref[c, 5 + SPEED_OF[f]] * outer_l[f]
                + terms_ref[c, 8 + SPEED_OF[f]] * outer_r[f]
                for f in range(5)
            ]
            density = flow_ref[0, :, c * LANES : (c + 1) * LANES]
            vel_u, vel_v, vel_w, kinetic, half_admittance, inverse_squared = load(points_ref.at[c])
            dp = 0.5 * (wave[0] + wave[4])
            dv = (wave[4] - wave[0]) * half_admittance
            dr = (wave[1] + dp) * inverse_squared
            du, dw = wave[2], wave[3]
            energy = (
                kinetic * dr + density * (vel_u * du + vel_v * dv + vel_w * dw)
                + dp * (1.0 / (GAMMA - 1.0))
            )
            result = [dr, vel_u * dr + density * du, vel_v * dr + density * dv, vel_w * dr + density * dw, energy]
            for f in range(5):
                out_ref[f, :, c * LANES : (c + 1) * LANES] = result[f]
        width = chunks // GROUPS * LANES
        part = (slice(None), slice(None), slice(s * width, (s + 1) * width))
        copies.append(pltpu.make_async_copy(out_ref.at[part], out_hbm.at[part], sems.at[s]))
        copies[-1].start()
    for copy in copies:
        copy.wait()


def call(kernel, args, outs, scratch=(), out_hbm=False):
    vmem, hbm = (pl.BlockSpec(memory_space=space) for space in (pltpu.VMEM, pltpu.HBM))
    return pl.pallas_call(
        kernel,
        out_shape=[jax.ShapeDtypeStruct(shape, jnp.float32) for shape in outs],
        in_specs=[vmem] * len(args),
        out_specs=[hbm if out_hbm else vmem] * len(outs),
        scratch_shapes=list(scratch),
        compiler_params=pltpu.CompilerParams(vmem_limit_bytes=16 * 1024 * 1024),
    )(*args)


def pairs_at(count, level):
    return [(i, i ^ (1 << level)) for i in range(count)]


def pairs_across(count, level):
    return [(i, i ^ (1 << level) ^ (1 if level else 0)) for i in range(count)]


def snake(count_x, count_y):
    pairs = []
    for x in range(count_x):
        for y in range(count_y):
            to = y + 1 if x % 2 == 0 else y - 1
            inside = 0 <= to < count_y
            pairs.append((x * count_y + y, x * count_y + to if inside else (x ^ 1) * count_y + y))
    return pairs


def ring_of_four(count, step):
    width = count // 4
    return [(i, (i + step * width) % count) for i in range(count)]


def levels_of(count):
    levels = count.bit_length() - 1
    assert count == 1 << levels and levels >= 2
    return levels


def local(flow, x_codes, y_codes):
    cells = flow.shape[1]
    columns = flow.shape[2]
    chunks = columns // LANES
    count_x, count_y = lax.axis_size("gx"), lax.axis_size("gy")
    levels_x, levels_y = levels_of(count_x), levels_of(count_y)
    tile_x, tile_y = (chunks, LANES), (cells, LANES)

    qx, one, two = call(pack_kernel, [flow], [(5, cells * chunks, LANES), (2,) + tile_y, (2,) + tile_y])
    round_trip = snake(count_x, count_y)
    one = lax.ppermute(one, ("gx", "gy"), round_trip)
    two = lax.ppermute(two, ("gx", "gy"), [(b, a) for a, b in round_trip])

    factors, inverse, lower, upper, left, right, xpoints, xweight = call(
        x_factor_kernel, [qx, x_codes],
        [(COEFS + 10,) + tile_x] + [(cells, 3) + tile_x] * 5 + [(cells, 2) + tile_x, (cells, 6) + tile_x],
    )
    source, ends = call(x_source_kernel, [qx, xweight], [(cells, 5) + tile_x, (10,) + tile_x])
    all_factors = []
    for level in range(levels_x):
        other = lax.ppermute(factors, "gx", pairs_across(count_x, level))
        all_factors.append((factors, other))
        if level < levels_x - 1:
            final = level == levels_x - 2
            (factors,) = call(
                functools.partial(x_merge_factor_kernel, level, final),
                [factors, other], [(8 if final else COEFS + 10,) + tile_x],
            )
    rows, extra = call(x_kernel, [flow, one, two, xweight, ends], [(10,) + tile_x, (5,) + tile_y])
    (own,) = call(x_own_kernel, [source, extra, inverse, lower, upper], [(cells, 5) + tile_x])
    (last,) = call(
        functools.partial(last_factors_kernel, levels_x - 1), [*all_factors[-1]],
        [(11,) + tile_x],
    )
    sides = []
    for level in range(levels_x - 1):
        other = lax.ppermute(rows, "gx", pairs_across(count_x, level))
        final = level == levels_x - 2
        rows, side_rows = call(
            functools.partial(x_merge_kernel, level, final),
            [rows, other, *all_factors[level]], [(5 if final else 10,) + tile_x, (11,) + tile_x],
        )
        sides.append(side_rows)
    other = lax.ppermute(rows, "gx", pairs_across(count_x, levels_x - 1))
    y_factors, yinverse, ylower, yup, yleft, yright, yjoin, yside, yweight = call(
        y_factor_kernel, [flow, one, two, y_codes],
        [(4,) + tile_y] + [(chunks, 3) + tile_y] * 5 + [(2, 15) + tile_y, (2, 6) + tile_y, (chunks, 6) + tile_y],
    )
    packed, turn = call(
        functools.partial(y_kernel, levels_x),
        [xpoints, own, left, right, rows, other, last, y_factors, yweight] + sides,
        [(8,) + tile_y, (5, cells * chunks, LANES)],
    )
    prepared = call(
        prepare_kernel, [flow, turn, yinverse, ylower, yup, yjoin, yleft, yright, yside],
        [(chunks, 11) + tile_y, (chunks, 6) + tile_y, (2, 11) + tile_y, (GROUPS, 11) + tile_y],
    )
    sides = []
    for level in range(levels_y - 2):
        other = lax.ppermute(packed, "gy", pairs_at(count_y, level))
        packed, side_rows = call(
            functools.partial(y_merge_kernel, level),
            [packed, other], [(8,) + tile_y, (4,) + tile_y],
        )
        sides.append(side_rows)
    arrived = []
    for step in range(1, 4):
        arrived.append(lax.ppermute(packed, "gy", ring_of_four(count_y, step)))
    (result,) = call(
        functools.partial(final_kernel, levels_y - 2),
        [flow, *prepared, packed, *arrived] + sides,
        [(5, cells, columns)],
        [pltpu.VMEM((5, cells, columns), jnp.float32), pltpu.SemaphoreType.DMA((GROUPS,))],
        out_hbm=True,
    )
    return result


def solution(mesh):
    in_specs = (P(None, "gx", "gy"), P(None, "gy"), P(None, "gx"))
    out_specs = P(None, "gx", "gy")
    return jax.shard_map(local, mesh=mesh, in_specs=in_specs, out_specs=out_specs, check_vma=False)
```

```python
import functools

import jax
import jax.numpy as jnp
from jax import lax
from jax.experimental import pallas as pl
from jax.experimental.pallas import tpu as pltpu
from jax.sharding import PartitionSpec as P


NZ = 32
GAMMA = 1.4
SIGMA = 0.5
DIFFUSE = 400.0
LANES = 128
GROUPS = LANES // NZ
SPEED_OF = (0, 1, 1, 1, 2)
COEFS = 12


def primitives(q):
    inverse = 1.0 / q[0]
    vel_u, vel_v, vel_w = q[1] * inverse, q[2] * inverse, q[3] * inverse
    kinetic = 0.5 * (vel_u * vel_u + vel_v * vel_v + vel_w * vel_w)
    pressure = (GAMMA - 1.0) * (q[4] - q[0] * kinetic)
    sound = jnp.sqrt(GAMMA * pressure * inverse)
    return inverse, vel_u, vel_v, vel_w, kinetic, pressure, sound


def flux_of(q, normal, speed, pressure):
    return [q[normal]] + [
        q[f] * speed + pressure if f == normal else q[f] * speed for f in (1, 2, 3)
    ] + [speed * (q[4] + pressure)]


def three_speeds(velocity, sound):
    return (velocity - sound, velocity, velocity + sound)


def x_characteristics(res, density, prim):
    inverse, vel_u, vel_v, vel_w, kinetic, _, sound = prim
    du = (res[1] - vel_u * res[0]) * inverse
    dv = (res[2] - vel_v * res[0]) * inverse
    dw = (res[3] - vel_w * res[0]) * inverse
    dp = (GAMMA - 1.0) * (
        res[4] - vel_u * res[1] - vel_v * res[2] - vel_w * res[3] + kinetic * res[0]
    )
    normal = density * sound * du
    return [dp - normal, sound * sound * res[0] - dp, dv, dw, dp + normal]


def factor(speeds, first, last, forced=False):
    cells = len(speeds) - 2
    inverses, lowers, ups, lefts = [], [], [], []
    for i in range(cells):
        parts = []
        for k in range(3):
            lower = -0.5 * SIGMA * speeds[i][k] - DIFFUSE
            upper = 0.5 * SIGMA * speeds[i + 2][k] - DIFFUSE
            main = 1.0 + 2.0 * DIFFUSE
            if i == 0:
                main = main + lower * first[1]
                lower = None if forced else lower * first[0]
            if i == cells - 1:
                main = main + upper * last[1]
                upper = None if forced else upper * last[0]
            pivot = main if i == 0 else main - lower * ups[-1][k]
            inverse = 1.0 / pivot
            scaled = -inverse if lower is None else lower * inverse
            left = -scaled if i == 0 else -scaled * lefts[-1][k]
            parts.append((inverse, scaled, -inverse if upper is None else upper * inverse, left))
        for out, values in zip((inverses, lowers, ups, lefts), zip(*parts)):
            out.append(list(values))
    rights = [None] * cells
    rights[-1] = [-u for u in ups[-1]]
    for i in range(cells - 2, -1, -1):
        lefts[i] = [lefts[i][k] - ups[i][k] * lefts[i + 1][k] for k in range(3)]
        rights[i] = [-ups[i][k] * rights[i + 1][k] for k in range(3)]
    return inverses, lowers, ups, lefts, rights


def substitute(inverses, lowers, ups, sources):
    cells = len(sources)
    owns = []
    for i in range(cells):
        own = [sources[i][f] * inverses[i][SPEED_OF[f]] for f in range(5)]
        if i:
            own = [own[f] - lowers[i][SPEED_OF[f]] * owns[-1][f] for f in range(5)]
        owns.append(own)
    for i in range(cells - 2, -1, -1):
        owns[i] = [owns[i][f] - ups[i][SPEED_OF[f]] * owns[i + 1][f] for f in range(5)]
    return owns


def unpack(rows, fields=5, speeds=3):
    out, at = [], 0
    for n in (fields, fields, speeds, speeds, speeds, speeds):
        out.append(rows[at : at + n])
        at += n
    return out


def join(before, after, speed_of):
    fields = len(speed_of)
    a_f, a_e, b_f, c_f, b_e, c_e = before
    speeds = len(b_f)
    a_g, a_h, b_g, c_g, b_h, c_h = after
    inv = [1.0 / (1.0 - c_e[k] * b_g[k]) for k in range(speeds)]
    e_1 = [b_e[k] * inv[k] for k in range(speeds)]
    f_2 = [c_g[k] * inv[k] for k in range(speeds)]
    e_2 = [c_e[k] * f_2[k] for k in range(speeds)]
    f_1 = [b_g[k] * e_1[k] for k in range(speeds)]
    e_0 = [(a_e[f] + c_e[speed_of[f]] * a_g[f]) * inv[speed_of[f]] for f in range(fields)]
    f_0 = [(a_g[f] + b_g[speed_of[f]] * a_e[f]) * inv[speed_of[f]] for f in range(fields)]
    joined = (
        [a_f[f] + c_f[speed_of[f]] * f_0[f] for f in range(fields)]
        + [a_h[f] + b_h[speed_of[f]] * e_0[f] for f in range(fields)]
        + [b_f[k] + c_f[k] * f_1[k] for k in range(speeds)]
        + [c_f[k] * f_2[k] for k in range(speeds)]
        + [b_h[k] * e_1[k] for k in range(speeds)]
        + [c_h[k] + b_h[k] * e_2[k] for k in range(speeds)]
    )
    return joined, e_0 + e_1 + e_2, f_0 + f_1 + f_2


def merge(low, own, other, speed_of):
    fields = len(speed_of)
    speeds = max(speed_of) + 1
    before = [jnp.where(low, a, b) for a, b in zip(own, other)]
    after = [jnp.where(low, b, a) for a, b in zip(own, other)]
    joined, e, f = join(unpack(before, fields, speeds), unpack(after, fields, speeds), speed_of)
    return joined, [jnp.where(low, b, a) for a, b in zip(e, f)]


def join_factors(q_before, q_after):
    prim_b, prim_a = primitives(q_before), primitives(q_after)
    flux_b = flux_of(q_before, 1, prim_b[1], prim_b[5])
    flux_a = flux_of(q_after, 1, prim_a[1], prim_a[5])
    change = [-0.5 * SIGMA * (a - b) for a, b in zip(flux_a, flux_b)]
    smooth = [DIFFUSE * (a - b) for a, b in zip(q_after, q_before)]
    h_b = x_characteristics([c + d for c, d in zip(change, smooth)], q_before[0], prim_b)
    h_a = x_characteristics([c - d for c, d in zip(change, smooth)], q_after[0], prim_a)
    u_b = [DIFFUSE - 0.5 * SIGMA * v for v in three_speeds(prim_a[1], prim_a[6])]
    l_a = [DIFFUSE + 0.5 * SIGMA * v for v in three_speeds(prim_b[1], prim_b[6])]
    return h_b, u_b, h_a, l_a


def merge_forced(low, own, other):
    before = [jnp.where(low, a, b) for a, b in zip(own, other)]
    after = [jnp.where(low, b, a) for a, b in zip(own, other)]
    q_before, q_after = before[-5:], after[-10:-5]
    h_b, u_b, h_a, l_a = join_factors(q_before, q_after)
    a_f, a_e, b_f, c_f, b_e, c_e = unpack(before)
    a_g, a_h, b_g, c_g, b_h, c_h = unpack(after)
    a_f, a_e = ([a[f] + c[SPEED_OF[f]] * h_b[f] for f in range(5)] for a, c in ((a_f, c_f), (a_e, c_e)))
    a_g, a_h = ([a[f] + b[SPEED_OF[f]] * h_a[f] for f in range(5)] for a, b in ((a_g, b_g), (a_h, b_h)))
    c_f, c_e = ([c[k] * u_b[k] for k in range(3)] for c in (c_f, c_e))
    b_g, b_h = ([b[k] * l_a[k] for k in range(3)] for b in (b_g, b_h))
    joined, e, f = join(
        (a_f, a_e, b_f, c_f, b_e, c_e), (a_g, a_h, b_g, c_g, b_h, c_h), SPEED_OF
    )
    to_low = [h_b[n] + u_b[SPEED_OF[n]] * f[n] for n in range(5)]
    to_low += [u_b[k] * f[5 + 3 * t + k] for t in range(2) for k in range(3)]
    to_high = [h_a[n] + l_a[SPEED_OF[n]] * e[n] for n in range(5)]
    to_high += [l_a[k] * e[5 + 3 * t + k] for t in range(2) for k in range(3)]
    return joined, [jnp.where(low, a, b) for a, b in zip(to_low, to_high)]


def merge_factors(low, own, other):
    before = [jnp.where(low, a, b) for a, b in zip(own, other)]
    after = [jnp.where(low, b, a) for a, b in zip(own, other)]
    prim_b, prim_a = (primitives(q) for q in (before[-5:], after[-10:-5]))
    u_b = [DIFFUSE - 0.5 * SIGMA * v for v in three_speeds(prim_a[1], prim_a[6])]
    l_a = [DIFFUSE + 0.5 * SIGMA * v for v in three_speeds(prim_b[1], prim_b[6])]
    b_f, c_f, b_e, c_e = (before[3 * n : 3 * n + 3] for n in range(4))
    b_g, c_g, b_h, c_h = (after[3 * n : 3 * n + 3] for n in range(4))
    c_f, c_e = ([c[k] * u_b[k] for k in range(3)] for c in (c_f, c_e))
    b_g, b_h = ([b[k] * l_a[k] for k in range(3)] for b in (b_g, b_h))
    joined, _, _ = join(([], [], b_f, c_f, b_e, c_e), ([], [], b_g, c_g, b_h, c_h), ())
    return joined, before[-10:-5], after[-5:]


def last_factors_kernel(level, own_ref, other_ref, out_ref):
    low = bit_low("gx", level)
    own, other = load(own_ref), load(other_ref)
    before = [jnp.where(low, a, b) for a, b in zip(own, other)]
    after = [jnp.where(low, b, a) for a, b in zip(own, other)]
    h_b, u_b, h_a, l_a = join_factors(before[3:], after[3:])
    h_own = [jnp.where(low, a, b) for a, b in zip(h_b, h_a)]
    h_other = [jnp.where(low, b, a) for a, b in zip(h_b, h_a)]
    k_own = [jnp.where(low, a, b) for a, b in zip(u_b, l_a)]
    k_other = [jnp.where(low, b, a) for a, b in zip(u_b, l_a)]
    mine = [own[k] * k_own[k] for k in range(3)]
    theirs = [other[k] * k_other[k] for k in range(3)]
    of_other = [k_own[k] / (1.0 - mine[k] * theirs[k]) for k in range(3)]
    of_own = [of_other[k] * theirs[k] for k in range(3)]
    constant = []
    for f in range(5):
        k = SPEED_OF[f]
        constant.append(h_own[f] + of_other[k] * (other[k] * h_other[f]) + of_own[k] * (own[k] * h_own[f]))
    store(out_ref, constant + of_other + of_own)


def step_down(low, side, outer, speed_of):
    fields = len(speed_of)
    speeds = max(speed_of) + 1
    left, right = outer
    new = [
        side[f] + side[fields + speed_of[f]] * left[f] + side[fields + speeds + speed_of[f]] * right[f]
        for f in range(fields)
    ]
    if isinstance(low, bool):
        return (left, new) if low else (new, right)
    return (
        [jnp.where(low, a, b) for a, b in zip(left, new)],
        [jnp.where(low, b, a) for a, b in zip(right, new)],
    )


def from_last(low, new):
    zero = jnp.zeros_like(new[0])
    return [jnp.where(low, zero, x) for x in new], [jnp.where(low, x, zero) for x in new]


def bit_low(axis, level):
    return (lax.axis_index(axis) >> level) % 2 == 0


def x_edges(codes_ref, shape):
    at, count = lax.axis_index("gx"), lax.axis_size("gx")
    lane = lax.broadcasted_iota(jnp.int32, shape, 1)
    sub = lax.broadcasted_iota(jnp.int32, shape, 0)
    width = codes_ref.shape[1]
    result = []
    place = lax.broadcasted_iota(jnp.int32, (shape[0], width), 1)
    row = lax.broadcasted_iota(jnp.int32, (shape[0], width), 0)
    for side, outer in ((0, at == 0), (1, at == count - 1)):
        codes = jnp.broadcast_to(codes_ref[side : side + 1, :], (shape[0], width))
        is_one = jnp.where(codes == 1, 1.0, 0.0)
        value = jnp.zeros(shape, jnp.float32)
        for g in range(GROUPS):
            mine = jnp.where(place == row * GROUPS + g, is_one, 0.0)
            column = jnp.sum(mine, axis=1, keepdims=True)
            value = jnp.where(lane // NZ == g, column, value)
        result.append(jnp.where(outer, value, 0.0))
    return result


def y_edges(codes_ref, shape):
    at, count = lax.axis_index("gy"), lax.axis_size("gy")
    group = lax.broadcasted_iota(jnp.int32, shape, 1) // NZ
    cells = shape[0]
    result = []
    place = lax.broadcasted_iota(jnp.int32, (cells, cells), 1)
    row = lax.broadcasted_iota(jnp.int32, (cells, cells), 0)
    for side, outer, face in ((0, at == 0, 0), (1, at == count - 1, GROUPS - 1)):
        codes = jnp.broadcast_to(codes_ref[side : side + 1, :], (cells, cells))
        mine = jnp.where(jnp.logical_and(codes == 1, place == row), 1.0, 0.0)
        value = jnp.broadcast_to(jnp.sum(mine, axis=1, keepdims=True), shape)
        at_face = jnp.logical_and(outer, group == face)
        result.append((jnp.where(at_face, 0.0, 1.0), jnp.where(at_face, value, 0.0)))
    return result


def to_group(value, source, target):
    shift = (target - source) * NZ % LANES
    return pltpu.roll(value, shift, 1) if shift else value


def pack_kernel(flow_ref, qx_ref, one_ref, two_ref):
    cells = flow_ref.shape[1]
    chunks = flow_ref.shape[2] // LANES
    even = bit_low("gx", 0)
    group = lax.broadcasted_iota(jnp.int32, (cells, LANES), 1) // NZ
    downs, ups = [], []
    for f in range(5):
        down = to_group(flow_ref[f, :, 0:LANES], 0, f % GROUPS)
        up = to_group(flow_ref[f, :, (chunks - 1) * LANES : chunks * LANES], GROUPS - 1, f % GROUPS)
        for rows, value in ((downs, down), (ups, up)):
            if f % GROUPS:
                rows[-1] = jnp.where(group == f % GROUPS, value, rows[-1])
            else:
                rows.append(value)
    for n, (down, up) in enumerate(zip(downs, ups)):
        one_ref[n] = jnp.where(even, up, down)
        two_ref[n] = jnp.where(even, down, up)
    for f in range(5):
        for c in range(chunks):
            qx_ref[f, pl.ds(c, cells, stride=chunks), :] = flow_ref[f, :, c * LANES : (c + 1) * LANES]


def y_halos(flow_ref, one_ref, two_ref, f):
    chunks = flow_ref.shape[2] // LANES
    at, count = lax.axis_index("gy"), lax.axis_size("gy")
    even = bit_low("gx", 0)
    low = jnp.where(even, one_ref[f // GROUPS], two_ref[f // GROUPS])
    high = jnp.where(even, two_ref[f // GROUPS], one_ref[f // GROUPS])
    low, high = to_group(low, f % GROUPS, GROUPS - 1), to_group(high, f % GROUPS, 0)
    own_low = to_group(flow_ref[f, :, 0:LANES], 0, GROUPS - 1)
    own_high = to_group(flow_ref[f, :, (chunks - 1) * LANES : chunks * LANES], GROUPS - 1, 0)
    return jnp.where(at == 0, own_low, low), jnp.where(at == count - 1, own_high, high)


def x_factor_kernel(
    qx_ref, codes_ref, out_ref, inverse_ref, lower_ref, up_ref, left_ref, right_ref, points_ref, weight_ref
):
    cells = inverse_ref.shape[0]
    chunks = inverse_ref.shape[2]
    rows = [[qx_ref[f, i * chunks : (i + 1) * chunks, :] for f in range(5)] for i in range(cells)]
    speeds, points = [], []
    for q in rows:
        prim = primitives(q)
        speeds.append(three_speeds(prim[1], prim[6]))
        impedance = q[0] * prim[6]
        points.append([impedance, 0.5 / impedance])
    for i in range(cells):
        store(points_ref.at[i], points[i])
    neumann = x_edges(codes_ref, (chunks, LANES))
    parts = factor(
        speeds[:1] + speeds + speeds[-1:], (None, neumann[0]), (None, neumann[1]), forced=True
    )
    for ref, values in zip((inverse_ref, lower_ref, up_ref, left_ref, right_ref), parts):
        for i in range(cells):
            store(ref.at[i], values[i])
    weights = [part_weights(*parts[:3], k) for k in range(3)]
    for i in range(cells):
        store(weight_ref.at[i], [weights[k][side][i] for side in range(2) for k in range(3)])
    lefts, rights = parts[3:]
    store(out_ref, lefts[0] + rights[0] + lefts[-1] + rights[-1] + rows[0] + rows[-1])


def x_source_kernel(qx_ref, weight_ref, out_ref, ends_ref):
    cells = out_ref.shape[0]
    chunks = out_ref.shape[2]
    lane = lax.broadcasted_iota(jnp.int32, (chunks, LANES), 1)
    sub = lax.broadcasted_iota(jnp.int32, (chunks, LANES), 0)
    z_of = lane % NZ
    rows = [[qx_ref[f, i * chunks : (i + 1) * chunks, :] for f in range(5)] for i in range(cells)]
    prims = [primitives(q) for q in rows]
    fluxes = [flux_of(q, 1, p[1], p[5]) for q, p in zip(rows, prims)]
    rows, fluxes = (v[:1] + v + v[-1:] for v in (rows, fluxes))
    up_edge = jnp.logical_and(sub == chunks - 1, lane >= LANES - NZ)
    down_edge = jnp.logical_and(sub == 0, lane < NZ)

    def y_next(value):
        turned = pltpu.roll(value, LANES - NZ, 1)
        turned = jnp.where(lane >= LANES - NZ, pltpu.roll(turned, chunks - 1, 0), turned)
        return jnp.where(up_edge, value, turned)

    def y_before(value):
        turned = pltpu.roll(value, NZ, 1)
        turned = jnp.where(lane < NZ, pltpu.roll(turned, 1, 0), turned)
        return jnp.where(down_edge, value, turned)

    def z_change(value):
        after = jnp.where(z_of == NZ - 1, pltpu.roll(value, NZ - 1, 1), pltpu.roll(value, LANES - 1, 1))
        before = jnp.where(z_of == 0, pltpu.roll(value, LANES - NZ + 1, 1), pltpu.roll(value, 1, 1))
        return after - before

    ends = None
    for i in range(cells):
        q = rows[i + 1]
        _, _, vel_v, vel_w, _, pressure, _ = prims[i]
        after = [y_next(v) for v in list(q) + [vel_v, pressure]]
        before = [y_before(v) for v in list(q) + [vel_v, pressure]]
        flux_after = flux_of(after, 2, after[5], after[6])
        flux_before = flux_of(before, 2, before[5], before[6])
        flux_z = flux_of(q, 3, vel_w, pressure)
        res = []
        for f in range(5):
            change = (
                (fluxes[i + 2][f] - fluxes[i][f])
                + (flux_after[f] - flux_before[f])
                + z_change(flux_z[f])
            )
            smooth = rows[i + 2][f] + rows[i][f] + after[f] + before[f] - 4.0 * q[f]
            res.append(-0.5 * SIGMA * change + DIFFUSE * smooth)
        source = x_characteristics(res, q[0], prims[i])
        store(out_ref.at[i], source)
        parts = [weight_ref[i, 3 * side + SPEED_OF[f]] * source[f] for side in range(2) for f in range(5)]
        ends = parts if ends is None else [a + b for a, b in zip(ends, parts)]
    store(ends_ref, ends)


def y_edge_mask(chunks):
    lane = lax.broadcasted_iota(jnp.int32, (chunks, LANES), 1)
    sub = lax.broadcasted_iota(jnp.int32, (chunks, LANES), 0)
    high = jnp.logical_and(sub == chunks - 1, lane >= LANES - NZ)
    return jnp.logical_or(high, jnp.logical_and(sub == 0, lane < NZ))


def x_kernel(flow_ref, one_ref, two_ref, weight_ref, ends_ref, rows_ref, extra_ref):
    cells = flow_ref.shape[1]
    chunks = flow_ref.shape[2] // LANES
    lows, highs = zip(*[y_halos(flow_ref, one_ref, two_ref, f) for f in range(5)])
    extras = []
    for ghosts, at, turn, sign in ((lows, 0, NZ, 1.0), (highs, chunks - 1, LANES - NZ, -1.0)):
        ghosts = [pltpu.roll(g, turn, 1) for g in ghosts]
        inner = [flow_ref[f, :, at * LANES : (at + 1) * LANES] for f in range(5)]
        ghost_prim, prim = primitives(ghosts), primitives(inner)
        ghost_flux = flux_of(ghosts, 2, ghost_prim[2], ghost_prim[5])
        inner_flux = flux_of(inner, 2, prim[2], prim[5])
        res = [
            sign * 0.5 * SIGMA * (ghost_flux[f] - inner_flux[f]) + DIFFUSE * (ghosts[f] - inner[f])
            for f in range(5)
        ]
        extras.append(x_characteristics(res, inner[0], prim))
    lane = lax.broadcasted_iota(jnp.int32, (cells, LANES), 1)
    store(extra_ref, [jnp.where(lane < LANES // 2, low, high) for low, high in zip(*extras)])
    edge = y_edge_mask(chunks)
    added = None
    for i in range(cells):
        extra = [jnp.broadcast_to(extra_ref[f, i : i + 1, :], (chunks, LANES)) for f in range(5)]
        parts = [weight_ref[i, 3 * side + SPEED_OF[f]] * extra[f] for side in range(2) for f in range(5)]
        added = parts if added is None else [a + b for a, b in zip(added, parts)]
    store(rows_ref, [ends_ref[n] + jnp.where(edge, value, 0.0) for n, value in enumerate(added)])


def x_own_kernel(source_ref, extra_ref, inverse_ref, lower_ref, up_ref, own_ref):
    cells, chunks = source_ref.shape[0], source_ref.shape[2]
    edge = y_edge_mask(chunks)
    sources = []
    for i in range(cells):
        extra = [jnp.broadcast_to(extra_ref[f, i : i + 1, :], (chunks, LANES)) for f in range(5)]
        sources.append([source_ref[i, f] + jnp.where(edge, extra[f], 0.0) for f in range(5)])
    owns = substitute(*([load(ref.at[i]) for i in range(cells)] for ref in (inverse_ref, lower_ref, up_ref)), sources)
    for i in range(cells):
        store(own_ref.at[i], owns[i])


def load(ref):
    return [ref[n] for n in range(ref.shape[0])]


def store(ref, values):
    for n, value in enumerate(values):
        ref[n] = value


def x_merge_factor_kernel(level, final, own_ref, other_ref, out_ref):
    joined, q_first, q_last = merge_factors(bit_low("gx", level), load(own_ref), load(other_ref))
    if final:
        low = bit_low("gx", level + 1)
        b_f, _, _, c_e = (joined[3 * n : 3 * n + 3] for n in range(4))
        pairs = list(zip(c_e, b_f)) + list(zip(q_last, q_first))
        store(out_ref, [jnp.where(low, e, f) for e, f in pairs])
    else:
        store(out_ref, joined + q_first + q_last)


def x_merge_kernel(level, final, own_ref, other_ref, own_factor_ref, other_factor_ref, out_ref, side_ref):
    joined, side = merge_forced(
        bit_low("gx", level), load(own_ref) + load(own_factor_ref), load(other_ref) + load(other_factor_ref)
    )
    a_f, a_e = joined[:5], joined[5:10]
    if final:
        low = bit_low("gx", level + 1)
        store(out_ref, [jnp.where(low, e, f) for e, f in zip(a_e, a_f)])
    else:
        store(out_ref, a_f + a_e)
    store(side_ref, side)


def y_merge_kernel(level, own_ref, other_ref, out_ref, side_ref):
    own, other = expand(load(own_ref)), expand(load(other_ref))
    joined, side = merge(bit_low("gy", level), own, other, PACKED_SPEED)
    store(out_ref, compress(joined))
    store(side_ref, side)


def outer_values(levels, own, other, factors, side_refs):
    low = bit_low("gx", levels - 1)
    new = [
        factors[f] + factors[5 + SPEED_OF[f]] * other[f] + factors[8 + SPEED_OF[f]] * own[f] for f in range(5)
    ]
    outer = from_last(low, new)
    for level in range(levels - 2, -1, -1):
        outer = step_down(bit_low("gx", level), load(side_refs[level]), outer, SPEED_OF)
    return outer


def pick(place, values):
    return [
        functools.reduce(lambda old, n: jnp.where(place == n, items[n], old), range(1, len(items)), items[0])
        for items in zip(*values)
    ]


def outer_of_four(place, own, arrived, speed_of):
    fields, speeds = len(speed_of), max(speed_of) + 1
    ring = [own] + arrived
    segments = [unpack(pick((place - n) % 4, ring), fields, speeds) for n in range(4)]
    left, e_left, f_left = join(segments[0], segments[1], speed_of)
    right, e_right, f_right = join(segments[2], segments[3], speed_of)
    a_e, c_e = (unpack(left, fields, speeds)[n] for n in (1, 5))
    a_f, b_f = (unpack(right, fields, speeds)[n] for n in (0, 2))
    e_mid, f_mid, zero = [], [], jnp.zeros_like(a_e[0])
    inverse = [1.0 / (1.0 - c_e[k] * b_f[k]) for k in range(speeds)]
    for n in range(fields):
        k = speed_of[n]
        e_mid.append((a_e[n] + c_e[k] * a_f[n]) * inverse[k])
        f_mid.append((a_f[n] + b_f[k] * a_e[n]) * inverse[k])

    def inner(terms, outer, side):
        return [terms[n] + terms[fields + side * speeds + speed_of[n]] * outer[n] for n in range(fields)]

    lefts = [[zero] * fields, inner(e_left, f_mid, 1), e_mid, inner(e_right, e_mid, 0)]
    rights = [inner(f_left, f_mid, 1), f_mid, inner(f_right, e_mid, 0), [zero] * fields]
    return pick(place, lefts), pick(place, rights)


PACKED_SPEED = (0, 0)


def regroup(parts, group):
    steps = len(parts)
    result = []
    for jj in range(steps):
        value = None
        for s in range(GROUPS):
            y = s * steps + jj
            piece = parts[y // GROUPS]
            shift = (s - y % GROUPS) * NZ % LANES
            piece = pltpu.roll(piece, shift, 1) if shift else piece
            value = piece if s == 0 else jnp.where(group == s, piece, value)
        result.append(value)
    return result


def lane_partner(values, group, level):
    if level == 0:
        return [
            jnp.where(group % 2 == 0, pltpu.roll(v, LANES - NZ, 1), pltpu.roll(v, NZ, 1)) for v in values
        ]
    return [pltpu.roll(v, LANES // 2, 1) for v in values]


def lane_low(group, level):
    return (group // 2 ** level) % 2 == 0


def y_factor_kernel(
    flow_ref, one_ref, two_ref, codes_ref,
    packed_ref, inverse_ref, lower_ref, up_ref, left_ref, right_ref, join_ref, side_ref, weight_ref,
):
    cells = flow_ref.shape[1]
    chunks = flow_ref.shape[2] // LANES
    lane = lax.broadcasted_iota(jnp.int32, (cells, LANES), 1)
    group = lane // NZ
    vels, sounds = [], []
    for c in range(chunks):
        prim = primitives([flow_ref[f, :, c * LANES : (c + 1) * LANES] for f in range(5)])
        vels.append(prim[2])
        sounds.append(prim[6])
    speeds = [three_speeds(v, c) for v, c in zip(regroup(vels, group), regroup(sounds, group))]
    lows, highs = zip(*[y_halos(flow_ref, one_ref, two_ref, f) for f in range(5)])
    low_prim, high_prim = primitives(lows), primitives(highs)
    low_speed = three_speeds(low_prim[2], low_prim[6])
    high_speed = three_speeds(high_prim[2], high_prim[6])
    before = tuple(
        pltpu.roll(jnp.where(group == GROUPS - 1, low_speed[k], speeds[-1][k]), NZ, 1) for k in range(3)
    )
    after = tuple(
        pltpu.roll(jnp.where(group == 0, high_speed[k], speeds[0][k]), LANES - NZ, 1) for k in range(3)
    )
    parts = factor([before] + speeds + [after], *y_edges(codes_ref, (cells, LANES)))
    for ref, values in zip((inverse_ref, lower_ref, up_ref, left_ref, right_ref), parts):
        for i in range(chunks):
            store(ref.at[i], values[i])
    lefts, rights = parts[3:]
    ends = lefts[0] + rights[0] + lefts[-1] + rights[-1]
    for level in range(2):
        low = lane_low(group, level)
        other = lane_partner(ends, group, level)
        before = [jnp.where(low, a, b) for a, b in zip(ends, other)]
        after = [jnp.where(low, b, a) for a, b in zip(ends, other)]
        b_f, c_f, b_e, c_e = (before[3 * n : 3 * n + 3] for n in range(4))
        b_g, c_g, b_h, c_h = (after[3 * n : 3 * n + 3] for n in range(4))
        inv = [1.0 / (1.0 - c_e[k] * b_g[k]) for k in range(3)]
        store(join_ref.at[level], inv + c_e + b_g + c_f + b_h)
        ends, e, f = join(([], [], b_f, c_f, b_e, c_e), ([], [], b_g, c_g, b_h, c_h), ())
        store(side_ref.at[level], [jnp.where(low, b, a) for a, b in zip(e, f)])
    store(packed_ref, [four(group, t[0], t[1], t[2], t[1]) for t in (ends[3 * n : 3 * n + 3] for n in range(4))])
    weights = end_weights(group, parts, [load(join_ref.at[level]) for level in range(2)])
    for c in range(chunks):
        store(weight_ref.at[c], [ungroup(column, c, group) for column in weights])


def part_weights(inverses, lowers, ups, k):
    steps = len(inverses)
    reach = [None] * steps
    passed = None
    for i in range(steps):
        reach[i] = passed
        passed = -ups[i][k] if passed is None else -passed * ups[i][k]
    first_w, last_w = [None] * steps, [None] * steps
    ahead_first, ahead_last = reach[-1], None
    for i in range(steps - 1, -1, -1):
        if i == steps - 1:
            last_w[i] = inverses[i][k]
        else:
            ahead_first = -lowers[i + 1][k] * ahead_first
            ahead_first = ahead_first + (1.0 if i == 0 else reach[i])
            ahead_last = -lowers[i + 1][k] if ahead_last is None else -lowers[i + 1][k] * ahead_last
            last_w[i] = ahead_last * inverses[i][k]
        first_w[i] = ahead_first * inverses[i][k]
    return first_w, last_w


def end_weights(group, parts, joins):
    columns = []
    for k in range(3):
        first_w, last_w = part_weights(*parts[:3], k)
        steps = len(first_w)
        shares = []
        for level in range(2):
            inv, c_e, b_g, c_f, b_h = (joins[level][3 * n + k] for n in range(5))
            low = lane_low(group, level)
            one, zero = jnp.ones_like(inv), jnp.zeros_like(inv)
            shares.append((
                jnp.where(low, one, c_f * inv),
                jnp.where(low, c_f * b_g * inv, zero),
                jnp.where(low, zero, b_h * c_e * inv),
                jnp.where(low, b_h * inv, one),
            ))
        (ff, lf, fl, ll), (top_ff, top_lf, top_fl, top_ll) = shares
        for top_first, top_last in ((top_ff, top_lf), (top_fl, top_ll)):
            share_first = top_first * ff + top_last * fl
            share_last = top_first * lf + top_last * ll
            columns.append([share_first * first_w[i] + share_last * last_w[i] for i in range(steps)])
    return columns[0::2] + columns[1::2]


def y_kernel(levels, *refs):
    (points_ref, own_ref, left_ref, right_ref, mine_ref, other_ref, last_ref, packed_ref, weight_ref) = refs[:9]
    sides = refs[9 : 9 + levels - 1]
    out_ref, turn_ref = refs[9 + levels - 1 :]
    chunks = own_ref.shape[2]
    cells = own_ref.shape[0]
    outer_l, outer_r = outer_values(levels, load(mine_ref), load(other_ref), load(last_ref), sides)
    for i in range(cells):
        impedance, half_admittance = load(points_ref.at[i])
        wave = [
            own_ref[i, f] + left_ref[i, SPEED_OF[f]] * outer_l[f] + right_ref[i, SPEED_OF[f]] * outer_r[f]
            for f in range(5)
        ]
        dp = 0.5 * (wave[0] + wave[4])
        du = (wave[4] - wave[0]) * half_admittance
        normal = impedance * wave[2]
        values = [dp - normal, wave[1], du, wave[3], dp + normal]
        for n, value in enumerate(values):
            turn_ref[n, i * chunks : (i + 1) * chunks, :] = value
    group = lax.broadcasted_iota(jnp.int32, (cells, LANES), 1) // NZ
    ends = []
    for side in range(2):
        for f in range(5):
            terms = [
                turn_ref[f, pl.ds(c, cells, stride=chunks), :] * weight_ref[c, 3 * side + SPEED_OF[f]]
                for c in range(chunks)
            ]
            while len(terms) > 1:
                terms = [a + b for a, b in zip(terms[0::2], terms[1::2])] + terms[len(terms) // 2 * 2 :]
            ends.append(terms[0])
    ends = [v + pltpu.roll(v, LANES // 2, 1) for v in ends]
    ends = [v + pltpu.roll(v, NZ, 1) for v in ends]
    rows = [four(group, a[0], a[1], a[4], a[2]) for a in (ends[:5], ends[5:])]
    rows.append(jnp.where(group == GROUPS - 1, ends[8], ends[3]))
    store(out_ref, rows + load(packed_ref))


def expand(rows):
    return [rows[0], rows[2], rows[1], pltpu.roll(rows[2], LANES // 2, 1)] + rows[3:]


def compress(rows):
    group = lax.broadcasted_iota(jnp.int32, rows[0].shape, 1) // NZ
    mixed = jnp.where(group == GROUPS - 1, pltpu.roll(rows[3], LANES // 2, 1), rows[1])
    return [rows[0], rows[2], mixed] + rows[4:]


def y_sweep(turn_ref, cells, group, factor_refs, join_ref):
    chunks = turn_ref.shape[1] // cells
    fields = [
        regroup([turn_ref[n, pl.ds(c, cells, stride=chunks), :] for c in range(chunks)], group)
        for n in range(5)
    ]
    sources = [[fields[f][jj] for f in range(5)] for jj in range(chunks)]
    owns = substitute(*([load(ref.at[i]) for i in range(chunks)] for ref in factor_refs), sources)
    a_f, a_e = owns[0], owns[-1]
    sides = []
    for level in range(2):
        low = lane_low(group, level)
        other = lane_partner(a_f + a_e, group, level)
        parts = load(join_ref.at[level])
        inv, c_e, b_g, c_f, b_h = (parts[3 * n : 3 * n + 3] for n in range(5))
        before = [jnp.where(low, a, b) for a, b in zip(a_f + a_e, other)]
        after = [jnp.where(low, b, a) for a, b in zip(a_f + a_e, other)]
        e, f, new_f, new_e = [], [], [], []
        for n in range(5):
            k = SPEED_OF[n]
            e.append((before[5 + n] + c_e[k] * after[n]) * inv[k])
            f.append((after[n] + b_g[k] * before[5 + n]) * inv[k])
            new_f.append(before[n] + c_f[k] * f[n])
            new_e.append(after[5 + n] + b_h[k] * e[n])
        a_f, a_e = new_f, new_e
        sides.append([jnp.where(low, b, a) for a, b in zip(e, f)])
    return owns, sides


def four(group, a, b, c, d):
    return jnp.where(group == 0, a, jnp.where(group == 1, b, jnp.where(group == 2, c, d)))


def spread(group, value, source):
    half = jnp.where(group // 2 == source // 2, value, pltpu.roll(value, LANES // 2, 1))
    down, up = pltpu.roll(half, NZ, 1), pltpu.roll(half, LANES - NZ, 1)
    if source % 2 == 0:
        return jnp.where(group % 2 == 0, half, down)
    return jnp.where(group % 2 == 1, half, up)


def ungroup(values, c, group):
    steps = len(values)
    result = None
    for g in range(GROUPS):
        y = c * GROUPS + g
        piece = to_group(values[y % steps], y // steps, g)
        result = piece if g == 0 else jnp.where(group == g, piece, result)
    return result


def prepare_kernel(
    flow_ref, turn_ref, inverse_ref, lower_ref, up_ref, join_ref, yleft_ref, yright_ref, side_ref,
    terms_ref, points_ref, half_ref, quarter_ref,
):
    cells = flow_ref.shape[1]
    chunks = flow_ref.shape[2] // LANES
    group = lax.broadcasted_iota(jnp.int32, (cells, LANES), 1) // NZ
    owns, ends = y_sweep(turn_ref, cells, group, (inverse_ref, lower_ref, up_ref), join_ref)
    columns = [[own[n] for own in owns] for n in range(5)] + [
        [ref[j, n] for j in range(chunks)] for ref in (yleft_ref, yright_ref) for n in range(3)
    ]
    for c in range(chunks):
        store(terms_ref.at[c], [ungroup(column, c, group) for column in columns])
        q = [flow_ref[f, :, c * LANES : (c + 1) * LANES] for f in range(5)]
        _, vel_u, vel_v, vel_w, kinetic, _, sound = primitives(q)
        store(
            points_ref.at[c],
            [vel_u, vel_v, vel_w, kinetic, 1.0 / (2.0 * q[0] * sound), 1.0 / (sound * sound)],
        )
    for level, ref, count in ((1, half_ref, 2), (0, quarter_ref, GROUPS)):
        rows = ends[level] + load(side_ref.at[level])
        for n in range(count):
            store(ref.at[n], [spread(group, row, n * GROUPS // count) for row in rows])


def final_kernel(levels, *refs):
    (flow_ref, terms_ref, points_ref, half_ref, quarter_ref, mine_ref) = refs[:6]
    arrived, sides = refs[6:9], refs[9 : 9 + levels]
    out_hbm, out_ref, sems = refs[9 + levels :]
    cells = flow_ref.shape[1]
    chunks = flow_ref.shape[2] // LANES
    group = lax.broadcasted_iota(jnp.int32, (cells, LANES), 1) // NZ
    place = (lax.axis_index("gy") >> levels) % 4
    outer = outer_of_four(place, expand(load(mine_ref)), [expand(load(ref)) for ref in arrived], PACKED_SPEED)
    for level in range(levels - 1, -1, -1):
        outer = step_down(bit_low("gy", level), load(sides[level]), outer, PACKED_SPEED)
    outer = tuple(
        [spread(group, v[0], 0), spread(group, v[0], 1), spread(group, v[0], 3),
         spread(group, v[1], 1), spread(group, v[0], 2)]
        for v in outer
    )
    copies = []
    for s in range(GROUPS):
        half = step_down(s < GROUPS // 2, load(half_ref.at[s * 2 // GROUPS]), outer, SPEED_OF)
        outer_l, outer_r = step_down(s % 2 == 0, load(quarter_ref.at[s]), half, SPEED_OF)
        for c in range(s * chunks // GROUPS, (s + 1) * chunks // GROUPS):
            wave = [
                terms_ref[c, f] + terms_ref[c, 5 + SPEED_OF[f]] * outer_l[f]
                + terms_ref[c, 8 + SPEED_OF[f]] * outer_r[f]
                for f in range(5)
            ]
            density = flow_ref[0, :, c * LANES : (c + 1) * LANES]
            vel_u, vel_v, vel_w, kinetic, half_admittance, inverse_squared = load(points_ref.at[c])
            dp = 0.5 * (wave[0] + wave[4])
            dv = (wave[4] - wave[0]) * half_admittance
            dr = (wave[1] + dp) * inverse_squared
            du, dw = wave[2], wave[3]
            energy = (
                kinetic * dr + density * (vel_u * du + vel_v * dv + vel_w * dw)
                + dp * (1.0 / (GAMMA - 1.0))
            )
            result = [dr, vel_u * dr + density * du, vel_v * dr + density * dv, vel_w * dr + density * dw, energy]
            for f in range(5):
                out_ref[f, :, c * LANES : (c + 1) * LANES] = result[f]
        width = chunks // GROUPS * LANES
        part = (slice(None), slice(None), slice(s * width, (s + 1) * width))
        copies.append(pltpu.make_async_copy(out_ref.at[part], out_hbm.at[part], sems.at[s]))
        copies[-1].start()
    for copy in copies:
        copy.wait()


def call(kernel, args, outs, scratch=(), out_hbm=False):
    vmem, hbm = (pl.BlockSpec(memory_space=space) for space in (pltpu.VMEM, pltpu.HBM))
    return pl.pallas_call(
        kernel,
        out_shape=[jax.ShapeDtypeStruct(shape, jnp.float32) for shape in outs],
        in_specs=[vmem] * len(args),
        out_specs=[hbm if out_hbm else vmem] * len(outs),
        scratch_shapes=list(scratch),
        compiler_params=pltpu.CompilerParams(vmem_limit_bytes=16 * 1024 * 1024),
    )(*args)


def pairs_at(count, level):
    return [(i, i ^ (1 << level)) for i in range(count)]


def pairs_across(count, level):
    return [(i, i ^ (1 << level) ^ (1 if level else 0)) for i in range(count)]


def snake(count_x, count_y):
    pairs = []
    for x in range(count_x):
        for y in range(count_y):
            to = y + 1 if x % 2 == 0 else y - 1
            inside = 0 <= to < count_y
            pairs.append((x * count_y + y, x * count_y + to if inside else (x ^ 1) * count_y + y))
    return pairs


def ring_of_four(count, step):
    width = count // 4
    return [(i, (i + step * width) % count) for i in range(count)]


def levels_of(count):
    levels = count.bit_length() - 1
    assert count == 1 << levels and levels >= 2
    return levels


def local(flow, x_codes, y_codes):
    cells = flow.shape[1]
    columns = flow.shape[2]
    chunks = columns // LANES
    count_x, count_y = lax.axis_size("gx"), lax.axis_size("gy")
    levels_x, levels_y = levels_of(count_x), levels_of(count_y)
    tile_x, tile_y = (chunks, LANES), (cells, LANES)

    qx, one, two = call(pack_kernel, [flow], [(5, cells * chunks, LANES), (2,) + tile_y, (2,) + tile_y])
    round_trip = snake(count_x, count_y)
    one = lax.ppermute(one, ("gx", "gy"), round_trip)
    two = lax.ppermute(two, ("gx", "gy"), [(b, a) for a, b in round_trip])

    factors, inverse, lower, upper, left, right, xpoints, xweight = call(
        x_factor_kernel, [qx, x_codes],
        [(COEFS + 10,) + tile_x] + [(cells, 3) + tile_x] * 5 + [(cells, 2) + tile_x, (cells, 6) + tile_x],
    )
    source, ends = call(x_source_kernel, [qx, xweight], [(cells, 5) + tile_x, (10,) + tile_x])
    all_factors = []
    for level in range(levels_x):
        other = lax.ppermute(factors, "gx", pairs_across(count_x, level))
        all_factors.append((factors, other))
        if level < levels_x - 1:
            final = level == levels_x - 2
            (factors,) = call(
                functools.partial(x_merge_factor_kernel, level, final),
                [factors, other], [(8 if final else COEFS + 10,) + tile_x],
            )
    rows, extra = call(x_kernel, [flow, one, two, xweight, ends], [(10,) + tile_x, (5,) + tile_y])
    (own,) = call(x_own_kernel, [source, extra, inverse, lower, upper], [(cells, 5) + tile_x])
    (last,) = call(
        functools.partial(last_factors_kernel, levels_x - 1), [*all_factors[-1]],
        [(11,) + tile_x],
    )
    sides = []
    for level in range(levels_x - 1):
        other = lax.ppermute(rows, "gx", pairs_across(count_x, level))
        final = level == levels_x - 2
        rows, side_rows = call(
            functools.partial(x_merge_kernel, level, final),
            [rows, other, *all_factors[level]], [(5 if final else 10,) + tile_x, (11,) + tile_x],
        )
        sides.append(side_rows)
    other = lax.ppermute(rows, "gx", pairs_across(count_x, levels_x - 1))
    y_factors, yinverse, ylower, yup, yleft, yright, yjoin, yside, yweight = call(
        y_factor_kernel, [flow, one, two, y_codes],
        [(4,) + tile_y] + [(chunks, 3) + tile_y] * 5 + [(2, 15) + tile_y, (2, 6) + tile_y, (chunks, 6) + tile_y],
    )
    packed, turn = call(
        functools.partial(y_kernel, levels_x),
        [xpoints, own, left, right, rows, other, last, y_factors, yweight] + sides,
        [(7,) + tile_y, (5, cells * chunks, LANES)],
    )
    prepared = call(
        prepare_kernel, [flow, turn, yinverse, ylower, yup, yjoin, yleft, yright, yside],
        [(chunks, 11) + tile_y, (chunks, 6) + tile_y, (2, 11) + tile_y, (GROUPS, 11) + tile_y],
    )
    sides = []
    for level in range(levels_y - 2):
        other = lax.ppermute(packed, "gy", pairs_at(count_y, level))
        packed, side_rows = call(
            functools.partial(y_merge_kernel, level),
            [packed, other], [(7,) + tile_y, (4,) + tile_y],
        )
        sides.append(side_rows)
    arrived = []
    for step in range(1, 4):
        arrived.append(lax.ppermute(packed, "gy", ring_of_four(count_y, step)))
    (result,) = call(
        functools.partial(final_kernel, levels_y - 2),
        [flow, *prepared, packed, *arrived] + sides,
        [(5, cells, columns)],
        [pltpu.VMEM((5, cells, columns), jnp.float32), pltpu.SemaphoreType.DMA((GROUPS,))],
        out_hbm=True,
    )
    return result


def solution(mesh):
    in_specs = (P(None, "gx", "gy"), P(None, "gy"), P(None, "gx"))
    out_specs = P(None, "gx", "gy")
    return jax.shard_map(local, mesh=mesh, in_specs=in_specs, out_specs=out_specs, check_vma=False)
```
